512 devices in a mesh: sec: 32 (over z_lo, x), tile: 16 (over y, z_hi, core).
Axes of the slice: x: 4, y: 4, z: 16 (z_hi: 2, z_lo: 8; z = z_hi * 8 + z_lo), core: 2. Of those that a mesh axis runs over, the one named last changes fastest.
Arguments:
- images: bfloat16 [192, 8192, 512], P('sec', 'tile'), may hold values from -24 to 24
- displacement: float32 [192, 2, 2048, 128], P('sec', None, 'tile'), may hold values from -6 to 6
- offsets: int32 [192, 3, 2], P('sec'), may hold values from 0 to 3
- weights: int32 [192, 3], P('sec'), may hold values from 1 to 3
- stiffness: float32 [192], P('sec'), may hold values from 0.25 to 1
Outputs:
- aligned: float32 [192, 2, 2048, 128], P('sec', None, 'tile')
The draws below stay inside these ranges and needn't reach their ends.
All inputs are finite; a program needn't handle non-finite values.
Results may differ from the reference program's by a relative error of at most 0.005.
Values may be sent and summed in bfloat16 or wider, within the bound.
A program may use at most 64 MiB of HBM per device.

```python
import math
import jax
import jax.numpy as jnp
from jax import lax

PIXELS = 512
GRID = 128
SKIPS = 3
ITERS = 3
SECTIONS = 192
ROWS = 2048
PIXEL_ROWS = 8192
N_TILE = 16


def touch_ends(entries, rng, low, top_value):
    place = [jax.random.randint(jax.random.fold_in(rng, axis), (), 0, length) for axis, length in enumerate(entries.shape)]
    widest = entries.shape.index(max(entries.shape))
    neighbour = place[:widest] + [(place[widest] + 1) % entries.shape[widest]] + place[widest + 1:]
    return entries.at[tuple(place)].set(low).at[tuple(neighbour)].set(top_value)


def shard_levels(own_key, dims, shards, low, high):
    loudness, own = 1.0, jax.random.fold_in(own_key, 6)
    for dim, shards_of in shards:
        draws = jnp.exp(jax.random.uniform(jax.random.fold_in(own, dim), (shards_of,), jnp.float32, low / len(shards), high / len(shards)))
        loudness = loudness * jnp.repeat(draws, dims[dim] // shards_of).reshape([-1 if axis == dim else 1 for axis in range(len(dims))])
    return loudness


def noise(stream_key, shape, scale, bound, split=(), held_as=jnp.bfloat16):
    array = scale * jax.random.normal(stream_key, shape, jnp.float32)
    if split:
        array = array * shard_levels(stream_key, shape, split, -0.22, 0.18)
    return jnp.clip(array, -bound, bound).astype(held_as)


def setup_inputs(seed: int = 0) -> dict:
    keys = jax.random.split(jax.random.key(seed), 6)
    return {
        "images": noise(keys[0], (SECTIONS, PIXEL_ROWS, PIXELS), 4.0, 24.0, ((0, 32), (1, 16))),
        "displacement": noise(keys[1], (SECTIONS, 2, ROWS, GRID), 1.0, 6.0, ((0, 32), (2, 16)), jnp.float32),
        "offsets": touch_ends(jax.random.randint(keys[2], (SECTIONS, SKIPS, 2), 0, 4), jax.random.fold_in(keys[2], 1), 0, 3).astype(jnp.int32),
        "weights": touch_ends(jax.random.randint(keys[3], (SECTIONS, SKIPS), 1, 4), jax.random.fold_in(keys[3], 1), 1, 3).astype(jnp.int32),
        "stiffness": jnp.clip(jnp.exp(math.log(1.0) - 1.3862944 * jax.random.uniform(keys[4], (SECTIONS,), jnp.float32) ** shard_levels(keys[4], (SECTIONS,), ((0, 32),), -0.2, 0.2)), 0.25, 1.0),
    }


kernel_sigma = 2.0
force_step = 0.5
elastic_step = 0.1


def kernel_tables(offset, cells, pixels):
    spacing = pixels // cells
    centres = jnp.arange(cells, dtype=jnp.float32)[:, None]
    columns = jnp.arange(pixels, dtype=jnp.float32)[None, :]
    offset_value = jnp.asarray(offset).astype(jnp.float32)
    spread = columns - (spacing * centres + (spacing - 1) / 2.0 + offset_value)
    kernel = jnp.exp(-spread * spread / (2.0 * kernel_sigma * kernel_sigma))
    smooth = kernel / jnp.sum(kernel, axis=1, keepdims=True)
    slopes = smooth * spread / (kernel_sigma * kernel_sigma)
    return smooth.astype(jnp.bfloat16), slopes.astype(jnp.bfloat16)


def pair_cache(picture, offset_rows, offset_cols):
    row_smooth, row_slopes = kernel_tables(offset_rows, GRID, PIXELS)
    col_smooth, col_slopes = kernel_tables(offset_cols, GRID, PIXELS)
    col_tables = jnp.concatenate([col_smooth, col_slopes], axis=0).astype(jnp.float32)
    halfway = jnp.einsum("tpq,gq->tpg", picture.astype(jnp.float32), col_tables).astype(jnp.bfloat16)
    row_tables = jnp.concatenate([row_smooth, row_slopes], axis=0).astype(jnp.float32)
    pooled_rows = jnp.einsum("hp,tpg->thg", row_tables, halfway[:, :, :GRID].astype(jnp.float32))
    across = jnp.einsum("hp,tpg->thg", row_smooth.astype(jnp.float32), halfway[:, :, GRID:].astype(jnp.float32))
    stacked = jnp.stack([pooled_rows[:, :GRID], pooled_rows[:, GRID:], across]).astype(jnp.bfloat16)
    return stacked.reshape(3, -1, GRID)


def own_pool(picture):
    smooth, slopes = kernel_tables(0, GRID, PIXELS)
    halfway = jnp.einsum("tpq,gq->tpg", picture.astype(jnp.float32), smooth.astype(jnp.float32)).astype(jnp.bfloat16)
    pooled = jnp.einsum("hp,tpg->thg", smooth.astype(jnp.float32), halfway.astype(jnp.float32)).astype(jnp.bfloat16)
    return pooled.reshape(-1, GRID)


def laplace(current):
    padded = jnp.pad(current, ((0, 0), (0, 0), (1, 1), (1, 1)))
    beside_all = padded[:, :, 2:, 1:-1] + padded[:, :, :-2, 1:-1] + padded[:, :, 1:-1, 2:] + padded[:, :, 1:-1, :-2]
    return 4.0 * current - beside_all


def reference(images, displacement, offsets, weights, stiffness):
    sections = images.shape[0]
    tiled_images = images.reshape(sections, N_TILE, PIXELS, PIXELS)
    own_pooled = lax.map(own_pool, tiled_images).astype(jnp.float32)
    flat_ids = jnp.arange(sections * SKIPS, dtype=jnp.int32)

    def one_pair(pair_id):
        section = pair_id // SKIPS
        stride = pair_id % SKIPS + 1
        partner = jnp.minimum(section + stride, sections - 1).astype(jnp.int32)
        picture = lax.dynamic_index_in_dim(tiled_images, partner, 0, keepdims=False)
        shifts = offsets[section, stride - 1]
        return pair_cache(picture, shifts[0], shifts[1])

    caches = lax.map(one_pair, flat_ids).reshape(sections, SKIPS, 3, N_TILE * GRID, GRID)
    positions = jnp.arange(sections, dtype=jnp.int32)
    current = displacement
    for step_index in range(ITERS):
        forces = jnp.zeros_like(current)
        for stride in range(1, SKIPS + 1):
            partner = jnp.concatenate([current[stride:], jnp.zeros_like(current[:stride])], axis=0)
            cached = caches[:, stride - 1].astype(jnp.float32)
            mismatch = (cached[:, 0] - own_pooled + cached[:, 1] * (partner[:, 0] - current[:, 0])
                        + cached[:, 2] * (partner[:, 1] - current[:, 1]))
            robust = mismatch / (1.0 + mismatch * mismatch)
            present = (positions + stride < sections).astype(jnp.float32)
            weighting = weights[:, stride - 1].astype(jnp.float32) * present
            pulled = (weighting[:, None, None] * robust)[:, None] * cached[:, 1:3]
            forces = forces + pulled - jnp.concatenate([jnp.zeros_like(pulled[:stride]), pulled[:-stride]], axis=0)
        current = current + force_step * forces - elastic_step * stiffness[:, None, None, None] * laplace(current)
    return current
```

```python
import functools

import jax
import jax.numpy as jnp
from jax import lax
from jax.experimental import pallas as pl
from jax.experimental.pallas import tpu as pltpu
from jax.sharding import PartitionSpec as P

PIXELS = 512
GRID = 128
SKIPS = 3
ITERS = 3
RES = 6
FIELDS = 2 * RES
PAD = 8
BLOCK = 16
F32, BF16 = jnp.float32, jnp.bfloat16
MESH = pl.DeviceIdType.MESH

SEGS = ((0, 16), (112, 16), (16, 32), (48, 32), (80, 32))
CROSS = ((0, 1), (0, 2), (0, 3), (1, 2), (1, 3), (2, 3))
LOCAL = ((1, 1), (2, 1), (2, 2), (3, 1), (3, 2), (3, 3), (4, 1), (4, 2), (4, 3), (5, 1), (5, 2), (5, 3))

kernel_sigma = 2.0
force_step = 0.5
elastic_step = 0.1


def bell(spread, axis):
    peak = jnp.exp(-spread * spread / (2.0 * kernel_sigma * kernel_sigma))
    smooth = peak / jnp.sum(peak, axis=axis, keepdims=True)
    slopes = smooth * spread / (kernel_sigma * kernel_sigma)
    return smooth.astype(BF16), slopes.astype(BF16)


def kernel(disp, images, offsets, weights, stiffness, out, img, rows_t, cols_t, cache, crecv, pool, precv,
           pad_a, pad_b, pad_c, fin, part, usend, uprev, unext, rimsend, rimrecv, meta_v, meta_r, meta_s,
           img_sem, loc_sem, u_ssem, u_rsem, c_ssem, c_rsem, q_sem, rim_ssem, rim_rsem, m_sem):
    me, col = lax.axis_index("sec"), lax.axis_index("tile")
    has_prev, has_next = me > 0, me < lax.axis_size("sec") - 1
    has_up, has_down = col > 0, col < lax.axis_size("tile") - 1
    pads = (pad_a, pad_b, pad_c)

    barrier = pltpu.get_barrier_semaphore()
    sides = ((has_prev, {"sec": me - 1}), (has_next, {"sec": me + 1}), (has_up, {"tile": col - 1}), (has_down, {"tile": col + 1}))
    for there, target in sides:
        @pl.when(there)
        def _():
            pl.semaphore_signal(barrier, inc=1, device_id=target, device_id_type=MESH)

    def fetch(section):
        return pltpu.make_async_copy(images.at[section], img.at[section], img_sem.at[section])

    load_u = pltpu.make_async_copy(disp, pad_a.at[:, pl.ds(PAD, GRID), :], loc_sem.at[0])
    load_u.start()
    for section in (3, 4, 5, 0, 1, 2):
        fetch(section).start()

    spacing = PIXELS // GRID

    def table(offset, carry):
        shift = (spacing - 1) / 2.0 + offset.astype(F32)
        cell = lax.broadcasted_iota(jnp.int32, (GRID, PIXELS), 0).astype(F32)
        pixel = lax.broadcasted_iota(jnp.int32, (GRID, PIXELS), 1).astype(F32)
        smooth, slopes = bell(pixel - (spacing * cell + shift), 1)
        rows_t[offset, 0:GRID, :] = smooth
        rows_t[offset, GRID:2 * GRID, :] = slopes
        cell = lax.broadcasted_iota(jnp.int32, (PIXELS, GRID), 1).astype(F32)
        pixel = lax.broadcasted_iota(jnp.int32, (PIXELS, GRID), 0).astype(F32)
        smooth, slopes = bell(pixel - (spacing * cell + shift), 0)
        cols_t[offset, :, 0:GRID] = smooth
        cols_t[offset, :, GRID:2 * GRID] = slopes
        return carry

    lax.fori_loop(0, SKIPS + 1, table, 0)

    lane = lax.broadcasted_iota(jnp.int32, (8, 128), 1)
    facts = jnp.zeros((8, 128), jnp.int32)
    for section in range(SKIPS):
        for stride in range(SKIPS):
            base = (section * SKIPS + stride) * 3
            facts = jnp.where(lane == base, offsets[(section + SKIPS), stride, 0], facts)
            facts = jnp.where(lane == base + 1, offsets[(section + SKIPS), stride, 1], facts)
            facts = jnp.where(lane == base + 2, weights[(section + SKIPS), stride], facts)
    meta_v[...] = facts

    load_u.wait()

    def halve(block, carry):
        at = pl.ds(pl.multiple_of(block * BLOCK, BLOCK), BLOCK)
        from_pad = pl.ds(pl.multiple_of(block * BLOCK + PAD, PAD), BLOCK)
        for field in range(FIELDS):
            usend[0, field, at, :] = pad_a[field, from_pad, :].astype(BF16)
        return carry

    lax.fori_loop(0, GRID // BLOCK, halve, 0)

    zero_row = jnp.zeros((PAD, GRID), F32)
    for pad in pads:
        for field in range(FIELDS):
            pad[field, 0:PAD, :] = zero_row
            pad[field, PAD + GRID:, :] = zero_row

    def keep_rims(step, source, base):
        for field in range(FIELDS):
            rimsend[step, 0, field:field + 1, :] = source[field, base:base + 1, :]
            rimsend[step, 1, field:field + 1, :] = source[field, base + GRID - 1:base + GRID, :]

    rimsend[...] = jnp.zeros_like(rimsend)
    keep_rims(0, pad_a, PAD)

    @pl.when(jnp.logical_not(has_prev))
    def _():
        meta_r[...] = jnp.zeros_like(meta_r)
        uprev[...] = jnp.zeros_like(uprev)
        precv[...] = jnp.zeros_like(precv)

    @pl.when(jnp.logical_not(has_next))
    def _():
        unext[...] = jnp.zeros_like(unext)
        crecv[...] = jnp.zeros_like(crecv)

    @pl.when(jnp.logical_not(has_up))
    def _():
        rimrecv[:, 1] = jnp.zeros((ITERS, 16, GRID), F32)

    @pl.when(jnp.logical_not(has_down))
    def _():
        rimrecv[:, 0] = jnp.zeros((ITERS, 16, GRID), F32)

    pl.semaphore_wait(barrier, sum(there.astype(jnp.int32) for there, _ in sides))

    half = SKIPS * 2

    def facts_copy():
        return pltpu.make_async_remote_copy(
            src_ref=meta_v, dst_ref=meta_r, send_sem=m_sem.at[0], recv_sem=m_sem.at[1], device_id={"sec": me + 1}, device_id_type=MESH)

    def u_back(step, seg):
        start, size = SEGS[seg]
        at = pl.ds(start, size)
        return pltpu.make_async_remote_copy(
            src_ref=usend.at[step, pl.ds(0, half), at, :], dst_ref=unext.at[step, :, at, :], send_sem=u_ssem.at[step, 0, seg],
            recv_sem=u_rsem.at[step, 0, seg], device_id={"sec": me - 1}, device_id_type=MESH)

    def u_forth(step, seg):
        start, size = SEGS[seg]
        at = pl.ds(start, size)
        return pltpu.make_async_remote_copy(
            src_ref=usend.at[step, pl.ds(half, half), at, :], dst_ref=uprev.at[step, :, at, :], send_sem=u_ssem.at[step, 1, seg],
            recv_sem=u_rsem.at[step, 1, seg], device_id={"sec": me + 1}, device_id_type=MESH)

    def c_back(pair, seg):
        start, size = SEGS[seg]
        at = pl.ds(start, size)
        return pltpu.make_async_remote_copy(
            src_ref=cache.at[pair, :, at, :], dst_ref=crecv.at[pair, :, at, :], send_sem=c_ssem.at[pair, seg],
            recv_sem=c_rsem.at[pair, seg], device_id={"sec": me - 1}, device_id_type=MESH)

    def q_forth():
        return pltpu.make_async_remote_copy(
            src_ref=pool.at[pl.ds(SKIPS, SKIPS)], dst_ref=precv, send_sem=q_sem.at[0], recv_sem=q_sem.at[1],
            device_id={"sec": me + 1}, device_id_type=MESH)

    def rim_copy(step, side):
        target = col - 1 if side == 0 else col + 1
        return pltpu.make_async_remote_copy(
            src_ref=rimsend.at[step, side], dst_ref=rimrecv.at[step, side], send_sem=rim_ssem.at[step, side],
            recv_sem=rim_rsem.at[step, side], device_id={"tile": target}, device_id_type=MESH)

    def send_rims(step):
        @pl.when(has_up)
        def _():
            rim_copy(step, 0).start()

        @pl.when(has_down)
        def _():
            rim_copy(step, 1).start()

    @pl.when(has_next)
    def _():
        facts_copy().start()
        for seg in range(len(SEGS)):
            u_forth(0, seg).start()

    @pl.when(has_prev)
    def _():
        for seg in range(len(SEGS)):
            u_back(0, seg).start()

    send_rims(0)

    def own_pool(section):
        halfway = jnp.dot(img[section], cols_t[0, :, 0:GRID], preferred_element_type=F32).astype(BF16)
        pool[section] = jnp.dot(rows_t[0, 0:GRID, :], halfway, preferred_element_type=F32).astype(BF16)

    def pair_cache(slot, section, off_r, off_c):
        halfway = jnp.dot(img[section], cols_t[off_c], preferred_element_type=F32).astype(BF16)
        pooled = jnp.dot(rows_t[off_r], halfway, preferred_element_type=F32).astype(BF16)
        cache[slot, 0] = pooled[:GRID, :GRID]
        cache[slot, 1] = pooled[GRID:, :GRID]
        cache[slot, 2] = pooled[:GRID, GRID:]

    def own_step(section, carry):
        fetch(section).wait()
        own_pool(section)
        return carry

    lax.fori_loop(SKIPS, RES, own_step, 0)

    @pl.when(has_next)
    def _():
        q_forth().start()

    for section in range(SKIPS):
        fetch(section).wait()

    @pl.when(has_prev)
    def _():
        facts_copy().wait_recv()

    to_scalars = pltpu.make_async_copy(meta_r, meta_s, loc_sem.at[1])
    to_scalars.start()
    to_scalars.wait()

    def cross_step(slot, carry):
        first, second = (slot >= 3).astype(jnp.int32), (slot >= 5).astype(jnp.int32)
        section = first + second
        stride = slot + 1 - 2 * first - second
        base = ((section - stride + SKIPS) * SKIPS + stride - 1) * 3
        pair_cache(slot, section, meta_s[0, base], meta_s[0, base + 1])

        @pl.when(has_prev)
        def _():
            c_back(slot, 0).start()
            c_back(slot, 1).start()

        return carry

    lax.fori_loop(0, len(CROSS), cross_step, 0)

    @pl.when(has_prev)
    def _():
        for seg in range(2, len(SEGS)):
            for pair in range(len(CROSS)):
                c_back(pair, seg).start()

    def own_first(section, carry):
        own_pool(section)
        return carry

    lax.fori_loop(0, SKIPS, own_first, 0)

    def local_step(step, carry):
        late = (step >= 3).astype(jnp.int32)
        section = late * (3 + (step - 3) // 3) + (1 - late) * (1 + (step >= 1).astype(jnp.int32))
        stride = late * ((step - 3) % 3 + 1) + (1 - late) * (1 + (step >= 2).astype(jnp.int32))
        earlier = section - stride
        pair_cache(len(CROSS) + step, section, offsets[earlier, stride - 1, 0], offsets[earlier, stride - 1, 1])
        return carry

    lax.fori_loop(0, len(LOCAL), local_step, 0)

    gain = [[force_step * weights[s, k - 1].astype(F32) for k in range(1, SKIPS + 1)] for s in range(RES)]
    onward = has_next.astype(F32)
    stiff = [elastic_step * stiffness[s] for s in range(RES)]

    def pull(pair_ref, slot, at, earlier_pool, row_gap, col_gap, scale):
        steep = (pair_ref[slot, 1, at, :].astype(F32), pair_ref[slot, 2, at, :].astype(F32))
        miss = pair_ref[slot, 0, at, :].astype(F32) - earlier_pool + steep[0] * row_gap + steep[1] * col_gap
        weighted = scale * (miss / (1.0 + miss * miss))
        return weighted * steep[0], weighted * steep[1]

    def local_pass(pad):
        def block_step(block, carry):
            start = block * BLOCK
            at = pl.ds(pl.multiple_of(start, BLOCK), BLOCK)
            mid = pl.ds(pl.multiple_of(start + PAD, PAD), BLOCK)
            above = pl.ds(start + PAD - 1, BLOCK)
            below = pl.ds(start + PAD + 1, BLOCK)
            edge = lax.broadcasted_iota(jnp.int32, (BLOCK, GRID), 1)
            total = []
            for field in range(FIELDS):
                here = pad[field, mid, :]
                left = jnp.where(edge == 0, 0.0, pltpu.roll(here, 1, 1))
                right = jnp.where(edge == GRID - 1, 0.0, pltpu.roll(here, GRID - 1, 1))
                beside = pad[field, above, :] + pad[field, below, :] + left + right
                total.append(here - stiff[field // 2] * (4.0 * here - beside))
            for index, (later, stride) in enumerate(LOCAL):
                earlier = later - stride
                gaps = [pad[2 * later + c, mid, :] - pad[2 * earlier + c, mid, :] for c in range(2)]
                pulled = pull(cache, len(CROSS) + index, at, pool[earlier, at, :].astype(F32), gaps[0], gaps[1], gain[earlier][stride - 1])
                for c in range(2):
                    total[2 * earlier + c] += pulled[c]
                    total[2 * later + c] -= pulled[c]
            for field in range(FIELDS):
                part[field, at, :] = total[field]
            return carry

        lax.fori_loop(0, GRID // BLOCK, block_step, 0)

    cross_gain = []
    for later, stride in CROSS:
        base = ((later - stride + SKIPS) * SKIPS + stride - 1) * 3
        cross_gain.append(force_step * meta_s[0, base + 2].astype(F32))

    def cross_pass(step, pad, seg):
        first, size = SEGS[seg]

        def block_step(index, carry):
            start = first + index * BLOCK
            at = pl.ds(pl.multiple_of(start, BLOCK), BLOCK)
            mid = pl.ds(pl.multiple_of(start + PAD, PAD), BLOCK)
            total = [part[field, at, :] for field in range(FIELDS)]
            for slot, (later, stride) in enumerate(CROSS):
                earlier = later - stride + SKIPS
                gaps = [pad[2 * later + c, mid, :] - uprev[step, 2 * earlier + c, at, :].astype(F32) for c in range(2)]
                pulled = pull(cache, slot, at, precv[earlier, at, :].astype(F32), gaps[0], gaps[1], cross_gain[slot])
                for c in range(2):
                    total[2 * later + c] -= pulled[c]
            for slot, (later, stride) in enumerate(CROSS):
                earlier = later - stride + RES
                gaps = [unext[step, 2 * later + c, at, :].astype(F32) - pad[2 * earlier + c, mid, :] for c in range(2)]
                pulled = pull(crecv, slot, at, pool[earlier, at, :].astype(F32), gaps[0], gaps[1], onward * gain[earlier][stride - 1])
                for c in range(2):
                    total[2 * earlier + c] += pulled[c]
            for field in range(FIELDS):
                if step + 1 < ITERS:
                    pads[step + 1][field, mid, :] = total[field]
                    usend[step + 1, field, at, :] = total[field].astype(BF16)
                else:
                    fin[field, at, :] = total[field]
            return carry

        lax.fori_loop(0, size // BLOCK, block_step, 0)

    def store(seg):
        start, size = SEGS[seg]
        return pltpu.make_async_copy(fin.at[:, pl.ds(start, size), :], out.at[:, pl.ds(start, size), :], loc_sem.at[2 + seg])

    for step in range(ITERS):
        pad = pads[step]
        local_pass(pad)
        if step == 0:
            @pl.when(has_prev)
            def _():
                q_forth().wait_recv()

        order = (0, 1, 2, 3, 4) if step == 0 else (2, 3, 4, 0, 1)
        for seg in order:
            @pl.when(has_prev)
            def _():
                u_forth(step, seg).wait_recv()

            @pl.when(has_next)
            def _():
                u_back(step, seg).wait_recv()
                if step == 0:
                    for pair in range(len(CROSS)):
                        c_back(pair, seg).wait_recv()

            if seg == 0:
                @pl.when(has_up)
                def _():
                    rim_copy(step, 1).wait_recv()

                for field in range(FIELDS):
                    part[field, 0:1, :] = part[field, 0:1, :] + stiff[field // 2] * rimrecv[step, 1, field:field + 1, :]
            if seg == 1:
                @pl.when(has_down)
                def _():
                    rim_copy(step, 0).wait_recv()

                for field in range(FIELDS):
                    part[field, GRID - 1:GRID, :] = part[field, GRID - 1:GRID, :] + stiff[field // 2] * rimrecv[step, 0, field:field + 1, :]
            cross_pass(step, pad, seg)
            if step + 1 < ITERS:
                @pl.when(has_prev)
                def _():
                    u_back(step + 1, seg).start()

                @pl.when(has_next)
                def _():
                    u_forth(step + 1, seg).start()

                if seg == 1:
                    keep_rims(step + 1, pads[step + 1], PAD)
                    send_rims(step + 1)
            else:
                store(seg).start()

    for seg in range(len(SEGS)):
        store(seg).wait()

    @pl.when(has_prev)
    def _():
        for seg in range(len(SEGS)):
            for step in range(ITERS):
                u_back(step, seg).wait_send()
            for pair in range(len(CROSS)):
                c_back(pair, seg).wait_send()

    @pl.when(has_next)
    def _():
        facts_copy().wait_send()
        q_forth().wait_send()
        for seg in range(len(SEGS)):
            for step in range(ITERS):
                u_forth(step, seg).wait_send()

    for step in range(ITERS):
        @pl.when(has_up)
        def _():
            rim_copy(step, 0).wait_send()

        @pl.when(has_down)
        def _():
            rim_copy(step, 1).wait_send()


def local(images, displacement, offsets, weights, stiffness):
    anywhere = pl.BlockSpec(memory_space=pl.ANY)
    scalars = pl.BlockSpec(memory_space=pltpu.SMEM)
    dma, vmem = pltpu.SemaphoreType.DMA, pltpu.VMEM
    segs, cross = len(SEGS), len(CROSS)
    moved = pl.pallas_call(
        kernel,
        out_shape=jax.ShapeDtypeStruct((FIELDS, GRID, GRID), F32),
        in_specs=[anywhere, anywhere, scalars, scalars, scalars],
        out_specs=anywhere,
        scratch_shapes=[
            vmem((RES, PIXELS, PIXELS), BF16),
            vmem((SKIPS + 1, 2 * GRID, PIXELS), BF16),
            vmem((SKIPS + 1, PIXELS, 2 * GRID), BF16),
            vmem((cross + len(LOCAL), 3, GRID, GRID), BF16),
            vmem((cross, 3, GRID, GRID), BF16),
            vmem((RES, GRID, GRID), BF16),
            vmem((SKIPS, GRID, GRID), BF16),
            vmem((FIELDS, GRID + 2 * PAD, GRID), F32),
            vmem((FIELDS, GRID + 2 * PAD, GRID), F32),
            vmem((FIELDS, GRID + 2 * PAD, GRID), F32),
            vmem((FIELDS, GRID, GRID), F32),
            vmem((FIELDS, GRID, GRID), F32),
            vmem((ITERS, FIELDS, GRID, GRID), BF16),
            vmem((ITERS, 2 * SKIPS, GRID, GRID), BF16),
            vmem((ITERS, 2 * SKIPS, GRID, GRID), BF16),
            vmem((ITERS, 2, 16, GRID), F32),
            vmem((ITERS, 2, 16, GRID), F32),
            vmem((8, 128), jnp.int32),
            vmem((8, 128), jnp.int32),
            pltpu.SMEM((8, 128), jnp.int32),
            dma((RES,)),
            dma((2 + segs,)),
            dma((ITERS, 2, segs)),
            dma((ITERS, 2, segs)),
            dma((cross, segs)),
            dma((cross, segs)),
            dma((2,)),
            dma((ITERS, 2)),
            dma((ITERS, 2)),
            dma((2,)),
        ],
        compiler_params=pltpu.CompilerParams(collective_id=0, has_side_effects=True, vmem_limit_bytes=67_000_000),
    )(displacement.reshape(FIELDS, GRID, GRID), images, offsets, weights, stiffness)
    return moved.reshape(RES, 2, GRID, GRID)


def solution(mesh):
    placed = (
        P("sec", "tile", None),
        P("sec", None, "tile", None),
        P("sec", None, None),
        P("sec", None),
        P("sec"),
    )
    return jax.shard_map(
        local, mesh=mesh, in_specs=placed, out_specs=P("sec", None, "tile", None), check_vma=False
    )
```

```python
import jax
import jax.numpy as jnp
from jax import lax
from jax.experimental import pallas as pl
from jax.experimental.pallas import tpu as pltpu
from jax.sharding import PartitionSpec as P

PIXELS = 512
HALF = PIXELS // 2
GRID = 128
SKIPS = 3
ITERS = 3
RES = 6
FIELDS = 2 * RES
EDGE = 2 * SKIPS
PAD = 8
BLOCK = 16
REACH = 72
MEET = 2 * REACH - GRID
F32, BF16 = jnp.float32, jnp.bfloat16
MESH = pl.DeviceIdType.MESH

SEGS = ((0, 16), (112, 16), (16, 32), (48, 32), (80, 32))
CROSS = ((0, 1), (0, 2), (0, 3), (1, 2), (1, 3), (2, 3))
LOCAL = ((1, 1), (2, 1), (2, 2), (3, 1), (3, 2), (3, 3), (4, 1), (4, 2), (4, 3), (5, 1), (5, 2), (5, 3))

kernel_sigma = 2.0
force_step = 0.5
elastic_step = 0.1


def dot_rows(left, right):
    return lax.dot_general(left, right, (((1,), (1,)), ((), ())), preferred_element_type=F32)


def meet(top, bottom):
    own = REACH - MEET
    return jnp.concatenate([top[:own], top[own:] + bottom[:MEET], bottom[MEET:]], axis=0)


def kernel(disp, images, offsets_hbm, weights_hbm, stiffness_hbm, out, img, first_t, last_t, cache, pool, precv,
           pad_a, pad_b, pad_c, fin, cross_own, usend, uprev, fsend, frecv, rimsend, rimrecv, meta_v, meta_r, meta_s,
           offsets, weights, stiffness, img_sem, loc_sem, u_ssem, u_rsem, f_ssem, f_rsem, q_ssem, q_rsem, rim_ssem, rim_rsem, m_sem):
    me, col = lax.axis_index("sec"), lax.axis_index("tile")
    has_prev, has_next = me > 0, me < lax.axis_size("sec") - 1
    has_up, has_down = col > 0, col < lax.axis_size("tile") - 1
    before, after = {"sec": me - 1}, {"sec": me + 1}
    pads = (pad_a, pad_b, pad_c)
    segments = range(len(SEGS))

    barrier = pltpu.get_barrier_semaphore()
    sides = ((has_prev, before), (has_next, after), (has_up, {"tile": col - 1}), (has_down, {"tile": col + 1}))
    for there, target in sides:
        @pl.when(there)
        def _():
            pl.semaphore_signal(barrier, inc=1, device_id=target, device_id_type=MESH)

    scalars = [pltpu.make_async_copy(src, dst, loc_sem.at[place]) for place, (src, dst) in enumerate(
        ((offsets_hbm, offsets), (weights_hbm, weights), (stiffness_hbm, stiffness)))]
    for copy in scalars:
        copy.start()
    load_u = pltpu.make_async_copy(disp, pad_a.at[:, pl.ds(PAD, GRID), :], loc_sem.at[3])
    load_u.start()

    def fetch(section):
        return pltpu.make_async_copy(images.at[section], img.at[section], img_sem.at[section])

    for section in (3, 4, 5, 0, 1, 2):
        fetch(section).start()

    spacing = PIXELS // GRID

    def table(offset, carry):
        shift = (spacing - 1) / 2.0 + offset.astype(F32)
        cell = lax.broadcasted_iota(jnp.int32, (REACH, HALF), 0).astype(F32)
        pixel = lax.broadcasted_iota(jnp.int32, (REACH, HALF), 1).astype(F32)
        spread, peak, mass = [], [], []
        for low_cell, low_pixel in ((0, 0), (GRID - REACH, HALF)):
            gap = (pixel + low_pixel) - (spacing * (cell + low_cell) + shift)
            spread.append(gap)
            peak.append(jnp.exp(-gap * gap / (2.0 * kernel_sigma * kernel_sigma)))
            mass.append(jnp.sum(peak[-1], axis=1, keepdims=True))
        own = REACH - MEET
        shared = mass[0][own:] + mass[1][:MEET]
        mass = (jnp.concatenate([mass[0][:own], shared], axis=0), jnp.concatenate([shared, mass[1][MEET:]], axis=0))
        for half, ref in enumerate((first_t, last_t)):
            smooth = peak[half] / mass[half]
            ref[offset, 0:REACH, :] = smooth.astype(BF16)
            ref[offset, REACH:2 * REACH, :] = (smooth * spread[half] / (kernel_sigma * kernel_sigma)).astype(BF16)
        return carry

    for copy in scalars:
        copy.wait()

    lane = lax.broadcasted_iota(jnp.int32, (8, 128), 1)
    facts = jnp.zeros((8, 128), jnp.int32)
    for section in range(SKIPS):
        for stride in range(SKIPS):
            base = (section * SKIPS + stride) * 3
            facts = jnp.where(lane == base, offsets[stride, 0, section + SKIPS], facts)
            facts = jnp.where(lane == base + 1, offsets[stride, 1, section + SKIPS], facts)
            facts = jnp.where(lane == base + 2, weights[stride, section + SKIPS], facts)
    meta_v[...] = facts
    rimsend[...] = jnp.zeros_like(rimsend)

    @pl.when(jnp.logical_not(has_prev))
    def _():
        meta_r[...] = jnp.zeros_like(meta_r)
        uprev[...] = jnp.zeros_like(uprev)
        precv[...] = jnp.zeros_like(precv)

    @pl.when(jnp.logical_not(has_next))
    def _():
        frecv[...] = jnp.zeros_like(frecv)

    @pl.when(jnp.logical_not(has_up))
    def _():
        rimrecv[:, 1] = jnp.zeros((ITERS, 16, GRID), F32)

    @pl.when(jnp.logical_not(has_down))
    def _():
        rimrecv[:, 0] = jnp.zeros((ITERS, 16, GRID), F32)

    load_u.wait()

    def halve(block, carry):
        at = pl.ds(pl.multiple_of(block * BLOCK, BLOCK), BLOCK)
        from_pad = pl.ds(pl.multiple_of(block * BLOCK + PAD, PAD), BLOCK)
        for field in range(EDGE):
            usend[0, field, at, :] = pad_a[EDGE + field, from_pad, :].astype(BF16)
        return carry

    lax.fori_loop(0, GRID // BLOCK, halve, 0)

    def keep_rims(step, source):
        for field in range(FIELDS):
            rimsend[step, 0, field:field + 1, :] = source[field, PAD:PAD + 1, :]
            rimsend[step, 1, field:field + 1, :] = source[field, PAD + GRID - 1:PAD + GRID, :]

    keep_rims(0, pad_a)


    pl.semaphore_wait(barrier, sum(there.astype(jnp.int32) for there, _ in sides))


    def remote(src, dst, send_sem, recv_sem, target):
        return pltpu.make_async_remote_copy(
            src_ref=src, dst_ref=dst, send_sem=send_sem, recv_sem=recv_sem, device_id=target, device_id_type=MESH)

    def facts_copy():
        return remote(meta_v, meta_r, m_sem.at[0], m_sem.at[1], after)

    def rows_of(seg):
        start, size = SEGS[seg]
        return pl.ds(start, size)

    def u_forth(step, seg):
        at = rows_of(seg)
        return remote(usend.at[step, :, at, :], uprev.at[step, :, at, :], u_ssem.at[step, seg], u_rsem.at[step, seg], after)

    def f_back(step, seg):
        at = rows_of(seg)
        return remote(fsend.at[step, :, at, :], frecv.at[step, :, at, :], f_ssem.at[step, seg], f_rsem.at[step, seg], before)

    def q_forth(index):
        return remote(pool.at[index + SKIPS], precv.at[index], q_ssem.at[index], q_rsem.at[index], after)

    def rim_copy(step, side):
        target = {"tile": col - 1 if side == 0 else col + 1}
        return remote(rimsend.at[step, side], rimrecv.at[step, side], rim_ssem.at[step, side], rim_rsem.at[step, side], target)

    def send_rims(step):
        @pl.when(has_up)
        def _():
            rim_copy(step, 0).start()

        @pl.when(has_down)
        def _():
            rim_copy(step, 1).start()

    @pl.when(has_next)
    def _():
        facts_copy().start()
        for seg in segments:
            u_forth(0, seg).start()

    send_rims(0)


    lax.fori_loop(0, SKIPS + 1, table, 0)
    zero_row = jnp.zeros((PAD, GRID), F32)
    for pad in pads:
        for field in range(FIELDS):
            pad[field, 0:PAD, :] = zero_row
            pad[field, PAD + GRID:, :] = zero_row

    def columns(section, first, last, count):
        parts = []
        for low in (0, HALF):
            top = dot_rows(first, img[section, low:low + HALF, 0:HALF])
            bottom = dot_rows(last, img[section, low:low + HALF, HALF:])
            parts.append(jnp.concatenate([
                meet(top[REACH * one:REACH * (one + 1)], bottom[REACH * one:REACH * (one + 1)]) for one in range(count)], axis=0).astype(BF16))
        return parts

    def own_pool(section):
        parts = columns(section, first_t[0, 0:REACH, :], last_t[0, 0:REACH, :], 1)
        pool[section] = meet(dot_rows(first_t[0, 0:REACH, :], parts[0]), dot_rows(last_t[0, 0:REACH, :], parts[1])).astype(BF16)

    def pair_cache(slot, section, off_r, off_c):
        parts = columns(section, first_t[off_c], last_t[off_c], 2)
        top, bottom = dot_rows(first_t[off_r], parts[0]), dot_rows(last_t[off_r], parts[1])
        smooth = meet(top[:REACH], bottom[:REACH]).astype(BF16)
        cache[slot, 0] = smooth[:, :GRID]
        cache[slot, 1] = meet(top[REACH:, :GRID], bottom[REACH:, :GRID]).astype(BF16)
        cache[slot, 2] = smooth[:, GRID:]


    def own_step(section, carry):
        fetch(section).wait()
        own_pool(section)

        @pl.when(has_next)
        def _():
            q_forth(section - SKIPS).start()

        return carry

    lax.fori_loop(SKIPS, RES, own_step, 0)

    for section in range(SKIPS):
        fetch(section).wait()


    @pl.when(has_prev)
    def _():
        facts_copy().wait_recv()

    to_scalars = pltpu.make_async_copy(meta_r, meta_s, loc_sem.at[4])
    to_scalars.start()
    to_scalars.wait()


    def cross_step(slot, carry):
        first, second = (slot >= 3).astype(jnp.int32), (slot >= 5).astype(jnp.int32)
        section = first + second
        stride = slot + 1 - 2 * first - second
        base = ((section - stride + SKIPS) * SKIPS + stride - 1) * 3
        pair_cache(slot, section, meta_s[0, base], meta_s[0, base + 1])
        return carry

    lax.fori_loop(0, len(CROSS), cross_step, 0)

    gain = [[force_step * weights[k - 1, s].astype(F32) for k in range(1, SKIPS + 1)] for s in range(RES)]
    stiff = [elastic_step * stiffness[s] for s in range(RES)]
    cross_gain = []
    for later, stride in CROSS:
        base = ((later - stride + SKIPS) * SKIPS + stride - 1) * 3
        cross_gain.append(force_step * meta_s[0, base + 2].astype(F32))

    def pull(slot, at, earlier_pool, row_gap, col_gap, scale):
        steep = (cache[slot, 1, at, :].astype(F32), cache[slot, 2, at, :].astype(F32))
        miss = cache[slot, 0, at, :].astype(F32) - earlier_pool + steep[0] * row_gap + steep[1] * col_gap
        weighted = scale * (miss / (1.0 + miss * miss))
        return weighted * steep[0], weighted * steep[1]

    def over(seg, body):
        start, size = SEGS[seg]

        def block_step(index, carry):
            low = start + index * BLOCK
            body(low, pl.ds(pl.multiple_of(low, BLOCK), BLOCK), pl.ds(pl.multiple_of(low + PAD, PAD), BLOCK))
            return carry

        lax.fori_loop(0, size // BLOCK, block_step, 0)

    def cross_pass(step, seg):
        pad = pads[step]

        def body(low, at, mid):
            own, back = [None] * EDGE, [None] * EDGE
            for slot, (later, stride) in enumerate(CROSS):
                earlier = later - stride + SKIPS
                gaps = [pad[2 * later + c, mid, :] - uprev[step, 2 * earlier + c, at, :].astype(F32) for c in range(2)]
                pulled = pull(slot, at, precv[earlier, at, :].astype(F32), gaps[0], gaps[1], cross_gain[slot])
                for c in range(2):
                    here, there = 2 * later + c, 2 * earlier + c
                    own[here] = pulled[c] if own[here] is None else own[here] + pulled[c]
                    back[there] = pulled[c] if back[there] is None else back[there] + pulled[c]
            for field in range(EDGE):
                cross_own[field, at, :] = own[field]
                fsend[step, field, at, :] = back[field].astype(BF16)

        over(seg, body)

    def cross_turn(step, seg):
        @pl.when(has_prev)
        def _():
            u_forth(step, seg).wait_recv()

        cross_pass(step, seg)

        @pl.when(has_prev)
        def _():
            f_back(step, seg).start()

    def goal(step):
        return (pads[step + 1], PAD) if step + 1 < ITERS else (fin, 0)

    def local_pass(step, seg):
        pad, (target, base) = pads[step], goal(step)

        def body(low, at, mid):
            put = pl.ds(pl.multiple_of(low + base, PAD), BLOCK)
            above, below = pl.ds(low + PAD - 1, BLOCK), pl.ds(low + PAD + 1, BLOCK)
            edge = lax.broadcasted_iota(jnp.int32, (BLOCK, GRID), 1)
            total = []
            for field in range(FIELDS):
                here = pad[field, mid, :]
                left = jnp.where(edge == 0, 0.0, pltpu.roll(here, 1, 1))
                right = jnp.where(edge == GRID - 1, 0.0, pltpu.roll(here, GRID - 1, 1))
                beside = pad[field, above, :] + pad[field, below, :] + left + right
                total.append(here - stiff[field // 2] * (4.0 * here - beside))
                if field < EDGE:
                    total[field] -= cross_own[field, at, :]
            for index, (later, stride) in enumerate(LOCAL):
                earlier = later - stride
                gaps = [pad[2 * later + c, mid, :] - pad[2 * earlier + c, mid, :] for c in range(2)]
                pulled = pull(len(CROSS) + index, at, pool[earlier, at, :].astype(F32), gaps[0], gaps[1], gain[earlier][stride - 1])
                for c in range(2):
                    total[2 * earlier + c] += pulled[c]
                    total[2 * later + c] -= pulled[c]
            for field in range(FIELDS):
                target[field, put, :] = total[field]

        over(seg, body)

    def finish(step, seg):
        target, base = goal(step)
        if seg < 2:
            side, row = ((1, 0), (0, GRID - 1))[seg]

            @pl.when((has_up, has_down)[seg])
            def _():
                rim_copy(step, side).wait_recv()

            for field in range(FIELDS):
                spot = slice(base + row, base + row + 1)
                target[field, spot, :] = target[field, spot, :] + stiff[field // 2] * rimrecv[step, side, field:field + 1, :]

        @pl.when(has_next)
        def _():
            f_back(step, seg).wait_recv()

        def body(low, at, mid):
            put = pl.ds(pl.multiple_of(low + base, PAD), BLOCK)
            for field in range(EDGE):
                done = target[EDGE + field, put, :] + frecv[step, field, at, :].astype(F32)
                target[EDGE + field, put, :] = done
                if step + 1 < ITERS:
                    usend[step + 1, field, at, :] = done.astype(BF16)

        over(seg, body)
        if step + 1 < ITERS:
            @pl.when(has_next)
            def _():
                u_forth(step + 1, seg).start()

            if seg == 1:
                keep_rims(step + 1, pads[step + 1])
                send_rims(step + 1)
        else:
            store(seg).start()

    def store(seg):
        at = rows_of(seg)
        return pltpu.make_async_copy(fin.at[:, at, :], out.at[:, at, :], loc_sem.at[5 + seg])


    @pl.when(has_prev)
    def _():
        for index in range(SKIPS):
            q_forth(index).wait_recv()


    for seg in segments:
        cross_turn(0, seg)


    def own_first(section, carry):
        own_pool(section)
        return carry

    lax.fori_loop(0, SKIPS, own_first, 0)


    def local_step(step, carry):
        late = (step >= 3).astype(jnp.int32)
        section = late * (3 + (step - 3) // 3) + (1 - late) * (1 + (step >= 1).astype(jnp.int32))
        stride = late * ((step - 3) % 3 + 1) + (1 - late) * (1 + (step >= 2).astype(jnp.int32))
        earlier = section - stride
        pair_cache(len(CROSS) + step, section, offsets[stride - 1, 0, earlier], offsets[stride - 1, 1, earlier])
        return carry

    lax.fori_loop(0, len(LOCAL), local_step, 0)

    for step in range(ITERS):
        for seg in segments:
            if step > 0:

                cross_turn(step, seg)

            local_pass(step, seg)
        for seg in segments:

            finish(step, seg)


    for seg in segments:
        store(seg).wait()

    @pl.when(has_prev)
    def _():
        for seg in segments:
            for step in range(ITERS):
                f_back(step, seg).wait_send()

    @pl.when(has_next)
    def _():
        facts_copy().wait_send()
        for index in range(SKIPS):
            q_forth(index).wait_send()
        for seg in segments:
            for step in range(ITERS):
                u_forth(step, seg).wait_send()

    for step in range(ITERS):
        @pl.when(has_up)
        def _():
            rim_copy(step, 0).wait_send()

        @pl.when(has_down)
        def _():
            rim_copy(step, 1).wait_send()


def local(images, displacement, offsets, weights, stiffness):
    anywhere = pl.BlockSpec(memory_space=pl.ANY)
    dma, vmem, smem = pltpu.SemaphoreType.DMA, pltpu.VMEM, pltpu.SMEM
    segs, cross = len(SEGS), len(CROSS)
    moved = pl.pallas_call(
        kernel,
        out_shape=jax.ShapeDtypeStruct((FIELDS, GRID, GRID), F32),
        in_specs=[anywhere] * 5,
        out_specs=anywhere,
        scratch_shapes=[
            vmem((RES, PIXELS, PIXELS), BF16),
            vmem((SKIPS + 1, 2 * REACH, HALF), BF16),
            vmem((SKIPS + 1, 2 * REACH, HALF), BF16),
            vmem((cross + len(LOCAL), 3, GRID, GRID), BF16),
            vmem((RES, GRID, GRID), BF16),
            vmem((SKIPS, GRID, GRID), BF16),
            vmem((FIELDS, GRID + 2 * PAD, GRID), F32),
            vmem((FIELDS, GRID + 2 * PAD, GRID), F32),
            vmem((FIELDS, GRID + 2 * PAD, GRID), F32),
            vmem((FIELDS, GRID, GRID), F32),
            vmem((EDGE, GRID, GRID), F32),
            vmem((ITERS, EDGE, GRID, GRID), BF16),
            vmem((ITERS, EDGE, GRID, GRID), BF16),
            vmem((ITERS, EDGE, GRID, GRID), BF16),
            vmem((ITERS, EDGE, GRID, GRID), BF16),
            vmem((ITERS, 2, 16, GRID), F32),
            vmem((ITERS, 2, 16, GRID), F32),
            vmem((8, 128), jnp.int32),
            vmem((8, 128), jnp.int32),
            smem((8, 128), jnp.int32),
            smem((SKIPS, 2, RES), jnp.int32),
            smem((SKIPS, RES), jnp.int32),
            smem((RES,), F32),
            dma((RES,)),
            dma((5 + segs,)),
            dma((ITERS, segs)),
            dma((ITERS, segs)),
            dma((ITERS, segs)),
            dma((ITERS, segs)),
            dma((SKIPS,)),
            dma((SKIPS,)),
            dma((ITERS, 2)),
            dma((ITERS, 2)),
            dma((2,)),
        ],
        compiler_params=pltpu.CompilerParams(collective_id=0, has_side_effects=True, vmem_limit_bytes=67_000_000),
    )(displacement.reshape(FIELDS, GRID, GRID), images, offsets.transpose(1, 2, 0), weights.T, stiffness)
    return moved.reshape(RES, 2, GRID, GRID)


def solution(mesh):
    placed = (
        P("sec", "tile", None),
        P("sec", None, "tile", None),
        P("sec", None, None),
        P("sec", None),
        P("sec"),
    )
    return jax.shard_map(
        local, mesh=mesh, in_specs=placed, out_specs=P("sec", None, "tile", None), check_vma=False
    )
```

```python
import jax
import jax.numpy as jnp
from jax import lax
from jax.experimental import pallas as pl
from jax.experimental.pallas import tpu as pltpu
from jax.sharding import PartitionSpec as P

PIXELS = 512
HALF = PIXELS // 2
GRID = 128
SKIPS = 3
ITERS = 3
RES = 6
FIELDS = 2 * RES
EDGE = 2 * SKIPS
PAD = 8
BLOCK = 16
REACH = 72
MEET = 2 * REACH - GRID
F32, BF16 = jnp.float32, jnp.bfloat16
MESH = pl.DeviceIdType.MESH
X_SIZE, Z_LOW = 4, 8

SEGS = ((0, 16), (112, 16), (16, 32), (48, 32), (80, 32))
PAIRS = tuple((later, stride) for later in range(RES) for stride in range(1, SKIPS + 1))
CROSS = tuple(pair for pair in PAIRS if pair[0] < pair[1])
LOCAL = tuple(pair for pair in PAIRS if pair[0] >= pair[1])

kernel_sigma = 2.0
force_step = 0.5
elastic_step = 0.1


def slot_of(later, stride):
    return later * SKIPS + stride - 1


def dot_rows(left, right):
    return lax.dot_general(left, right, (((1,), (1,)), ((), ())), preferred_element_type=F32)


def meet(top, bottom):
    own = REACH - MEET
    return jnp.concatenate([top[:own], top[own:] + bottom[:MEET], bottom[MEET:]], axis=0)


def kernel(disp, images, offsets_hbm, weights_hbm, stiffness_hbm, out, img, first_t, last_t, cache, pool, precv,
           pad_a, pad_b, pad_c, fin, cross_own, usend, uprev, fsend, frecv, rimsend, rimrecv, meta_v, meta_r, meta_s, shift_s,
           offsets, weights, stiffness, img_sem, loc_sem, u_ssem, u_rsem, f_ssem, f_rsem, q_ssem, q_rsem, rim_ssem, rim_rsem, m_sem, round_sem):
    me, col = lax.axis_index("sec"), lax.axis_index("tile")
    has_prev, has_next = me > 0, me < lax.axis_size("sec") - 1
    has_up, has_down = col > 0, col < lax.axis_size("tile") - 1
    before, after = {"sec": me - 1}, {"sec": me + 1}
    pads = (pad_a, pad_b, pad_c)
    segments = range(len(SEGS))

    barrier = pltpu.get_barrier_semaphore()
    rank = col % 4
    height, across = (rank // 2) * Z_LOW + me // X_SIZE, me % X_SIZE

    def along(shift):
        to = height + shift
        return (to >= 0) & (to < 2 * Z_LOW), {"sec": (to % Z_LOW) * X_SIZE + across, "tile": col - rank + (to // Z_LOW) * 2 + col % 2}

    def count(*conditions):
        return sum(condition.astype(jnp.int32) for condition in conditions)

    def tell(semaphore, there, target):
        @pl.when(there)
        def _():
            pl.semaphore_signal(semaphore, inc=1, device_id=target, device_id_type=MESH)

    last_col = lax.axis_size("tile") - 1
    upper, lower = along(1), along(-1)
    partner = {"tile": col + 1 - 2 * (col % 2)}
    hears_y = ((rank == 3) & (col < last_col)) | ((rank == 0) & (col > 0))
    tells_y = ((rank == 2) & (col > 2)) | ((rank == 1) & (col < last_col - 3))
    hears_from = {"tile": jnp.where(rank == 3, col + 3, col - 3)}
    tells_core = (rank == 0) | (rank == 3)
    tells_to = {"tile": jnp.where(tells_core, col + 1 - 2 * (col % 2), jnp.where(rank == 1, col + 3, col - 3))}
    has_far = (col > 0) & (col < last_col)
    for there, target in ((has_prev, before), (has_next, after), upper, lower, (col >= 0, partner), (hears_y, hears_from)):
        tell(barrier, there, target)

    scalars = [pltpu.make_async_copy(src, dst, loc_sem.at[place]) for place, (src, dst) in enumerate(
        ((offsets_hbm, offsets), (weights_hbm, weights), (stiffness_hbm, stiffness)))]
    for copy in scalars:
        copy.start()
    load_u = pltpu.make_async_copy(disp, pad_a.at[:, pl.ds(PAD, GRID), :], loc_sem.at[3])
    load_u.start()

    def fetch(section):
        return pltpu.make_async_copy(images.at[section], img.at[section], img_sem.at[section])

    for section in (3, 4, 5, 0, 1, 2):
        fetch(section).start()

    spacing = PIXELS // GRID

    def table(offset, carry):
        shift = (spacing - 1) / 2.0 + offset.astype(F32)
        cell = lax.broadcasted_iota(jnp.int32, (REACH, HALF), 0).astype(F32)
        pixel = lax.broadcasted_iota(jnp.int32, (REACH, HALF), 1).astype(F32)
        spread, peak, mass = [], [], []
        for low_cell, low_pixel in ((0, 0), (GRID - REACH, HALF)):
            gap = (pixel + low_pixel) - (spacing * (cell + low_cell) + shift)
            spread.append(gap)
            peak.append(jnp.exp(-gap * gap / (2.0 * kernel_sigma * kernel_sigma)))
            mass.append(jnp.sum(peak[-1], axis=1, keepdims=True))
        own = REACH - MEET
        shared = mass[0][own:] + mass[1][:MEET]
        mass = (jnp.concatenate([mass[0][:own], shared], axis=0), jnp.concatenate([shared, mass[1][MEET:]], axis=0))
        for half, ref in enumerate((first_t, last_t)):
            smooth = peak[half] / mass[half]
            ref[offset, 0:REACH, :] = smooth.astype(BF16)
            ref[offset, REACH:2 * REACH, :] = (smooth * spread[half] / (kernel_sigma * kernel_sigma)).astype(BF16)
        return carry

    lax.fori_loop(0, SKIPS + 1, table, 0)
    for copy in scalars:
        copy.wait()

    lane = lax.broadcasted_iota(jnp.int32, (8, 128), 1)
    facts = jnp.zeros((8, 128), jnp.int32)
    for section in range(SKIPS):
        for stride in range(SKIPS):
            base = (section * SKIPS + stride) * 3
            facts = jnp.where(lane == base, offsets[stride, 0, section + SKIPS], facts)
            facts = jnp.where(lane == base + 1, offsets[stride, 1, section + SKIPS], facts)
            facts = jnp.where(lane == base + 2, weights[stride, section + SKIPS], facts)
    meta_v[...] = facts
    for section in range(RES):
        for stride in range(SKIPS):
            for axis in range(2):
                shift_s[axis, (section + SKIPS) * SKIPS + stride] = offsets[stride, axis, section]
    rimsend[...] = jnp.zeros_like(rimsend)

    @pl.when(jnp.logical_not(has_prev))
    def _():
        meta_r[...] = jnp.zeros_like(meta_r)
        uprev[...] = jnp.zeros_like(uprev)
        precv[...] = jnp.zeros_like(precv)

    @pl.when(jnp.logical_not(has_next))
    def _():
        frecv[...] = jnp.zeros_like(frecv)

    @pl.when(jnp.logical_not(has_up))
    def _():
        rimrecv[:, 1] = jnp.zeros((ITERS, 16, GRID), F32)

    @pl.when(jnp.logical_not(has_down))
    def _():
        rimrecv[:, 0] = jnp.zeros((ITERS, 16, GRID), F32)

    load_u.wait()

    def halve(block, carry):
        at = pl.ds(pl.multiple_of(block * BLOCK, BLOCK), BLOCK)
        from_pad = pl.ds(pl.multiple_of(block * BLOCK + PAD, PAD), BLOCK)
        for field in range(EDGE):
            usend[0, field, at, :] = pad_a[EDGE + field, from_pad, :].astype(BF16)
        return carry

    lax.fori_loop(0, GRID // BLOCK, halve, 0)

    def keep_rims(step, source):
        for field in range(FIELDS):
            rimsend[step, 0, field:field + 1, :] = source[field, PAD:PAD + 1, :]
            rimsend[step, 1, field:field + 1, :] = source[field, PAD + GRID - 1:PAD + GRID, :]

    keep_rims(0, pad_a)

    pl.semaphore_wait(barrier, count(has_prev, has_next, upper[0], lower[0], col >= 0, tells_y))
    tell(round_sem.at[0], *upper)
    tell(round_sem.at[0], *lower)

    def remote(src, dst, send_sem, recv_sem, target):
        return pltpu.make_async_remote_copy(
            src_ref=src, dst_ref=dst, send_sem=send_sem, recv_sem=recv_sem, device_id=target, device_id_type=MESH)

    def facts_copy():
        return remote(meta_v, meta_r, m_sem.at[0], m_sem.at[1], after)

    def rows_of(seg):
        start, size = SEGS[seg]
        return pl.ds(start, size)

    def u_forth(step, seg):
        at = rows_of(seg)
        return remote(usend.at[step, :, at, :], uprev.at[step, :, at, :], u_ssem.at[step, seg], u_rsem.at[step, seg], after)

    def f_back(step, seg):
        at = rows_of(seg)
        return remote(fsend.at[step, :, at, :], frecv.at[step, :, at, :], f_ssem.at[step, seg], f_rsem.at[step, seg], before)

    def q_forth(index):
        return remote(pool.at[index + SKIPS], precv.at[index], q_ssem.at[index], q_rsem.at[index], after)

    def rim_copy(step, side):
        target = {"tile": col - 1 if side == 0 else col + 1}
        return remote(rimsend.at[step, side], rimrecv.at[step, side], rim_ssem.at[step, side], rim_rsem.at[step, side], target)

    def send_rims(step):
        @pl.when(has_up)
        def _():
            rim_copy(step, 0).start()

        @pl.when(has_down)
        def _():
            rim_copy(step, 1).start()

    @pl.when(has_next)
    def _():
        facts_copy().start()
        for seg in segments[:2]:
            u_forth(0, seg).start()

    zero_row = jnp.zeros((PAD, GRID), F32)
    for pad in pads:
        for field in range(FIELDS):
            pad[field, 0:PAD, :] = zero_row
            pad[field, PAD + GRID:, :] = zero_row

    def columns(section, first, last, count):
        halves = []
        for low in (0, HALF):
            top = dot_rows(first, img[section, low:low + HALF, 0:HALF])
            bottom = dot_rows(last, img[section, low:low + HALF, HALF:])
            halves.append([meet(top[REACH * one:REACH * (one + 1)], bottom[REACH * one:REACH * (one + 1)]).astype(BF16) for one in range(count)])
        return halves

    def section_pool(section):
        shifts = []
        for stride in range(1, SKIPS + 1):
            place = (section - stride + SKIPS) * SKIPS + stride - 1
            shifts.append((shift_s[0, place], shift_s[1, place]))
        first = jnp.concatenate([first_t[off_c] for _, off_c in shifts] + [first_t[0, 0:REACH, :]], axis=0)
        last = jnp.concatenate([last_t[off_c] for _, off_c in shifts] + [last_t[0, 0:REACH, :]], axis=0)
        low, high = columns(section, first, last, 2 * SKIPS + 1)
        for index, (off_r, _) in enumerate(shifts):
            slot = section * SKIPS + index
            top = dot_rows(first_t[off_r], jnp.concatenate(low[2 * index:2 * index + 2], axis=0))
            bottom = dot_rows(last_t[off_r], jnp.concatenate(high[2 * index:2 * index + 2], axis=0))
            smooth = meet(top[:REACH], bottom[:REACH]).astype(BF16)
            cache[slot, 0] = smooth[:, :GRID]
            cache[slot, 1] = meet(top[REACH:, :GRID], bottom[REACH:, :GRID]).astype(BF16)
            cache[slot, 2] = smooth[:, GRID:]
        pool[section] = meet(dot_rows(first_t[0, 0:REACH, :], low[-1]), dot_rows(last_t[0, 0:REACH, :], high[-1])).astype(BF16)

    def late_step(section, carry):
        fetch(section).wait()
        section_pool(section)

        @pl.when(has_next)
        def _():
            q_forth(section - SKIPS).start()

        return carry

    lax.fori_loop(SKIPS, RES - 1, late_step, 0)
    pl.semaphore_wait(round_sem.at[0], count(upper[0], lower[0]))
    tell(round_sem.at[1], *along(2))
    tell(round_sem.at[1], *along(-2))
    lax.fori_loop(RES - 1, RES, late_step, 0)

    @pl.when(has_next)
    def _():
        for seg in segments[2:]:
            u_forth(0, seg).start()

    for section in range(SKIPS):
        fetch(section).wait()

    @pl.when(has_prev)
    def _():
        facts_copy().wait_recv()

    to_scalars = pltpu.make_async_copy(meta_r, meta_s, loc_sem.at[4])
    to_scalars.start()
    to_scalars.wait()
    for place in range(SKIPS * SKIPS):
        for axis in range(2):
            shift_s[axis, place] = meta_s[0, 3 * place + axis]

    pl.semaphore_wait(round_sem.at[1], count(along(2)[0], along(-2)[0]))
    tell(round_sem.at[2], *along(4))
    tell(round_sem.at[2], *along(-4))

    def early_step(section, carry):
        section_pool(section)
        return carry

    lax.fori_loop(0, SKIPS, early_step, 0)

    pl.semaphore_wait(round_sem.at[2], count(along(4)[0], along(-4)[0]))
    tell(round_sem.at[3], tells_core | tells_y, tells_to)

    gain = [[force_step * weights[k - 1, s].astype(F32) for k in range(1, SKIPS + 1)] for s in range(RES)]
    stiff = [elastic_step * stiffness[s] for s in range(RES)]
    cross_gain = []
    for later, stride in CROSS:
        base = ((later - stride + SKIPS) * SKIPS + stride - 1) * 3
        cross_gain.append(force_step * meta_s[0, base + 2].astype(F32))

    def pull(slot, at, earlier_pool, row_gap, col_gap, scale):
        steep = (cache[slot, 1, at, :].astype(F32), cache[slot, 2, at, :].astype(F32))
        miss = cache[slot, 0, at, :].astype(F32) - earlier_pool + steep[0] * row_gap + steep[1] * col_gap
        weighted = scale * (miss / (1.0 + miss * miss))
        return weighted * steep[0], weighted * steep[1]

    def over(seg, body):
        start, size = SEGS[seg]

        def block_step(index, carry):
            low = start + index * BLOCK
            body(low, pl.ds(pl.multiple_of(low, BLOCK), BLOCK), pl.ds(pl.multiple_of(low + PAD, PAD), BLOCK))
            return carry

        lax.fori_loop(0, size // BLOCK, block_step, 0)

    def cross_pass(step, seg):
        pad = pads[step]

        def body(low, at, mid):
            own, back = [None] * EDGE, [None] * EDGE
            for index, (later, stride) in enumerate(CROSS):
                earlier = later - stride + SKIPS
                gaps = [pad[2 * later + c, mid, :] - uprev[step, 2 * earlier + c, at, :].astype(F32) for c in range(2)]
                pulled = pull(slot_of(later, stride), at, precv[earlier, at, :].astype(F32), gaps[0], gaps[1], cross_gain[index])
                for c in range(2):
                    here, there = 2 * later + c, 2 * earlier + c
                    own[here] = pulled[c] if own[here] is None else own[here] + pulled[c]
                    back[there] = pulled[c] if back[there] is None else back[there] + pulled[c]
            for field in range(EDGE):
                cross_own[field, at, :] = own[field]
                fsend[step, field, at, :] = back[field].astype(BF16)

        over(seg, body)

    def cross_turn(step, seg):
        @pl.when(has_prev)
        def _():
            u_forth(step, seg).wait_recv()

        cross_pass(step, seg)

        @pl.when(has_prev)
        def _():
            f_back(step, seg).start()

    def goal(step):
        return (pads[step + 1], PAD) if step + 1 < ITERS else (fin, 0)

    def local_pass(step, seg):
        pad, (target, base) = pads[step], goal(step)

        def body(low, at, mid):
            put = pl.ds(pl.multiple_of(low + base, PAD), BLOCK)
            above, below = pl.ds(low + PAD - 1, BLOCK), pl.ds(low + PAD + 1, BLOCK)
            edge = lax.broadcasted_iota(jnp.int32, (BLOCK, GRID), 1)
            total = []
            for field in range(FIELDS):
                here = pad[field, mid, :]
                left = jnp.where(edge == 0, 0.0, pltpu.roll(here, 1, 1))
                right = jnp.where(edge == GRID - 1, 0.0, pltpu.roll(here, GRID - 1, 1))
                beside = pad[field, above, :] + pad[field, below, :] + left + right
                total.append(here - stiff[field // 2] * (4.0 * here - beside))
                if field < EDGE:
                    total[field] -= cross_own[field, at, :]
            for later, stride in LOCAL:
                earlier = later - stride
                gaps = [pad[2 * later + c, mid, :] - pad[2 * earlier + c, mid, :] for c in range(2)]
                pulled = pull(slot_of(later, stride), at, pool[earlier, at, :].astype(F32), gaps[0], gaps[1], gain[earlier][stride - 1])
                for c in range(2):
                    total[2 * earlier + c] += pulled[c]
                    total[2 * later + c] -= pulled[c]
            for field in range(FIELDS):
                target[field, put, :] = total[field]

        over(seg, body)

    def finish(step, seg):
        target, base = goal(step)
        if seg < 2:
            side, row = ((1, 0), (0, GRID - 1))[seg]

            @pl.when((has_up, has_down)[seg])
            def _():
                rim_copy(step, side).wait_recv()

            for field in range(FIELDS):
                spot = slice(base + row, base + row + 1)
                target[field, spot, :] = target[field, spot, :] + stiff[field // 2] * rimrecv[step, side, field:field + 1, :]

        @pl.when(has_next)
        def _():
            f_back(step, seg).wait_recv()

        def body(low, at, mid):
            put = pl.ds(pl.multiple_of(low + base, PAD), BLOCK)
            for field in range(EDGE):
                done = target[EDGE + field, put, :] + frecv[step, field, at, :].astype(F32)
                target[EDGE + field, put, :] = done
                if step + 1 < ITERS:
                    usend[step + 1, field, at, :] = done.astype(BF16)

        over(seg, body)
        if step + 1 < ITERS:
            @pl.when(has_next)
            def _():
                u_forth(step + 1, seg).start()

            if seg == 1:
                keep_rims(step + 1, pads[step + 1])
                send_rims(step + 1)
        else:
            store(seg).start()

    def store(seg):
        at = rows_of(seg)
        return pltpu.make_async_copy(fin.at[:, at, :], out.at[:, at, :], loc_sem.at[5 + seg])

    @pl.when(has_prev)
    def _():
        for index in range(SKIPS):
            q_forth(index).wait_recv()

    for seg in segments:
        cross_turn(0, seg)

    @pl.when(has_far)
    def _():
        pl.semaphore_wait(round_sem.at[3], 1)

    send_rims(0)

    for step in range(ITERS):
        for seg in segments:
            if step > 0:
                cross_turn(step, seg)
            local_pass(step, seg)
        for seg in segments:
            finish(step, seg)

    for seg in segments:
        store(seg).wait()

    @pl.when(has_prev)
    def _():
        for seg in segments:
            for step in range(ITERS):
                f_back(step, seg).wait_send()

    @pl.when(has_next)
    def _():
        facts_copy().wait_send()
        for index in range(SKIPS):
            q_forth(index).wait_send()
        for seg in segments:
            for step in range(ITERS):
                u_forth(step, seg).wait_send()

    for step in range(ITERS):
        @pl.when(has_up)
        def _():
            rim_copy(step, 0).wait_send()

        @pl.when(has_down)
        def _():
            rim_copy(step, 1).wait_send()


def local(images, displacement, offsets, weights, stiffness):
    anywhere = pl.BlockSpec(memory_space=pl.ANY)
    dma, vmem, smem = pltpu.SemaphoreType.DMA, pltpu.VMEM, pltpu.SMEM
    segs = len(SEGS)
    moved = pl.pallas_call(
        kernel,
        out_shape=jax.ShapeDtypeStruct((FIELDS, GRID, GRID), F32),
        in_specs=[anywhere] * 5,
        out_specs=anywhere,
        scratch_shapes=[
            vmem((RES, PIXELS, PIXELS), BF16),
            vmem((SKIPS + 1, 2 * REACH, HALF), BF16),
            vmem((SKIPS + 1, 2 * REACH, HALF), BF16),
            vmem((len(PAIRS), 3, GRID, GRID), BF16),
            vmem((RES, GRID, GRID), BF16),
            vmem((SKIPS, GRID, GRID), BF16),
            vmem((FIELDS, GRID + 2 * PAD, GRID), F32),
            vmem((FIELDS, GRID + 2 * PAD, GRID), F32),
            vmem((FIELDS, GRID + 2 * PAD, GRID), F32),
            vmem((FIELDS, GRID, GRID), F32),
            vmem((EDGE, GRID, GRID), F32),
            vmem((ITERS, EDGE, GRID, GRID), BF16),
            vmem((ITERS, EDGE, GRID, GRID), BF16),
            vmem((ITERS, EDGE, GRID, GRID), BF16),
            vmem((ITERS, EDGE, GRID, GRID), BF16),
            vmem((ITERS, 2, 16, GRID), F32),
            vmem((ITERS, 2, 16, GRID), F32),
            vmem((8, 128), jnp.int32),
            vmem((8, 128), jnp.int32),
            smem((8, 128), jnp.int32),
            smem((2, (RES + SKIPS) * SKIPS), jnp.int32),
            smem((SKIPS, 2, RES), jnp.int32),
            smem((SKIPS, RES), jnp.int32),
            smem((RES,), F32),
            dma((RES,)),
            dma((5 + segs,)),
            dma((ITERS, segs)),
            dma((ITERS, segs)),
            dma((ITERS, segs)),
            dma((ITERS, segs)),
            dma((SKIPS,)),
            dma((SKIPS,)),
            dma((ITERS, 2)),
            dma((ITERS, 2)),
            dma((2,)),
            pltpu.SemaphoreType.REGULAR((4,)),
        ],
        compiler_params=pltpu.CompilerParams(collective_id=0, has_side_effects=True, vmem_limit_bytes=67_000_000),
    )(displacement.reshape(FIELDS, GRID, GRID), images, offsets.transpose(1, 2, 0), weights.T, stiffness)
    return moved.reshape(RES, 2, GRID, GRID)


def solution(mesh):
    placed = (
        P("sec", "tile", None),
        P("sec", None, "tile", None),
        P("sec", None, None),
        P("sec", None),
        P("sec"),
    )
    return jax.shard_map(
        local, mesh=mesh, in_specs=placed, out_specs=P("sec", None, "tile", None), check_vma=False
    )
```

```python
import jax
import jax.numpy as jnp
from jax import lax
from jax.experimental import pallas as pl
from jax.experimental.pallas import tpu as pltpu
from jax.sharding import PartitionSpec as P

PIXELS = 512
HALF = PIXELS // 2
GRID = 128
SKIPS = 3
ITERS = 3
RES = 6
FIELDS = 2 * RES
EDGE = 2 * SKIPS
PAD = 8
BLOCK = 16
REACH = 72
MEET = 2 * REACH - GRID
F32, BF16 = jnp.float32, jnp.bfloat16
MESH = pl.DeviceIdType.MESH
X_SIZE, Z_LOW = 4, 8

SEGS = ((0, 16), (112, 16), (16, 32), (48, 32), (80, 32))
ORDER = (2, 3, 4, 0, 1)
PAIRS = tuple((later, stride) for later in range(RES) for stride in range(1, SKIPS + 1))
CROSS = tuple(pair for pair in PAIRS if pair[0] < pair[1])
LOCAL = tuple(pair for pair in PAIRS if pair[0] >= pair[1])

kernel_sigma = 2.0
force_step = 0.5
elastic_step = 0.1


def slot_of(later, stride):
    return later * SKIPS + stride - 1


def dot_rows(left, right):
    return lax.dot_general(left, right, (((1,), (1,)), ((), ())), preferred_element_type=F32)


def meet(top, bottom):
    own = REACH - MEET
    return jnp.concatenate([top[:own], top[own:] + bottom[:MEET], bottom[MEET:]], axis=0)


def kernel(disp, images, offsets_hbm, weights_hbm, stiffness_hbm, out, img, first_t, last_t, cache, pool, precv,
           pad_a, pad_b, pad_c, fin, cross_own, usend, uprev, fsend, frecv, rimsend, rimrecv, meta_v, meta_r, meta_s, shift_s,
           offsets, weights, stiffness, img_sem, loc_sem, u_ssem, u_rsem, f_ssem, f_rsem, q_ssem, q_rsem, rim_ssem, rim_rsem, m_sem, round_sem):
    me, col = lax.axis_index("sec"), lax.axis_index("tile")
    has_prev, has_next = me > 0, me < lax.axis_size("sec") - 1
    has_up, has_down = col > 0, col < lax.axis_size("tile") - 1
    before, after = {"sec": me - 1}, {"sec": me + 1}
    pads = (pad_a, pad_b, pad_c)
    segments = range(len(SEGS))

    barrier = pltpu.get_barrier_semaphore()
    rank = col % 4
    height, across = (rank // 2) * Z_LOW + me // X_SIZE, me % X_SIZE

    def along(shift):
        to = height + shift
        return (to >= 0) & (to < 2 * Z_LOW), {"sec": (to % Z_LOW) * X_SIZE + across, "tile": col - rank + (to // Z_LOW) * 2 + col % 2}

    def count(*conditions):
        return sum(condition.astype(jnp.int32) for condition in conditions)

    def tell(semaphore, there, target):
        @pl.when(there)
        def _():
            pl.semaphore_signal(semaphore, inc=1, device_id=target, device_id_type=MESH)

    last_col = lax.axis_size("tile") - 1
    upper, lower = along(1), along(-1)
    partner = {"tile": col + 1 - 2 * (col % 2)}
    hears_y = ((rank == 3) & (col < last_col)) | ((rank == 0) & (col > 0))
    tells_y = ((rank == 2) & (col > 2)) | ((rank == 1) & (col < last_col - 3))
    hears_from = {"tile": jnp.where(rank == 3, col + 3, col - 3)}
    tells_core = (rank == 0) | (rank == 3)
    tells_to = {"tile": jnp.where(tells_core, col + 1 - 2 * (col % 2), jnp.where(rank == 1, col + 3, col - 3))}
    has_far = (col > 0) & (col < last_col)
    for there, target in ((has_prev, before), (has_next, after), upper, lower, (col >= 0, partner), (hears_y, hears_from)):
        tell(barrier, there, target)

    scalars = [pltpu.make_async_copy(src, dst, loc_sem.at[place]) for place, (src, dst) in enumerate(
        ((offsets_hbm, offsets), (weights_hbm, weights), (stiffness_hbm, stiffness)))]
    for copy in scalars:
        copy.start()
    load_u = pltpu.make_async_copy(disp, pad_a.at[:, pl.ds(PAD, GRID), :], loc_sem.at[3])
    load_u.start()

    def fetch(section):
        return pltpu.make_async_copy(images.at[section], img.at[section], img_sem.at[section])

    for section in (3, 4, 5, 0, 1, 2):
        fetch(section).start()

    spacing = PIXELS // GRID

    def table(offset, carry):
        shift = (spacing - 1) / 2.0 + offset.astype(F32)
        cell = lax.broadcasted_iota(jnp.int32, (REACH, HALF), 0).astype(F32)
        pixel = lax.broadcasted_iota(jnp.int32, (REACH, HALF), 1).astype(F32)
        spread, peak, mass = [], [], []
        for low_cell, low_pixel in ((0, 0), (GRID - REACH, HALF)):
            gap = (pixel + low_pixel) - (spacing * (cell + low_cell) + shift)
            spread.append(gap)
            peak.append(jnp.exp(-gap * gap / (2.0 * kernel_sigma * kernel_sigma)))
            mass.append(jnp.sum(peak[-1], axis=1, keepdims=True))
        own = REACH - MEET
        shared = mass[0][own:] + mass[1][:MEET]
        mass = (jnp.concatenate([mass[0][:own], shared], axis=0), jnp.concatenate([shared, mass[1][MEET:]], axis=0))
        for half, ref in enumerate((first_t, last_t)):
            smooth = peak[half] / mass[half]
            ref[offset, 0:REACH, :] = smooth.astype(BF16)
            ref[offset, REACH:2 * REACH, :] = (smooth * spread[half] / (kernel_sigma * kernel_sigma)).astype(BF16)
        return carry

    lax.fori_loop(0, SKIPS + 1, table, 0)
    pl.semaphore_wait(barrier, count(has_prev, has_next, upper[0], lower[0], col >= 0, tells_y))

    def within(low, high):
        return (height >= low) & (height <= high)

    def hear(place, there):
        @pl.when(there)
        def _():
            pl.semaphore_wait(round_sem.at[place], 1)

    def pass_up(low, high):
        here = within(low, high)
        hear(0, here & lower[0])
        there, target = upper
        tell(round_sem.at[0], here & there, target)
        tell(round_sem.at[4], here & (height >= Z_LOW) & (tells_core | tells_y), tells_to)

    def pass_down(step, low, high):
        _, target = along(-(1 << step))
        tell(round_sem.at[1 + step], within(low, high), target)

    pass_down(0, 7, 14)
    pass_up(0, 9)
    for copy in scalars:
        copy.wait()

    lane = lax.broadcasted_iota(jnp.int32, (8, 128), 1)
    facts = jnp.zeros((8, 128), jnp.int32)
    for section in range(SKIPS):
        for stride in range(SKIPS):
            base = (section * SKIPS + stride) * 3
            facts = jnp.where(lane == base, offsets[stride, 0, section + SKIPS], facts)
            facts = jnp.where(lane == base + 1, offsets[stride, 1, section + SKIPS], facts)
            facts = jnp.where(lane == base + 2, weights[stride, section + SKIPS], facts)
    meta_v[...] = facts
    for section in range(RES):
        for stride in range(SKIPS):
            for axis in range(2):
                shift_s[axis, (section + SKIPS) * SKIPS + stride] = offsets[stride, axis, section]
    rimsend[...] = jnp.zeros_like(rimsend)

    @pl.when(jnp.logical_not(has_prev))
    def _():
        meta_r[...] = jnp.zeros_like(meta_r)
        uprev[...] = jnp.zeros_like(uprev)
        precv[...] = jnp.zeros_like(precv)

    @pl.when(jnp.logical_not(has_next))
    def _():
        frecv[...] = jnp.zeros_like(frecv)

    @pl.when(jnp.logical_not(has_up))
    def _():
        rimrecv[:, 1] = jnp.zeros((ITERS, 16, GRID), F32)

    @pl.when(jnp.logical_not(has_down))
    def _():
        rimrecv[:, 0] = jnp.zeros((ITERS, 16, GRID), F32)

    load_u.wait()

    def halve(block, carry):
        at = pl.ds(pl.multiple_of(block * BLOCK, BLOCK), BLOCK)
        from_pad = pl.ds(pl.multiple_of(block * BLOCK + PAD, PAD), BLOCK)
        for field in range(EDGE):
            usend[0, field, at, :] = pad_a[EDGE + field, from_pad, :].astype(BF16)
        return carry

    lax.fori_loop(0, GRID // BLOCK, halve, 0)

    def keep_rims(step, source):
        for field in range(FIELDS):
            rimsend[step, 0, field:field + 1, :] = source[field, PAD:PAD + 1, :]
            rimsend[step, 1, field:field + 1, :] = source[field, PAD + GRID - 1:PAD + GRID, :]

    keep_rims(0, pad_a)

    def remote(src, dst, send_sem, recv_sem, target):
        return pltpu.make_async_remote_copy(
            src_ref=src, dst_ref=dst, send_sem=send_sem, recv_sem=recv_sem, device_id=target, device_id_type=MESH)

    def facts_copy():
        return remote(meta_v, meta_r, m_sem.at[0], m_sem.at[1], after)

    def rows_of(seg):
        start, size = SEGS[seg]
        return pl.ds(start, size)

    def u_forth(step, seg):
        at = rows_of(seg)
        return remote(usend.at[step, :, at, :], uprev.at[step, :, at, :], u_ssem.at[step, seg], u_rsem.at[step, seg], after)

    def f_back(step, seg):
        at = rows_of(seg)
        return remote(fsend.at[step, :, at, :], frecv.at[step, :, at, :], f_ssem.at[step, seg], f_rsem.at[step, seg], before)

    def q_forth(index):
        return remote(pool.at[index + SKIPS], precv.at[index], q_ssem.at[index], q_rsem.at[index], after)

    def rim_copy(step, side):
        target = {"tile": col - 1 if side == 0 else col + 1}
        return remote(rimsend.at[step, side], rimrecv.at[step, side], rim_ssem.at[step, side], rim_rsem.at[step, side], target)

    def send_rims(step):
        @pl.when(has_up)
        def _():
            rim_copy(step, 0).start()

        @pl.when(has_down)
        def _():
            rim_copy(step, 1).start()

    @pl.when(has_next)
    def _():
        facts_copy().start()
        for seg in segments[:2]:
            u_forth(0, seg).start()

    zero_row = jnp.zeros((PAD, GRID), F32)
    for pad in pads:
        for field in range(FIELDS):
            pad[field, 0:PAD, :] = zero_row
            pad[field, PAD + GRID:, :] = zero_row

    def columns(section, first, last, count):
        halves = []
        for low in (0, HALF):
            top = dot_rows(first, img[section, low:low + HALF, 0:HALF])
            bottom = dot_rows(last, img[section, low:low + HALF, HALF:])
            halves.append([meet(top[REACH * one:REACH * (one + 1)], bottom[REACH * one:REACH * (one + 1)]).astype(BF16) for one in range(count)])
        return halves

    def section_pool(section):
        shifts = []
        for stride in range(1, SKIPS + 1):
            place = (section - stride + SKIPS) * SKIPS + stride - 1
            shifts.append((shift_s[0, place], shift_s[1, place]))
        first = jnp.concatenate([first_t[off_c] for _, off_c in shifts] + [first_t[0, 0:REACH, :]], axis=0)
        last = jnp.concatenate([last_t[off_c] for _, off_c in shifts] + [last_t[0, 0:REACH, :]], axis=0)
        low, high = columns(section, first, last, 2 * SKIPS + 1)
        for index, (off_r, _) in enumerate(shifts):
            slot = section * SKIPS + index
            top = dot_rows(first_t[off_r], jnp.concatenate(low[2 * index:2 * index + 2], axis=0))
            bottom = dot_rows(last_t[off_r], jnp.concatenate(high[2 * index:2 * index + 2], axis=0))
            smooth = meet(top[:REACH], bottom[:REACH]).astype(BF16)
            cache[slot, 0] = smooth[:, :GRID]
            cache[slot, 1] = meet(top[REACH:, :GRID], bottom[REACH:, :GRID]).astype(BF16)
            cache[slot, 2] = smooth[:, GRID:]
        pool[section] = meet(dot_rows(first_t[0, 0:REACH, :], low[-1]), dot_rows(last_t[0, 0:REACH, :], high[-1])).astype(BF16)

    def late_step(section, carry):
        fetch(section).wait()
        section_pool(section)

        @pl.when(has_next)
        def _():
            q_forth(section - SKIPS).start()

        return carry

    pass_up(10, 11)
    lax.fori_loop(SKIPS, RES - 1, late_step, 0)
    pass_up(12, 13)
    lax.fori_loop(RES - 1, RES, late_step, 0)
    pass_up(14, 15)
    hear(1, within(6, 13))
    pass_down(1, 6, 13)

    @pl.when(has_next)
    def _():
        for seg in segments[2:]:
            u_forth(0, seg).start()

    for section in range(SKIPS):
        fetch(section).wait()

    @pl.when(has_prev)
    def _():
        facts_copy().wait_recv()

    to_scalars = pltpu.make_async_copy(meta_r, meta_s, loc_sem.at[4])
    to_scalars.start()
    to_scalars.wait()
    for place in range(SKIPS * SKIPS):
        for axis in range(2):
            shift_s[axis, place] = meta_s[0, 3 * place + axis]

    def open_rims(low, high):
        here = within(low, high)
        hear(4, here & has_far)

        @pl.when(here & has_up)
        def _():
            rim_copy(0, 0).start()

        @pl.when(here & has_down)
        def _():
            rim_copy(0, 1).start()

    open_rims(8, 11)
    def early_step(section, carry):
        section_pool(section)
        return carry

    lax.fori_loop(0, SKIPS, early_step, 0)

    open_rims(12, 15)
    hear(2, within(4, 11))
    pass_down(2, 4, 11)

    gain = [[force_step * weights[k - 1, s].astype(F32) for k in range(1, SKIPS + 1)] for s in range(RES)]
    stiff = [elastic_step * stiffness[s] for s in range(RES)]
    cross_gain = []
    for later, stride in CROSS:
        base = ((later - stride + SKIPS) * SKIPS + stride - 1) * 3
        cross_gain.append(force_step * meta_s[0, base + 2].astype(F32))

    def pull(slot, at, earlier_pool, row_gap, col_gap, scale):
        steep = (cache[slot, 1, at, :].astype(F32), cache[slot, 2, at, :].astype(F32))
        miss = cache[slot, 0, at, :].astype(F32) - earlier_pool + steep[0] * row_gap + steep[1] * col_gap
        weighted = scale * (miss / (1.0 + miss * miss))
        return weighted * steep[0], weighted * steep[1]

    def over(seg, body):
        start, size = SEGS[seg]

        def block_step(index, carry):
            low = start + index * BLOCK
            body(low, pl.ds(pl.multiple_of(low, BLOCK), BLOCK), pl.ds(pl.multiple_of(low + PAD, PAD), BLOCK))
            return carry

        lax.fori_loop(0, size // BLOCK, block_step, 0)

    def cross_pass(step, seg):
        pad = pads[step]

        def body(low, at, mid):
            own, back = [None] * EDGE, [None] * EDGE
            for index, (later, stride) in enumerate(CROSS):
                earlier = later - stride + SKIPS
                gaps = [pad[2 * later + c, mid, :] - uprev[step, 2 * earlier + c, at, :].astype(F32) for c in range(2)]
                pulled = pull(slot_of(later, stride), at, precv[earlier, at, :].astype(F32), gaps[0], gaps[1], cross_gain[index])
                for c in range(2):
                    here, there = 2 * later + c, 2 * earlier + c
                    own[here] = pulled[c] if own[here] is None else own[here] + pulled[c]
                    back[there] = pulled[c] if back[there] is None else back[there] + pulled[c]
            for field in range(EDGE):
                cross_own[field, at, :] = own[field]
                fsend[step, field, at, :] = back[field].astype(BF16)

        over(seg, body)

    def cross_turn(step, seg):
        @pl.when(has_prev)
        def _():
            u_forth(step, seg).wait_recv()

        cross_pass(step, seg)

        @pl.when(has_prev)
        def _():
            f_back(step, seg).start()

    def goal(step):
        return (pads[step + 1], PAD) if step + 1 < ITERS else (fin, 0)

    def local_pass(step, seg):
        pad, (target, base) = pads[step], goal(step)

        def body(low, at, mid):
            put = pl.ds(pl.multiple_of(low + base, PAD), BLOCK)
            above, below = pl.ds(low + PAD - 1, BLOCK), pl.ds(low + PAD + 1, BLOCK)
            edge = lax.broadcasted_iota(jnp.int32, (BLOCK, GRID), 1)
            total = []
            for field in range(FIELDS):
                here = pad[field, mid, :]
                left = jnp.where(edge == 0, 0.0, pltpu.roll(here, 1, 1))
                right = jnp.where(edge == GRID - 1, 0.0, pltpu.roll(here, GRID - 1, 1))
                beside = pad[field, above, :] + pad[field, below, :] + left + right
                total.append(here - stiff[field // 2] * (4.0 * here - beside))
                if field < EDGE:
                    total[field] -= cross_own[field, at, :]
            for later, stride in LOCAL:
                earlier = later - stride
                gaps = [pad[2 * later + c, mid, :] - pad[2 * earlier + c, mid, :] for c in range(2)]
                pulled = pull(slot_of(later, stride), at, pool[earlier, at, :].astype(F32), gaps[0], gaps[1], gain[earlier][stride - 1])
                for c in range(2):
                    total[2 * earlier + c] += pulled[c]
                    total[2 * later + c] -= pulled[c]
            for field in range(FIELDS):
                target[field, put, :] = total[field]

        over(seg, body)

    def finish(step, seg):
        target, base = goal(step)
        if seg < 2:
            side, row = ((1, 0), (0, GRID - 1))[seg]

            @pl.when((has_up, has_down)[seg])
            def _():
                rim_copy(step, side).wait_recv()

            for field in range(FIELDS):
                spot = slice(base + row, base + row + 1)
                target[field, spot, :] = target[field, spot, :] + stiff[field // 2] * rimrecv[step, side, field:field + 1, :]

        @pl.when(has_next)
        def _():
            f_back(step, seg).wait_recv()

        def body(low, at, mid):
            put = pl.ds(pl.multiple_of(low + base, PAD), BLOCK)
            for field in range(EDGE):
                done = target[EDGE + field, put, :] + frecv[step, field, at, :].astype(F32)
                target[EDGE + field, put, :] = done
                if step + 1 < ITERS:
                    usend[step + 1, field, at, :] = done.astype(BF16)

        over(seg, body)
        if step + 1 < ITERS:
            @pl.when(has_next)
            def _():
                u_forth(step + 1, seg).start()

            if seg == 1:
                keep_rims(step + 1, pads[step + 1])
                send_rims(step + 1)
        else:
            store(seg).start()

    def store(seg):
        at = rows_of(seg)
        return pltpu.make_async_copy(fin.at[:, at, :], out.at[:, at, :], loc_sem.at[5 + seg])

    @pl.when(has_prev)
    def _():
        for index in range(SKIPS):
            q_forth(index).wait_recv()

    for seg in ORDER:
        cross_turn(0, seg)
    for seg in ORDER:
        local_pass(0, seg)
    hear(3, within(0, 7))
    tell(round_sem.at[4], within(0, 7) & (tells_core | tells_y), tells_to)
    open_rims(0, 7)

    for step in range(ITERS):
        if step > 0:
            for group in (ORDER[:3], ORDER[3:]):
                for seg in group:
                    cross_turn(step, seg)
                for seg in group:
                    local_pass(step, seg)
        for seg in ORDER:
            finish(step, seg)

    for seg in segments:
        store(seg).wait()

    @pl.when(has_prev)
    def _():
        for seg in segments:
            for step in range(ITERS):
                f_back(step, seg).wait_send()

    @pl.when(has_next)
    def _():
        facts_copy().wait_send()
        for index in range(SKIPS):
            q_forth(index).wait_send()
        for seg in segments:
            for step in range(ITERS):
                u_forth(step, seg).wait_send()

    for step in range(ITERS):
        @pl.when(has_up)
        def _():
            rim_copy(step, 0).wait_send()

        @pl.when(has_down)
        def _():
            rim_copy(step, 1).wait_send()


def local(images, displacement, offsets, weights, stiffness):
    anywhere = pl.BlockSpec(memory_space=pl.ANY)
    dma, vmem, smem = pltpu.SemaphoreType.DMA, pltpu.VMEM, pltpu.SMEM
    segs = len(SEGS)
    moved = pl.pallas_call(
        kernel,
        out_shape=jax.ShapeDtypeStruct((FIELDS, GRID, GRID), F32),
        in_specs=[anywhere] * 5,
        out_specs=anywhere,
        scratch_shapes=[
            vmem((RES, PIXELS, PIXELS), BF16),
            vmem((SKIPS + 1, 2 * REACH, HALF), BF16),
            vmem((SKIPS + 1, 2 * REACH, HALF), BF16),
            vmem((len(PAIRS), 3, GRID, GRID), BF16),
            vmem((RES, GRID, GRID), BF16),
            vmem((SKIPS, GRID, GRID), BF16),
            vmem((FIELDS, GRID + 2 * PAD, GRID), F32),
            vmem((FIELDS, GRID + 2 * PAD, GRID), F32),
            vmem((FIELDS, GRID + 2 * PAD, GRID), F32),
            vmem((FIELDS, GRID, GRID), F32),
            vmem((EDGE, GRID, GRID), F32),
            vmem((ITERS, EDGE, GRID, GRID), BF16),
            vmem((ITERS, EDGE, GRID, GRID), BF16),
            vmem((ITERS, EDGE, GRID, GRID), BF16),
            vmem((ITERS, EDGE, GRID, GRID), BF16),
            vmem((ITERS, 2, 16, GRID), F32),
            vmem((ITERS, 2, 16, GRID), F32),
            vmem((8, 128), jnp.int32),
            vmem((8, 128), jnp.int32),
            smem((8, 128), jnp.int32),
            smem((2, (RES + SKIPS) * SKIPS), jnp.int32),
            smem((SKIPS, 2, RES), jnp.int32),
            smem((SKIPS, RES), jnp.int32),
            smem((RES,), F32),
            dma((RES,)),
            dma((5 + segs,)),
            dma((ITERS, segs)),
            dma((ITERS, segs)),
            dma((ITERS, segs)),
            dma((ITERS, segs)),
            dma((SKIPS,)),
            dma((SKIPS,)),
            dma((ITERS, 2)),
            dma((ITERS, 2)),
            dma((2,)),
            pltpu.SemaphoreType.REGULAR((5,)),
        ],
        compiler_params=pltpu.CompilerParams(collective_id=0, has_side_effects=True, vmem_limit_bytes=67_000_000),
    )(displacement.reshape(FIELDS, GRID, GRID), images, offsets.transpose(1, 2, 0), weights.T, stiffness)
    return moved.reshape(RES, 2, GRID, GRID)


def solution(mesh):
    placed = (
        P("sec", "tile", None),
        P("sec", None, "tile", None),
        P("sec", None, None),
        P("sec", None),
        P("sec"),
    )
    return jax.shard_map(
        local, mesh=mesh, in_specs=placed, out_specs=P("sec", None, "tile", None), check_vma=False
    )
```

```python
import jax
import jax.numpy as jnp
from jax import lax
from jax.experimental import pallas as pl
from jax.experimental.pallas import tpu as pltpu
from jax.sharding import PartitionSpec as P

PIXELS = 512
HALF = PIXELS // 2
GRID = 128
SKIPS = 3
ITERS = 3
RES = 6
FIELDS = 2 * RES
EDGE = 2 * SKIPS
PAD = 8
BLOCK = 16
REACH = 72
MEET = 2 * REACH - GRID
F32, BF16 = jnp.float32, jnp.bfloat16
MESH = pl.DeviceIdType.MESH

SEGS = ((0, 16), (112, 16), (16, 32), (48, 32), (80, 32))
PAIRS = tuple((later, stride) for later in range(RES) for stride in range(1, SKIPS + 1))
CROSS = tuple(pair for pair in PAIRS if pair[0] < pair[1])
LOCAL = tuple(pair for pair in PAIRS if pair[0] >= pair[1])

kernel_sigma = 2.0
force_step = 0.5
elastic_step = 0.1


def slot_of(later, stride):
    return later * SKIPS + stride - 1


def dot_rows(left, right):
    return lax.dot_general(left, right, (((1,), (1,)), ((), ())), preferred_element_type=F32)


def meet(top, bottom):
    own = REACH - MEET
    return jnp.concatenate([top[:own], top[own:] + bottom[:MEET], bottom[MEET:]], axis=0)


def kernel(disp, images, offsets_hbm, weights_hbm, stiffness_hbm, out, img, first_t, last_t, cache, pool, precv,
           pad_a, pad_b, pad_c, fin, cross_own, usend, uprev, fsend, frecv, rimsend, rimrecv, meta_v, meta_r, meta_s, shift_s,
           offsets, weights, stiffness, img_sem, loc_sem, u_ssem, u_rsem, f_ssem, f_rsem, q_ssem, q_rsem, rim_ssem, rim_rsem, m_sem, round_sem):
    me, col = lax.axis_index("sec"), lax.axis_index("tile")
    has_prev, has_next = me > 0, me < lax.axis_size("sec") - 1
    has_up, has_down = col > 0, col < lax.axis_size("tile") - 1
    before, after = {"sec": me - 1}, {"sec": me + 1}
    pads = (pad_a, pad_b, pad_c)
    segments = range(len(SEGS))

    barrier = pltpu.get_barrier_semaphore()
    low_half, high_half = col % 4 < 2, col % 4 >= 2
    odd = col % 2
    partner, far = {"tile": col + 1 - 2 * odd}, {"tile": col - 1 + 2 * odd}
    has_far = (col > 0) & (col < lax.axis_size("tile") - 1)

    def tell(semaphore, there, target):
        @pl.when(there)
        def _():
            pl.semaphore_signal(semaphore, inc=1, device_id=target, device_id_type=MESH)

    for there, target in ((low_half & has_far, far), (has_prev, before), (has_next, after), (col >= 0, partner)):
        tell(barrier, there, target)

    scalars = [pltpu.make_async_copy(src, dst, loc_sem.at[place]) for place, (src, dst) in enumerate(
        ((offsets_hbm, offsets), (weights_hbm, weights), (stiffness_hbm, stiffness)))]
    for copy in scalars:
        copy.start()
    load_u = pltpu.make_async_copy(disp, pad_a.at[:, pl.ds(PAD, GRID), :], loc_sem.at[3])
    load_u.start()

    def fetch(section):
        return pltpu.make_async_copy(images.at[section], img.at[section], img_sem.at[section])

    for section in (3, 4, 5, 0, 1, 2):
        fetch(section).start()

    spacing = PIXELS // GRID

    def table(offset, carry):
        shift = (spacing - 1) / 2.0 + offset.astype(F32)
        cell = lax.broadcasted_iota(jnp.int32, (REACH, HALF), 0).astype(F32)
        pixel = lax.broadcasted_iota(jnp.int32, (REACH, HALF), 1).astype(F32)
        spread, peak, mass = [], [], []
        for low_cell, low_pixel in ((0, 0), (GRID - REACH, HALF)):
            gap = (pixel + low_pixel) - (spacing * (cell + low_cell) + shift)
            spread.append(gap)
            peak.append(jnp.exp(-gap * gap / (2.0 * kernel_sigma * kernel_sigma)))
            mass.append(jnp.sum(peak[-1], axis=1, keepdims=True))
        own = REACH - MEET
        shared = mass[0][own:] + mass[1][:MEET]
        mass = (jnp.concatenate([mass[0][:own], shared], axis=0), jnp.concatenate([shared, mass[1][MEET:]], axis=0))
        for half, ref in enumerate((first_t, last_t)):
            smooth = peak[half] / mass[half]
            ref[offset, 0:REACH, :] = smooth.astype(BF16)
            ref[offset, REACH:2 * REACH, :] = (smooth * spread[half] / (kernel_sigma * kernel_sigma)).astype(BF16)
        return carry

    pl.semaphore_wait(barrier, sum(there.astype(jnp.int32) for there in (has_prev, has_next, col >= 0, high_half & has_far)))
    tell(round_sem, high_half & has_far, far)
    lax.fori_loop(0, SKIPS + 1, table, 0)
    for copy in scalars:
        copy.wait()

    lane = lax.broadcasted_iota(jnp.int32, (8, 128), 1)
    facts = jnp.zeros((8, 128), jnp.int32)
    for section in range(SKIPS):
        for stride in range(SKIPS):
            base = (section * SKIPS + stride) * 3
            facts = jnp.where(lane == base, offsets[stride, 0, section + SKIPS], facts)
            facts = jnp.where(lane == base + 1, offsets[stride, 1, section + SKIPS], facts)
            facts = jnp.where(lane == base + 2, weights[stride, section + SKIPS], facts)
    meta_v[...] = facts
    for section in range(RES):
        for stride in range(SKIPS):
            for axis in range(2):
                shift_s[axis, (section + SKIPS) * SKIPS + stride] = offsets[stride, axis, section]
    rimsend[...] = jnp.zeros_like(rimsend)

    @pl.when(jnp.logical_not(has_prev))
    def _():
        meta_r[...] = jnp.zeros_like(meta_r)
        uprev[...] = jnp.zeros_like(uprev)
        precv[...] = jnp.zeros_like(precv)

    @pl.when(jnp.logical_not(has_next))
    def _():
        frecv[...] = jnp.zeros_like(frecv)

    @pl.when(jnp.logical_not(has_up))
    def _():
        rimrecv[:, 1] = jnp.zeros((ITERS, 16, GRID), F32)

    @pl.when(jnp.logical_not(has_down))
    def _():
        rimrecv[:, 0] = jnp.zeros((ITERS, 16, GRID), F32)

    load_u.wait()

    def halve(block, carry):
        at = pl.ds(pl.multiple_of(block * BLOCK, BLOCK), BLOCK)
        from_pad = pl.ds(pl.multiple_of(block * BLOCK + PAD, PAD), BLOCK)
        for field in range(EDGE):
            usend[0, field, at, :] = pad_a[EDGE + field, from_pad, :].astype(BF16)
        return carry

    lax.fori_loop(0, GRID // BLOCK, halve, 0)

    def keep_rims(step, source):
        for field in range(FIELDS):
            rimsend[step, 0, field:field + 1, :] = source[field, PAD:PAD + 1, :]
            rimsend[step, 1, field:field + 1, :] = source[field, PAD + GRID - 1:PAD + GRID, :]

    keep_rims(0, pad_a)

    def remote(src, dst, send_sem, recv_sem, target):
        return pltpu.make_async_remote_copy(
            src_ref=src, dst_ref=dst, send_sem=send_sem, recv_sem=recv_sem, device_id=target, device_id_type=MESH)

    def facts_copy():
        return remote(meta_v, meta_r, m_sem.at[0], m_sem.at[1], after)

    def rows_of(seg):
        start, size = SEGS[seg]
        return pl.ds(start, size)

    def u_forth(step, seg):
        at = rows_of(seg)
        return remote(usend.at[step, :, at, :], uprev.at[step, :, at, :], u_ssem.at[step, seg], u_rsem.at[step, seg], after)

    def f_back(step, seg):
        at = rows_of(seg)
        return remote(fsend.at[step, :, at, :], frecv.at[step, :, at, :], f_ssem.at[step, seg], f_rsem.at[step, seg], before)

    def q_forth(index):
        return remote(pool.at[index + SKIPS], precv.at[index], q_ssem.at[index], q_rsem.at[index], after)

    def rim_copy(step, side):
        target = {"tile": col - 1 if side == 0 else col + 1}
        return remote(rimsend.at[step, side], rimrecv.at[step, side], rim_ssem.at[step, side], rim_rsem.at[step, side], target)

    def send_rims(step):
        @pl.when(has_up)
        def _():
            rim_copy(step, 0).start()

        @pl.when(has_down)
        def _():
            rim_copy(step, 1).start()

    @pl.when(has_next)
    def _():
        facts_copy().start()
        for seg in segments[:2]:
            u_forth(0, seg).start()

    @pl.when(high_half)
    def _():
        send_rims(0)

    zero_row = jnp.zeros((PAD, GRID), F32)
    for pad in pads:
        for field in range(FIELDS):
            pad[field, 0:PAD, :] = zero_row
            pad[field, PAD + GRID:, :] = zero_row

    def columns(section, first, last, count):
        halves = []
        for low in (0, HALF):
            top = dot_rows(first, img[section, low:low + HALF, 0:HALF])
            bottom = dot_rows(last, img[section, low:low + HALF, HALF:])
            halves.append([meet(top[REACH * one:REACH * (one + 1)], bottom[REACH * one:REACH * (one + 1)]).astype(BF16) for one in range(count)])
        return halves

    def section_pool(section):
        shifts = []
        for stride in range(1, SKIPS + 1):
            place = (section - stride + SKIPS) * SKIPS + stride - 1
            shifts.append((shift_s[0, place], shift_s[1, place]))
        first = jnp.concatenate([first_t[off_c] for _, off_c in shifts] + [first_t[0, 0:REACH, :]], axis=0)
        last = jnp.concatenate([last_t[off_c] for _, off_c in shifts] + [last_t[0, 0:REACH, :]], axis=0)
        low, high = columns(section, first, last, 2 * SKIPS + 1)
        for index, (off_r, _) in enumerate(shifts):
            slot = section * SKIPS + index
            top = dot_rows(first_t[off_r], jnp.concatenate(low[2 * index:2 * index + 2], axis=0))
            bottom = dot_rows(last_t[off_r], jnp.concatenate(high[2 * index:2 * index + 2], axis=0))
            smooth = meet(top[:REACH], bottom[:REACH]).astype(BF16)
            cache[slot, 0] = smooth[:, :GRID]
            cache[slot, 1] = meet(top[REACH:, :GRID], bottom[REACH:, :GRID]).astype(BF16)
            cache[slot, 2] = smooth[:, GRID:]
        pool[section] = meet(dot_rows(first_t[0, 0:REACH, :], low[-1]), dot_rows(last_t[0, 0:REACH, :], high[-1])).astype(BF16)

    def late_step(section, carry):
        fetch(section).wait()
        section_pool(section)

        @pl.when(has_next)
        def _():
            q_forth(section - SKIPS).start()

        return carry

    lax.fori_loop(SKIPS, RES, late_step, 0)

    @pl.when(has_next)
    def _():
        for seg in segments[2:]:
            u_forth(0, seg).start()

    for section in range(SKIPS):
        fetch(section).wait()

    @pl.when(has_prev)
    def _():
        facts_copy().wait_recv()

    to_scalars = pltpu.make_async_copy(meta_r, meta_s, loc_sem.at[4])
    to_scalars.start()
    to_scalars.wait()
    for place in range(SKIPS * SKIPS):
        for axis in range(2):
            shift_s[axis, place] = meta_s[0, 3 * place + axis]

    def early_step(section, carry):
        section_pool(section)
        return carry

    lax.fori_loop(0, SKIPS, early_step, 0)

    gain = [[force_step * weights[k - 1, s].astype(F32) for k in range(1, SKIPS + 1)] for s in range(RES)]
    stiff = [elastic_step * stiffness[s] for s in range(RES)]
    cross_gain = []
    for later, stride in CROSS:
        base = ((later - stride + SKIPS) * SKIPS + stride - 1) * 3
        cross_gain.append(force_step * meta_s[0, base + 2].astype(F32))

    def pull(slot, at, earlier_pool, row_gap, col_gap, scale):
        steep = (cache[slot, 1, at, :].astype(F32), cache[slot, 2, at, :].astype(F32))
        miss = cache[slot, 0, at, :].astype(F32) - earlier_pool + steep[0] * row_gap + steep[1] * col_gap
        weighted = scale * (miss / (1.0 + miss * miss))
        return weighted * steep[0], weighted * steep[1]

    def over(seg, body):
        start, size = SEGS[seg]

        def block_step(index, carry):
            low = start + index * BLOCK
            body(low, pl.ds(pl.multiple_of(low, BLOCK), BLOCK), pl.ds(pl.multiple_of(low + PAD, PAD), BLOCK))
            return carry

        lax.fori_loop(0, size // BLOCK, block_step, 0)

    def cross_pass(step, seg):
        pad = pads[step]

        def body(low, at, mid):
            own, back = [None] * EDGE, [None] * EDGE
            for index, (later, stride) in enumerate(CROSS):
                earlier = later - stride + SKIPS
                gaps = [pad[2 * later + c, mid, :] - uprev[step, 2 * earlier + c, at, :].astype(F32) for c in range(2)]
                pulled = pull(slot_of(later, stride), at, precv[earlier, at, :].astype(F32), gaps[0], gaps[1], cross_gain[index])
                for c in range(2):
                    here, there = 2 * later + c, 2 * earlier + c
                    own[here] = pulled[c] if own[here] is None else own[here] + pulled[c]
                    back[there] = pulled[c] if back[there] is None else back[there] + pulled[c]
            for field in range(EDGE):
                cross_own[field, at, :] = own[field]
                fsend[step, field, at, :] = back[field].astype(BF16)

        over(seg, body)

    def cross_turn(step, seg):
        @pl.when(has_prev)
        def _():
            u_forth(step, seg).wait_recv()

        cross_pass(step, seg)

        @pl.when(has_prev)
        def _():
            f_back(step, seg).start()

    def goal(step):
        return (pads[step + 1], PAD) if step + 1 < ITERS else (fin, 0)

    def local_pass(step, seg):
        pad, (target, base) = pads[step], goal(step)

        def body(low, at, mid):
            put = pl.ds(pl.multiple_of(low + base, PAD), BLOCK)
            above, below = pl.ds(low + PAD - 1, BLOCK), pl.ds(low + PAD + 1, BLOCK)
            edge = lax.broadcasted_iota(jnp.int32, (BLOCK, GRID), 1)
            total = []
            for field in range(FIELDS):
                here = pad[field, mid, :]
                left = jnp.where(edge == 0, 0.0, pltpu.roll(here, 1, 1))
                right = jnp.where(edge == GRID - 1, 0.0, pltpu.roll(here, GRID - 1, 1))
                beside = pad[field, above, :] + pad[field, below, :] + left + right
                total.append(here - stiff[field // 2] * (4.0 * here - beside))
                if field < EDGE:
                    total[field] -= cross_own[field, at, :]
            for later, stride in LOCAL:
                earlier = later - stride
                gaps = [pad[2 * later + c, mid, :] - pad[2 * earlier + c, mid, :] for c in range(2)]
                pulled = pull(slot_of(later, stride), at, pool[earlier, at, :].astype(F32), gaps[0], gaps[1], gain[earlier][stride - 1])
                for c in range(2):
                    total[2 * earlier + c] += pulled[c]
                    total[2 * later + c] -= pulled[c]
            for field in range(FIELDS):
                target[field, put, :] = total[field]

        over(seg, body)

    def finish(step, seg):
        target, base = goal(step)
        if seg < 2:
            side, row = ((1, 0), (0, GRID - 1))[seg]

            @pl.when((has_up, has_down)[seg])
            def _():
                rim_copy(step, side).wait_recv()

            for field in range(FIELDS):
                spot = slice(base + row, base + row + 1)
                target[field, spot, :] = target[field, spot, :] + stiff[field // 2] * rimrecv[step, side, field:field + 1, :]

        @pl.when(has_next)
        def _():
            f_back(step, seg).wait_recv()

        def body(low, at, mid):
            put = pl.ds(pl.multiple_of(low + base, PAD), BLOCK)
            for field in range(EDGE):
                done = target[EDGE + field, put, :] + frecv[step, field, at, :].astype(F32)
                target[EDGE + field, put, :] = done
                if step + 1 < ITERS:
                    usend[step + 1, field, at, :] = done.astype(BF16)

        over(seg, body)
        if step + 1 < ITERS:
            @pl.when(has_next)
            def _():
                u_forth(step + 1, seg).start()

            if seg == 1:
                keep_rims(step + 1, pads[step + 1])
                send_rims(step + 1)
        else:
            store(seg).start()

    def store(seg):
        at = rows_of(seg)
        return pltpu.make_async_copy(fin.at[:, at, :], out.at[:, at, :], loc_sem.at[5 + seg])

    @pl.when(has_prev)
    def _():
        for index in range(SKIPS):
            q_forth(index).wait_recv()

    for seg in segments:
        cross_turn(0, seg)
    for seg in segments:
        local_pass(0, seg)
    edges, inner = segments[:2], segments[2:]

    def turns(step, group):
        for seg in group:
            cross_turn(step, seg)

    def passes(step, group):
        for seg in group:
            local_pass(step, seg)

    def finishes(step, group):
        for seg in group:
            finish(step, seg)

    @pl.when(high_half)
    def _():
        finishes(0, segments)
        for step in range(1, ITERS):
            turns(step, edges)
            passes(step, edges)
            turns(step, inner)
            passes(step, inner)
            finishes(step, segments)

    @pl.when(low_half)
    def _():
        finishes(0, inner)
        @pl.when(has_far)
        def _():
            pl.semaphore_wait(round_sem, 1)

        send_rims(0)
        for step in range(1, ITERS):
            turns(step, inner)
            finishes(step - 1, edges)
            turns(step, edges)
            passes(step, segments)
            finishes(step, inner)
        finishes(ITERS - 1, edges)

    for seg in segments:
        store(seg).wait()

    @pl.when(has_prev)
    def _():
        for seg in segments:
            for step in range(ITERS):
                f_back(step, seg).wait_send()

    @pl.when(has_next)
    def _():
        facts_copy().wait_send()
        for index in range(SKIPS):
            q_forth(index).wait_send()
        for seg in segments:
            for step in range(ITERS):
                u_forth(step, seg).wait_send()

    for step in range(ITERS):
        @pl.when(has_up)
        def _():
            rim_copy(step, 0).wait_send()

        @pl.when(has_down)
        def _():
            rim_copy(step, 1).wait_send()


def local(images, displacement, offsets, weights, stiffness):
    anywhere = pl.BlockSpec(memory_space=pl.ANY)
    dma, vmem, smem = pltpu.SemaphoreType.DMA, pltpu.VMEM, pltpu.SMEM
    segs = len(SEGS)
    moved = pl.pallas_call(
        kernel,
        out_shape=jax.ShapeDtypeStruct((FIELDS, GRID, GRID), F32),
        in_specs=[anywhere] * 5,
        out_specs=anywhere,
        scratch_shapes=[
            vmem((RES, PIXELS, PIXELS), BF16),
            vmem((SKIPS + 1, 2 * REACH, HALF), BF16),
            vmem((SKIPS + 1, 2 * REACH, HALF), BF16),
            vmem((len(PAIRS), 3, GRID, GRID), BF16),
            vmem((RES, GRID, GRID), BF16),
            vmem((SKIPS, GRID, GRID), BF16),
            vmem((FIELDS, GRID + 2 * PAD, GRID), F32),
            vmem((FIELDS, GRID + 2 * PAD, GRID), F32),
            vmem((FIELDS, GRID + 2 * PAD, GRID), F32),
            vmem((FIELDS, GRID, GRID), F32),
            vmem((EDGE, GRID, GRID), F32),
            vmem((ITERS, EDGE, GRID, GRID), BF16),
            vmem((ITERS, EDGE, GRID, GRID), BF16),
            vmem((ITERS, EDGE, GRID, GRID), BF16),
            vmem((ITERS, EDGE, GRID, GRID), BF16),
            vmem((ITERS, 2, 16, GRID), F32),
            vmem((ITERS, 2, 16, GRID), F32),
            vmem((8, 128), jnp.int32),
            vmem((8, 128), jnp.int32),
            smem((8, 128), jnp.int32),
            smem((2, (RES + SKIPS) * SKIPS), jnp.int32),
            smem((SKIPS, 2, RES), jnp.int32),
            smem((SKIPS, RES), jnp.int32),
            smem((RES,), F32),
            dma((RES,)),
            dma((5 + segs,)),
            dma((ITERS, segs)),
            dma((ITERS, segs)),
            dma((ITERS, segs)),
            dma((ITERS, segs)),
            dma((SKIPS,)),
            dma((SKIPS,)),
            dma((ITERS, 2)),
            dma((ITERS, 2)),
            dma((2,)),
            pltpu.SemaphoreType.REGULAR,
        ],
        compiler_params=pltpu.CompilerParams(collective_id=0, has_side_effects=True, vmem_limit_bytes=67_000_000),
    )(displacement.reshape(FIELDS, GRID, GRID), images, offsets.transpose(1, 2, 0), weights.T, stiffness)
    return moved.reshape(RES, 2, GRID, GRID)


def solution(mesh):
    placed = (
        P("sec", "tile", None),
        P("sec", None, "tile", None),
        P("sec", None, None),
        P("sec", None),
        P("sec"),
    )
    return jax.shard_map(
        local, mesh=mesh, in_specs=placed, out_specs=P("sec", None, "tile", None), check_vma=False
    )
```

```python
import jax
import jax.numpy as jnp
from jax import lax
from jax.experimental import pallas as pl
from jax.experimental.pallas import tpu as pltpu
from jax.sharding import PartitionSpec as P

PIXELS = 512
HALF = PIXELS // 2
GRID = 128
SKIPS = 3
ITERS = 3
RES = 6
FIELDS = 2 * RES
EDGE = 2 * SKIPS
PAD = 8
BLOCK = 16
REACH = 72
MEET = 2 * REACH - GRID
F32, BF16 = jnp.float32, jnp.bfloat16
MESH = pl.DeviceIdType.MESH

SEGS = ((0, 16), (112, 16), (16, 32), (48, 32), (80, 32))
PAIRS = tuple((later, stride) for later in range(RES) for stride in range(1, SKIPS + 1))
CROSS = tuple(pair for pair in PAIRS if pair[0] < pair[1])
LOCAL = tuple(pair for pair in PAIRS if pair[0] >= pair[1])

kernel_sigma = 2.0
force_step = 0.5
elastic_step = 0.1


def slot_of(later, stride):
    return later * SKIPS + stride - 1


def dot_rows(left, right):
    return lax.dot_general(left, right, (((1,), (1,)), ((), ())), preferred_element_type=F32)


def meet(top, bottom):
    own = REACH - MEET
    return jnp.concatenate([top[:own], top[own:] + bottom[:MEET], bottom[MEET:]], axis=0)


def kernel(disp, images, offsets_hbm, weights_hbm, stiffness_hbm, out, img, first_t, last_t, cache, pool, precv,
           pad_a, pad_b, pad_c, fin, cross_own, usend, uprev, fsend, frecv, rimsend, rimrecv, meta_v, meta_r, meta_s, shift_s,
           offsets, weights, stiffness, img_sem, loc_sem, u_ssem, u_rsem, f_ssem, f_rsem, q_ssem, q_rsem, rim_ssem, rim_rsem, m_sem, round_sem):
    me, col = lax.axis_index("sec"), lax.axis_index("tile")
    has_prev, has_next = me > 0, me < lax.axis_size("sec") - 1
    has_up, has_down = col > 0, col < lax.axis_size("tile") - 1
    before, after = {"sec": me - 1}, {"sec": me + 1}
    pads = (pad_a, pad_b, pad_c)
    segments = range(len(SEGS))

    barrier = pltpu.get_barrier_semaphore()
    low_half, high_half = col % 4 < 2, col % 4 >= 2
    odd = col % 2
    partner, far = {"tile": col + 1 - 2 * odd}, {"tile": col - 1 + 2 * odd}
    has_far = (col > 0) & (col < lax.axis_size("tile") - 1)

    def tell(semaphore, there, target):
        @pl.when(there)
        def _():
            pl.semaphore_signal(semaphore, inc=1, device_id=target, device_id_type=MESH)

    for there, target in ((low_half & has_far, far), (has_prev, before), (has_next, after), (col >= 0, partner)):
        tell(barrier, there, target)

    scalars = [pltpu.make_async_copy(src, dst, loc_sem.at[place]) for place, (src, dst) in enumerate(
        ((offsets_hbm, offsets), (weights_hbm, weights), (stiffness_hbm, stiffness)))]
    for copy in scalars:
        copy.start()
    load_u = pltpu.make_async_copy(disp, pad_a.at[:, pl.ds(PAD, GRID), :], loc_sem.at[3])
    load_u.start()

    def fetch(section):
        return pltpu.make_async_copy(images.at[section], img.at[section], img_sem.at[section])

    for section in (3, 4, 5, 0, 1, 2):
        fetch(section).start()

    spacing = PIXELS // GRID

    def table(offset, carry):
        shift = (spacing - 1) / 2.0 + offset.astype(F32)
        cell = lax.broadcasted_iota(jnp.int32, (REACH, HALF), 0).astype(F32)
        pixel = lax.broadcasted_iota(jnp.int32, (REACH, HALF), 1).astype(F32)
        spread, peak, mass = [], [], []
        for low_cell, low_pixel in ((0, 0), (GRID - REACH, HALF)):
            gap = (pixel + low_pixel) - (spacing * (cell + low_cell) + shift)
            spread.append(gap)
            peak.append(jnp.exp(-gap * gap / (2.0 * kernel_sigma * kernel_sigma)))
            mass.append(jnp.sum(peak[-1], axis=1, keepdims=True))
        own = REACH - MEET
        shared = mass[0][own:] + mass[1][:MEET]
        mass = (jnp.concatenate([mass[0][:own], shared], axis=0), jnp.concatenate([shared, mass[1][MEET:]], axis=0))
        for half, ref in enumerate((first_t, last_t)):
            smooth = peak[half] / mass[half]
            ref[offset, 0:REACH, :] = smooth.astype(BF16)
            ref[offset, REACH:2 * REACH, :] = (smooth * spread[half] / (kernel_sigma * kernel_sigma)).astype(BF16)
        return carry

    lax.fori_loop(0, SKIPS + 1, table, 0)
    for copy in scalars:
        copy.wait()

    lane = lax.broadcasted_iota(jnp.int32, (8, 128), 1)
    facts = jnp.zeros((8, 128), jnp.int32)
    for section in range(SKIPS):
        for stride in range(SKIPS):
            base = (section * SKIPS + stride) * 3
            facts = jnp.where(lane == base, offsets[stride, 0, section + SKIPS], facts)
            facts = jnp.where(lane == base + 1, offsets[stride, 1, section + SKIPS], facts)
            facts = jnp.where(lane == base + 2, weights[stride, section + SKIPS], facts)
    meta_v[...] = facts
    for section in range(RES):
        for stride in range(SKIPS):
            for axis in range(2):
                shift_s[axis, (section + SKIPS) * SKIPS + stride] = offsets[stride, axis, section]
    rimsend[...] = jnp.zeros_like(rimsend)

    @pl.when(jnp.logical_not(has_prev))
    def _():
        meta_r[...] = jnp.zeros_like(meta_r)
        uprev[...] = jnp.zeros_like(uprev)
        precv[...] = jnp.zeros_like(precv)

    @pl.when(jnp.logical_not(has_next))
    def _():
        frecv[...] = jnp.zeros_like(frecv)

    @pl.when(jnp.logical_not(has_up))
    def _():
        rimrecv[:, 1] = jnp.zeros((ITERS, 16, GRID), F32)

    @pl.when(jnp.logical_not(has_down))
    def _():
        rimrecv[:, 0] = jnp.zeros((ITERS, 16, GRID), F32)

    load_u.wait()

    def halve(block, carry):
        at = pl.ds(pl.multiple_of(block * BLOCK, BLOCK), BLOCK)
        from_pad = pl.ds(pl.multiple_of(block * BLOCK + PAD, PAD), BLOCK)
        for field in range(EDGE):
            usend[0, field, at, :] = pad_a[EDGE + field, from_pad, :].astype(BF16)
        return carry

    lax.fori_loop(0, GRID // BLOCK, halve, 0)

    def keep_rims(step, source):
        for field in range(FIELDS):
            rimsend[step, 0, field:field + 1, :] = source[field, PAD:PAD + 1, :]
            rimsend[step, 1, field:field + 1, :] = source[field, PAD + GRID - 1:PAD + GRID, :]

    keep_rims(0, pad_a)

    pl.semaphore_wait(barrier, sum(there.astype(jnp.int32) for there in (has_prev, has_next, col >= 0, high_half & has_far)))
    tell(round_sem, high_half & has_far, far)

    def remote(src, dst, send_sem, recv_sem, target):
        return pltpu.make_async_remote_copy(
            src_ref=src, dst_ref=dst, send_sem=send_sem, recv_sem=recv_sem, device_id=target, device_id_type=MESH)

    def facts_copy():
        return remote(meta_v, meta_r, m_sem.at[0], m_sem.at[1], after)

    def rows_of(seg):
        start, size = SEGS[seg]
        return pl.ds(start, size)

    def u_forth(step, seg):
        at = rows_of(seg)
        return remote(usend.at[step, :, at, :], uprev.at[step, :, at, :], u_ssem.at[step, seg], u_rsem.at[step, seg], after)

    def f_back(step, seg):
        at = rows_of(seg)
        return remote(fsend.at[step, :, at, :], frecv.at[step, :, at, :], f_ssem.at[step, seg], f_rsem.at[step, seg], before)

    def q_forth(seg):
        at = rows_of(seg)
        return remote(pool.at[pl.ds(SKIPS, SKIPS), at, :], precv.at[:, at, :], q_ssem.at[seg], q_rsem.at[seg], after)

    def rim_copy(step, side):
        target = {"tile": col - 1 if side == 0 else col + 1}
        return remote(rimsend.at[step, side], rimrecv.at[step, side], rim_ssem.at[step, side], rim_rsem.at[step, side], target)

    def send_rims(step):
        @pl.when(has_up)
        def _():
            rim_copy(step, 0).start()

        @pl.when(has_down)
        def _():
            rim_copy(step, 1).start()

    @pl.when(has_next)
    def _():
        facts_copy().start()
        for seg in segments:
            u_forth(0, seg).start()

    @pl.when(high_half)
    def _():
        send_rims(0)

    zero_row = jnp.zeros((PAD, GRID), F32)
    for pad in pads:
        for field in range(FIELDS):
            pad[field, 0:PAD, :] = zero_row
            pad[field, PAD + GRID:, :] = zero_row

    def columns(section, first, last, count):
        halves = []
        for low in (0, HALF):
            top = dot_rows(first, img[section, low:low + HALF, 0:HALF])
            bottom = dot_rows(last, img[section, low:low + HALF, HALF:])
            halves.append([meet(top[REACH * one:REACH * (one + 1)], bottom[REACH * one:REACH * (one + 1)]).astype(BF16) for one in range(count)])
        return halves

    def section_pool(section):
        shifts = []
        for stride in range(1, SKIPS + 1):
            place = (section - stride + SKIPS) * SKIPS + stride - 1
            shifts.append((shift_s[0, place], shift_s[1, place]))
        first = jnp.concatenate([first_t[off_c] for _, off_c in shifts] + [first_t[0, 0:REACH, :]], axis=0)
        last = jnp.concatenate([last_t[off_c] for _, off_c in shifts] + [last_t[0, 0:REACH, :]], axis=0)
        low, high = columns(section, first, last, 2 * SKIPS + 1)
        for index, (off_r, _) in enumerate(shifts):
            slot = section * SKIPS + index
            top = dot_rows(first_t[off_r], jnp.concatenate(low[2 * index:2 * index + 2], axis=0))
            bottom = dot_rows(last_t[off_r], jnp.concatenate(high[2 * index:2 * index + 2], axis=0))
            smooth = meet(top[:REACH], bottom[:REACH]).astype(BF16)
            cache[slot, 0] = smooth[:, :GRID]
            cache[slot, 1] = meet(top[REACH:, :GRID], bottom[REACH:, :GRID]).astype(BF16)
            cache[slot, 2] = smooth[:, GRID:]
        pool[section] = meet(dot_rows(first_t[0, 0:REACH, :], low[-1]), dot_rows(last_t[0, 0:REACH, :], high[-1])).astype(BF16)

    def late_step(section, carry):
        fetch(section).wait()
        section_pool(section)
        return carry

    lax.fori_loop(SKIPS, RES, late_step, 0)

    @pl.when(has_next)
    def _():
        for seg in segments:
            q_forth(seg).start()

    for section in range(SKIPS):
        fetch(section).wait()

    @pl.when(has_prev)
    def _():
        facts_copy().wait_recv()

    to_scalars = pltpu.make_async_copy(meta_r, meta_s, loc_sem.at[4])
    to_scalars.start()
    to_scalars.wait()
    for place in range(SKIPS * SKIPS):
        for axis in range(2):
            shift_s[axis, place] = meta_s[0, 3 * place + axis]

    def early_step(section, carry):
        section_pool(section)
        return carry

    lax.fori_loop(0, SKIPS, early_step, 0)

    gain = [[force_step * weights[k - 1, s].astype(F32) for k in range(1, SKIPS + 1)] for s in range(RES)]
    stiff = [elastic_step * stiffness[s] for s in range(RES)]
    cross_gain = []
    for later, stride in CROSS:
        base = ((later - stride + SKIPS) * SKIPS + stride - 1) * 3
        cross_gain.append(force_step * meta_s[0, base + 2].astype(F32))

    def pull(slot, at, earlier_pool, row_gap, col_gap, scale):
        steep = (cache[slot, 1, at, :].astype(F32), cache[slot, 2, at, :].astype(F32))
        miss = cache[slot, 0, at, :].astype(F32) - earlier_pool + steep[0] * row_gap + steep[1] * col_gap
        weighted = scale * (miss / (1.0 + miss * miss))
        return weighted * steep[0], weighted * steep[1]

    def over(seg, body):
        start, size = SEGS[seg]

        def block_step(index, carry):
            low = start + index * BLOCK
            body(low, pl.ds(pl.multiple_of(low, BLOCK), BLOCK), pl.ds(pl.multiple_of(low + PAD, PAD), BLOCK))
            return carry

        lax.fori_loop(0, size // BLOCK, block_step, 0)

    def cross_pass(step, seg):
        pad = pads[step]

        def body(low, at, mid):
            own, back = [None] * EDGE, [None] * EDGE
            for index, (later, stride) in enumerate(CROSS):
                earlier = later - stride + SKIPS
                gaps = [pad[2 * later + c, mid, :] - uprev[step, 2 * earlier + c, at, :].astype(F32) for c in range(2)]
                pulled = pull(slot_of(later, stride), at, precv[earlier, at, :].astype(F32), gaps[0], gaps[1], cross_gain[index])
                for c in range(2):
                    here, there = 2 * later + c, 2 * earlier + c
                    own[here] = pulled[c] if own[here] is None else own[here] + pulled[c]
                    back[there] = pulled[c] if back[there] is None else back[there] + pulled[c]
            for field in range(EDGE):
                cross_own[field, at, :] = own[field]
                fsend[step, field, at, :] = back[field].astype(BF16)

        over(seg, body)

    def cross_turn(step, seg):
        @pl.when(has_prev)
        def _():
            u_forth(step, seg).wait_recv()
            if step == 0:
                q_forth(seg).wait_recv()

        cross_pass(step, seg)

        @pl.when(has_prev)
        def _():
            f_back(step, seg).start()

    def goal(step):
        return (pads[step + 1], PAD) if step + 1 < ITERS else (fin, 0)

    def local_pass(step, seg):
        pad, (target, base) = pads[step], goal(step)

        def body(low, at, mid):
            put = pl.ds(pl.multiple_of(low + base, PAD), BLOCK)
            above, below = pl.ds(low + PAD - 1, BLOCK), pl.ds(low + PAD + 1, BLOCK)
            edge = lax.broadcasted_iota(jnp.int32, (BLOCK, GRID), 1)
            total = []
            for field in range(FIELDS):
                here = pad[field, mid, :]
                left = jnp.where(edge == 0, 0.0, pltpu.roll(here, 1, 1))
                right = jnp.where(edge == GRID - 1, 0.0, pltpu.roll(here, GRID - 1, 1))
                beside = pad[field, above, :] + pad[field, below, :] + left + right
                total.append(here - stiff[field // 2] * (4.0 * here - beside))
                if field < EDGE:
                    total[field] -= cross_own[field, at, :]
            for later, stride in LOCAL:
                earlier = later - stride
                gaps = [pad[2 * later + c, mid, :] - pad[2 * earlier + c, mid, :] for c in range(2)]
                pulled = pull(slot_of(later, stride), at, pool[earlier, at, :].astype(F32), gaps[0], gaps[1], gain[earlier][stride - 1])
                for c in range(2):
                    total[2 * earlier + c] += pulled[c]
                    total[2 * later + c] -= pulled[c]
            for field in range(FIELDS):
                target[field, put, :] = total[field]

        over(seg, body)

    def finish(step, seg):
        target, base = goal(step)
        if seg < 2:
            side, row = ((1, 0), (0, GRID - 1))[seg]

            @pl.when((has_up, has_down)[seg])
            def _():
                rim_copy(step, side).wait_recv()

            for field in range(FIELDS):
                spot = slice(base + row, base + row + 1)
                target[field, spot, :] = target[field, spot, :] + stiff[field // 2] * rimrecv[step, side, field:field + 1, :]

        @pl.when(has_next)
        def _():
            f_back(step, seg).wait_recv()

        def body(low, at, mid):
            put = pl.ds(pl.multiple_of(low + base, PAD), BLOCK)
            for field in range(EDGE):
                done = target[EDGE + field, put, :] + frecv[step, field, at, :].astype(F32)
                target[EDGE + field, put, :] = done
                if step + 1 < ITERS:
                    usend[step + 1, field, at, :] = done.astype(BF16)

        over(seg, body)
        if step + 1 < ITERS:
            @pl.when(has_next)
            def _():
                u_forth(step + 1, seg).start()

            if seg == 1:
                keep_rims(step + 1, pads[step + 1])
                send_rims(step + 1)
        else:
            store(seg).start()

    def store(seg):
        at = rows_of(seg)
        return pltpu.make_async_copy(fin.at[:, at, :], out.at[:, at, :], loc_sem.at[5 + seg])

    edges, inner = segments[:2], segments[2:]

    def turns(step, *group):
        for seg in group:
            cross_turn(step, seg)

    def passes(step, *group):
        for seg in group:
            local_pass(step, seg)

    def finishes(step, *group):
        for seg in group:
            finish(step, seg)

    for seg in segments:
        turns(0, seg)
        passes(0, seg)

    @pl.when(high_half)
    def _():
        finishes(0, 2, 0, 1, 3, 4)
        turns(1, 2, 0, 1)
        passes(1, 0, 1, 2)
        turns(1, 3)
        passes(1, 3)
        finishes(1, 0, 1)
        turns(1, 4)
        passes(1, 4)
        finishes(1, 2)
        turns(2, 0, 1)
        finishes(1, 3, 4)
        passes(2, 0, 1)
        turns(2, 2)
        passes(2, 2)
        turns(2, 3)
        passes(2, 3)
        turns(2, 4)
        passes(2, 4)
        finishes(2, 2, 3, 4, 0, 1)

    @pl.when(low_half)
    def _():
        finishes(0, *inner)
        @pl.when(has_far)
        def _():
            pl.semaphore_wait(round_sem, 1)

        send_rims(0)
        for step in range(1, ITERS):
            turns(step, *inner)
            finishes(step - 1, *edges)
            passes(step, *inner)
            turns(step, *edges)
            passes(step, *edges)
            finishes(step, *inner)
        finishes(ITERS - 1, *edges)

    for seg in segments:
        store(seg).wait()

    @pl.when(has_prev)
    def _():
        for seg in segments:
            for step in range(ITERS):
                f_back(step, seg).wait_send()

    @pl.when(has_next)
    def _():
        facts_copy().wait_send()
        for seg in segments:
            q_forth(seg).wait_send()
        for seg in segments:
            for step in range(ITERS):
                u_forth(step, seg).wait_send()

    for step in range(ITERS):
        @pl.when(has_up)
        def _():
            rim_copy(step, 0).wait_send()

        @pl.when(has_down)
        def _():
            rim_copy(step, 1).wait_send()


def local(images, displacement, offsets, weights, stiffness):
    anywhere = pl.BlockSpec(memory_space=pl.ANY)
    dma, vmem, smem = pltpu.SemaphoreType.DMA, pltpu.VMEM, pltpu.SMEM
    segs = len(SEGS)
    given = (displacement.reshape(FIELDS, GRID, GRID), images, offsets.transpose(1, 2, 0), weights.T, stiffness)
    moved = pl.pallas_call(
        kernel,
        out_shape=jax.ShapeDtypeStruct((FIELDS, GRID, GRID), F32),
        in_specs=[anywhere] * 5,
        out_specs=anywhere,
        scratch_shapes=[
            vmem((RES, PIXELS, PIXELS), BF16),
            vmem((SKIPS + 1, 2 * REACH, HALF), BF16),
            vmem((SKIPS + 1, 2 * REACH, HALF), BF16),
            vmem((len(PAIRS), 3, GRID, GRID), BF16),
            vmem((RES, GRID, GRID), BF16),
            vmem((SKIPS, GRID, GRID), BF16),
            vmem((FIELDS, GRID + 2 * PAD, GRID), F32),
            vmem((FIELDS, GRID + 2 * PAD, GRID), F32),
            vmem((FIELDS, GRID + 2 * PAD, GRID), F32),
            vmem((FIELDS, GRID, GRID), F32),
            vmem((EDGE, GRID, GRID), F32),
            vmem((ITERS, EDGE, GRID, GRID), BF16),
            vmem((ITERS, EDGE, GRID, GRID), BF16),
            vmem((ITERS, EDGE, GRID, GRID), BF16),
            vmem((ITERS, EDGE, GRID, GRID), BF16),
            vmem((ITERS, 2, 16, GRID), F32),
            vmem((ITERS, 2, 16, GRID), F32),
            vmem((8, 128), jnp.int32),
            vmem((8, 128), jnp.int32),
            smem((8, 128), jnp.int32),
            smem((2, (RES + SKIPS) * SKIPS), jnp.int32),
            smem((SKIPS, 2, RES), jnp.int32),
            smem((SKIPS, RES), jnp.int32),
            smem((RES,), F32),
            dma((RES,)),
            dma((5 + segs,)),
            dma((ITERS, segs)),
            dma((ITERS, segs)),
            dma((ITERS, segs)),
            dma((ITERS, segs)),
            dma((segs,)),
            dma((segs,)),
            dma((ITERS, 2)),
            dma((ITERS, 2)),
            dma((2,)),
            pltpu.SemaphoreType.REGULAR,
        ],
        compiler_params=pltpu.CompilerParams(collective_id=0, has_side_effects=True, vmem_limit_bytes=24 << 20),
    )(*(pltpu.with_memory_space_constraint(each, pltpu.HBM) for each in given))
    return moved.reshape(RES, 2, GRID, GRID)


def solution(mesh):
    placed = (
        P("sec", "tile", None),
        P("sec", None, "tile", None),
        P("sec", None, None),
        P("sec", None),
        P("sec"),
    )
    return jax.shard_map(
        local, mesh=mesh, in_specs=placed, out_specs=P("sec", None, "tile", None), check_vma=False
    )
```

```python
import jax
import jax.numpy as jnp
from jax import lax
from jax.experimental import pallas as pl
from jax.experimental.pallas import tpu as pltpu
from jax.sharding import PartitionSpec as P

PIXELS = 512
HALF = PIXELS // 2
GRID = 128
SKIPS = 3
ITERS = 3
RES = 6
FIELDS = 2 * RES
EDGE = 2 * SKIPS
PAD = 8
BLOCK = 16
REACH = 72
MEET = 2 * REACH - GRID
F32, BF16 = jnp.float32, jnp.bfloat16
MESH = pl.DeviceIdType.MESH

SEGS = ((0, 16), (112, 16), (16, 32), (48, 32), (80, 32))
PAIRS = tuple((later, stride) for later in range(RES) for stride in range(1, SKIPS + 1))
CROSS = tuple(pair for pair in PAIRS if pair[0] < pair[1])
LOCAL = tuple(pair for pair in PAIRS if pair[0] >= pair[1])

kernel_sigma = 2.0
force_step = 0.5
elastic_step = 0.1


def slot_of(later, stride):
    return later * SKIPS + stride - 1


def dot_rows(left, right):
    return lax.dot_general(left, right, (((1,), (1,)), ((), ())), preferred_element_type=F32)


def meet(top, bottom):
    own = REACH - MEET
    return jnp.concatenate([top[:own], top[own:] + bottom[:MEET], bottom[MEET:]], axis=0)


def kernel(disp, images, offsets_hbm, weights_hbm, stiffness_hbm, out, img, first_t, last_t, cache, pool, precv,
           pad_a, pad_b, pad_c, fin, cross_own, usend, uprev, fsend, frecv, rimsend, rimrecv, meta_v, meta_r, meta_s, shift_s,
           offsets, weights, stiffness, img_sem, loc_sem, u_ssem, u_rsem, f_ssem, f_rsem, q_ssem, q_rsem, rim_ssem, rim_rsem, m_sem, round_sem):
    me, col = lax.axis_index("sec"), lax.axis_index("tile")
    has_prev, has_next = me > 0, me < lax.axis_size("sec") - 1
    has_up, has_down = col > 0, col < lax.axis_size("tile") - 1
    before, after = {"sec": me - 1}, {"sec": me + 1}
    pads = (pad_a, pad_b, pad_c)
    segments = range(len(SEGS))

    barrier = pltpu.get_barrier_semaphore()
    low_half, high_half = col % 4 < 2, col % 4 >= 2
    odd = col % 2
    partner, far = {"tile": col + 1 - 2 * odd}, {"tile": col - 1 + 2 * odd}
    has_far = (col > 0) & (col < lax.axis_size("tile") - 1)

    def tell(semaphore, there, target):
        @pl.when(there)
        def _():
            pl.semaphore_signal(semaphore, inc=1, device_id=target, device_id_type=MESH)

    for there, target in ((low_half & has_far, far), (has_prev, before), (has_next, after), (col >= 0, partner)):
        tell(barrier, there, target)

    scalars = [pltpu.make_async_copy(src, dst, loc_sem.at[place]) for place, (src, dst) in enumerate(
        ((offsets_hbm, offsets), (weights_hbm, weights), (stiffness_hbm, stiffness)))]
    for copy in scalars:
        copy.start()
    load_u = pltpu.make_async_copy(disp, pad_a.at[:, pl.ds(PAD, GRID), :], loc_sem.at[3])
    load_u.start()

    def fetch(section):
        return pltpu.make_async_copy(images.at[section], img.at[section], img_sem.at[section])

    for section in (3, 4, 5, 0, 1, 2):
        fetch(section).start()

    spacing = PIXELS // GRID

    def table(offset, carry):
        shift = (spacing - 1) / 2.0 + offset.astype(F32)
        cell = lax.broadcasted_iota(jnp.int32, (REACH, HALF), 0).astype(F32)
        pixel = lax.broadcasted_iota(jnp.int32, (REACH, HALF), 1).astype(F32)
        spread, peak, mass = [], [], []
        for low_cell, low_pixel in ((0, 0), (GRID - REACH, HALF)):
            gap = (pixel + low_pixel) - (spacing * (cell + low_cell) + shift)
            spread.append(gap)
            peak.append(jnp.exp(-gap * gap / (2.0 * kernel_sigma * kernel_sigma)))
            mass.append(jnp.sum(peak[-1], axis=1, keepdims=True))
        own = REACH - MEET
        shared = mass[0][own:] + mass[1][:MEET]
        mass = (jnp.concatenate([mass[0][:own], shared], axis=0), jnp.concatenate([shared, mass[1][MEET:]], axis=0))
        for half, ref in enumerate((first_t, last_t)):
            smooth = peak[half] / mass[half]
            ref[offset, 0:REACH, :] = smooth.astype(BF16)
            ref[offset, REACH:2 * REACH, :] = (smooth * spread[half] / (kernel_sigma * kernel_sigma)).astype(BF16)
        return carry

    lax.fori_loop(0, SKIPS + 1, table, 0)
    for copy in scalars:
        copy.wait()

    lane = lax.broadcasted_iota(jnp.int32, (8, 128), 1)
    facts = jnp.zeros((8, 128), jnp.int32)
    for section in range(SKIPS):
        for stride in range(SKIPS):
            base = (section * SKIPS + stride) * 3
            facts = jnp.where(lane == base, offsets[stride, 0, section + SKIPS], facts)
            facts = jnp.where(lane == base + 1, offsets[stride, 1, section + SKIPS], facts)
            facts = jnp.where(lane == base + 2, weights[stride, section + SKIPS], facts)
    meta_v[...] = facts
    for section in range(RES):
        for stride in range(SKIPS):
            for axis in range(2):
                shift_s[axis, (section + SKIPS) * SKIPS + stride] = offsets[stride, axis, section]
    rimsend[...] = jnp.zeros_like(rimsend)

    @pl.when(jnp.logical_not(has_prev))
    def _():
        meta_r[...] = jnp.zeros_like(meta_r)
        uprev[...] = jnp.zeros_like(uprev)
        precv[...] = jnp.zeros_like(precv)

    @pl.when(jnp.logical_not(has_next))
    def _():
        frecv[...] = jnp.zeros_like(frecv)

    @pl.when(jnp.logical_not(has_up))
    def _():
        rimrecv[:, 1] = jnp.zeros((ITERS, 16, GRID), F32)

    @pl.when(jnp.logical_not(has_down))
    def _():
        rimrecv[:, 0] = jnp.zeros((ITERS, 16, GRID), F32)

    load_u.wait()

    def halve(block, carry):
        at = pl.ds(pl.multiple_of(block * BLOCK, BLOCK), BLOCK)
        from_pad = pl.ds(pl.multiple_of(block * BLOCK + PAD, PAD), BLOCK)
        for field in range(EDGE):
            usend[0, field, at, :] = pad_a[EDGE + field, from_pad, :].astype(BF16)
        return carry

    lax.fori_loop(0, GRID // BLOCK, halve, 0)

    def keep_rims(step, source):
        for field in range(FIELDS):
            rimsend[step, 0, field:field + 1, :] = source[field, PAD:PAD + 1, :]
            rimsend[step, 1, field:field + 1, :] = source[field, PAD + GRID - 1:PAD + GRID, :]

    keep_rims(0, pad_a)

    pl.semaphore_wait(barrier, sum(there.astype(jnp.int32) for there in (has_prev, has_next, col >= 0, high_half & has_far)))
    tell(round_sem, high_half & has_far, far)

    def remote(src, dst, send_sem, recv_sem, target):
        return pltpu.make_async_remote_copy(
            src_ref=src, dst_ref=dst, send_sem=send_sem, recv_sem=recv_sem, device_id=target, device_id_type=MESH)

    def facts_copy():
        return remote(meta_v, meta_r, m_sem.at[0], m_sem.at[1], after)

    def rows_of(seg):
        start, size = SEGS[seg]
        return pl.ds(start, size)

    def u_forth(step, seg):
        at = rows_of(seg)
        return remote(usend.at[step, :, at, :], uprev.at[step, :, at, :], u_ssem.at[step, seg], u_rsem.at[step, seg], after)

    def f_back(step, seg):
        at = rows_of(seg)
        return remote(fsend.at[step, :, at, :], frecv.at[step, :, at, :], f_ssem.at[step, seg], f_rsem.at[step, seg], before)

    def q_forth(seg):
        at = rows_of(seg)
        return remote(pool.at[pl.ds(SKIPS, SKIPS), at, :], precv.at[:, at, :], q_ssem.at[seg], q_rsem.at[seg], after)

    def rim_copy(step, side):
        target = {"tile": col - 1 if side == 0 else col + 1}
        return remote(rimsend.at[step, side], rimrecv.at[step, side], rim_ssem.at[step, side], rim_rsem.at[step, side], target)

    def send_rims(step):
        @pl.when(has_up)
        def _():
            rim_copy(step, 0).start()

        @pl.when(has_down)
        def _():
            rim_copy(step, 1).start()

    @pl.when(has_next)
    def _():
        facts_copy().start()
        for seg in segments[:3]:
            u_forth(0, seg).start()

    @pl.when(high_half)
    def _():
        send_rims(0)

    zero_row = jnp.zeros((PAD, GRID), F32)
    for pad in pads:
        for field in range(FIELDS):
            pad[field, 0:PAD, :] = zero_row
            pad[field, PAD + GRID:, :] = zero_row

    def columns(section, first, last, count):
        halves = []
        for low in (0, HALF):
            top = dot_rows(first, img[section, low:low + HALF, 0:HALF])
            bottom = dot_rows(last, img[section, low:low + HALF, HALF:])
            halves.append([meet(top[REACH * one:REACH * (one + 1)], bottom[REACH * one:REACH * (one + 1)]).astype(BF16) for one in range(count)])
        return halves

    def section_pool(section):
        shifts = []
        for stride in range(1, SKIPS + 1):
            place = (section - stride + SKIPS) * SKIPS + stride - 1
            shifts.append((shift_s[0, place], shift_s[1, place]))
        first = jnp.concatenate([first_t[off_c] for _, off_c in shifts] + [first_t[0, 0:REACH, :]], axis=0)
        last = jnp.concatenate([last_t[off_c] for _, off_c in shifts] + [last_t[0, 0:REACH, :]], axis=0)
        low, high = columns(section, first, last, 2 * SKIPS + 1)
        for index, (off_r, _) in enumerate(shifts):
            slot = section * SKIPS + index
            top = dot_rows(first_t[off_r], jnp.concatenate(low[2 * index:2 * index + 2], axis=0))
            bottom = dot_rows(last_t[off_r], jnp.concatenate(high[2 * index:2 * index + 2], axis=0))
            smooth = meet(top[:REACH], bottom[:REACH]).astype(BF16)
            cache[slot, 0] = smooth[:, :GRID]
            cache[slot, 1] = meet(top[REACH:, :GRID], bottom[REACH:, :GRID]).astype(BF16)
            cache[slot, 2] = smooth[:, GRID:]
        pool[section] = meet(dot_rows(first_t[0, 0:REACH, :], low[-1]), dot_rows(last_t[0, 0:REACH, :], high[-1])).astype(BF16)

    def late_step(section, carry):
        fetch(section).wait()
        section_pool(section)
        return carry

    lax.fori_loop(SKIPS, RES, late_step, 0)

    @pl.when(has_next)
    def _():
        for seg in segments:
            if seg >= 3:
                u_forth(0, seg).start()
            q_forth(seg).start()

    for section in range(SKIPS):
        fetch(section).wait()

    @pl.when(has_prev)
    def _():
        facts_copy().wait_recv()

    to_scalars = pltpu.make_async_copy(meta_r, meta_s, loc_sem.at[4])
    to_scalars.start()
    to_scalars.wait()
    for place in range(SKIPS * SKIPS):
        for axis in range(2):
            shift_s[axis, place] = meta_s[0, 3 * place + axis]

    def early_step(section, carry):
        section_pool(section)
        return carry

    lax.fori_loop(0, SKIPS, early_step, 0)

    gain = [[force_step * weights[k - 1, s].astype(F32) for k in range(1, SKIPS + 1)] for s in range(RES)]
    stiff = [elastic_step * stiffness[s] for s in range(RES)]
    cross_gain = []
    for later, stride in CROSS:
        base = ((later - stride + SKIPS) * SKIPS + stride - 1) * 3
        cross_gain.append(force_step * meta_s[0, base + 2].astype(F32))

    def pull(slot, at, earlier_pool, row_gap, col_gap, scale):
        steep = (cache[slot, 1, at, :].astype(F32), cache[slot, 2, at, :].astype(F32))
        miss = cache[slot, 0, at, :].astype(F32) - earlier_pool + steep[0] * row_gap + steep[1] * col_gap
        weighted = scale * (miss / (1.0 + miss * miss))
        return weighted * steep[0], weighted * steep[1]

    def over(seg, body):
        start, size = SEGS[seg]

        def block_step(index, carry):
            low = start + index * BLOCK
            body(low, pl.ds(pl.multiple_of(low, BLOCK), BLOCK), pl.ds(pl.multiple_of(low + PAD, PAD), BLOCK))
            return carry

        lax.fori_loop(0, size // BLOCK, block_step, 0)

    def cross_pass(step, seg):
        pad = pads[step]

        def body(low, at, mid):
            own, back = [None] * EDGE, [None] * EDGE
            for index, (later, stride) in enumerate(CROSS):
                earlier = later - stride + SKIPS
                gaps = [pad[2 * later + c, mid, :] - uprev[step, 2 * earlier + c, at, :].astype(F32) for c in range(2)]
                pulled = pull(slot_of(later, stride), at, precv[earlier, at, :].astype(F32), gaps[0], gaps[1], cross_gain[index])
                for c in range(2):
                    here, there = 2 * later + c, 2 * earlier + c
                    own[here] = pulled[c] if own[here] is None else own[here] + pulled[c]
                    back[there] = pulled[c] if back[there] is None else back[there] + pulled[c]
            for field in range(EDGE):
                cross_own[field, at, :] = own[field]
                fsend[step, field, at, :] = back[field].astype(BF16)

        over(seg, body)

    def cross_turn(step, seg):
        @pl.when(has_prev)
        def _():
            u_forth(step, seg).wait_recv()
            if step == 0:
                q_forth(seg).wait_recv()

        cross_pass(step, seg)

        @pl.when(has_prev)
        def _():
            f_back(step, seg).start()

    def goal(step):
        return (pads[step + 1], PAD) if step + 1 < ITERS else (fin, 0)

    def local_pass(step, seg):
        pad, (target, base) = pads[step], goal(step)

        def body(low, at, mid):
            put = pl.ds(pl.multiple_of(low + base, PAD), BLOCK)
            above, below = pl.ds(low + PAD - 1, BLOCK), pl.ds(low + PAD + 1, BLOCK)
            edge = lax.broadcasted_iota(jnp.int32, (BLOCK, GRID), 1)
            total = []
            for field in range(FIELDS):
                here = pad[field, mid, :]
                left = jnp.where(edge == 0, 0.0, pltpu.roll(here, 1, 1))
                right = jnp.where(edge == GRID - 1, 0.0, pltpu.roll(here, GRID - 1, 1))
                beside = pad[field, above, :] + pad[field, below, :] + left + right
                total.append(here - stiff[field // 2] * (4.0 * here - beside))
                if field < EDGE:
                    total[field] -= cross_own[field, at, :]
            for later, stride in LOCAL:
                earlier = later - stride
                gaps = [pad[2 * later + c, mid, :] - pad[2 * earlier + c, mid, :] for c in range(2)]
                pulled = pull(slot_of(later, stride), at, pool[earlier, at, :].astype(F32), gaps[0], gaps[1], gain[earlier][stride - 1])
                for c in range(2):
                    total[2 * earlier + c] += pulled[c]
                    total[2 * later + c] -= pulled[c]
            for field in range(FIELDS):
                target[field, put, :] = total[field]

        over(seg, body)

    def finish(step, seg):
        target, base = goal(step)
        if seg < 2:
            side, row = ((1, 0), (0, GRID - 1))[seg]

            @pl.when((has_up, has_down)[seg])
            def _():
                rim_copy(step, side).wait_recv()

            for field in range(FIELDS):
                spot = slice(base + row, base + row + 1)
                target[field, spot, :] = target[field, spot, :] + stiff[field // 2] * rimrecv[step, side, field:field + 1, :]

        @pl.when(has_next)
        def _():
            f_back(step, seg).wait_recv()

        def body(low, at, mid):
            put = pl.ds(pl.multiple_of(low + base, PAD), BLOCK)
            for field in range(EDGE):
                done = target[EDGE + field, put, :] + frecv[step, field, at, :].astype(F32)
                target[EDGE + field, put, :] = done
                if step + 1 < ITERS:
                    usend[step + 1, field, at, :] = done.astype(BF16)

        over(seg, body)
        if step + 1 < ITERS:
            @pl.when(has_next)
            def _():
                u_forth(step + 1, seg).start()

            if seg == 1:
                keep_rims(step + 1, pads[step + 1])
                send_rims(step + 1)
        else:
            store(seg).start()

    def store(seg):
        at = rows_of(seg)
        return pltpu.make_async_copy(fin.at[:, at, :], out.at[:, at, :], loc_sem.at[5 + seg])

    edges, inner = segments[:2], segments[2:]

    def turns(step, *group):
        for seg in group:
            cross_turn(step, seg)

    def passes(step, *group):
        for seg in group:
            local_pass(step, seg)

    def finishes(step, *group):
        for seg in group:
            finish(step, seg)

    turns(0, 0, 1, 2)
    passes(0, 0, 1)
    turns(0, 3)
    passes(0, 2)
    turns(0, 4)
    passes(0, 3, 4)

    @pl.when(low_half)
    def _():
        @pl.when(has_far)
        def _():
            pl.semaphore_wait(round_sem, 1)

        send_rims(0)

    early = low_half & (me < lax.axis_size("sec") // 2)

    @pl.when(jnp.logical_not(early))
    def _():
        finishes(0, *edges)
        finishes(0, 2)
        turns(1, *edges)
        finishes(0, 3, 4)
        passes(1, 0, 1)
        turns(1, 2)
        passes(1, 2)
        turns(1, 3)
        passes(1, 3)
        finishes(1, 0, 1)
        turns(1, 4)
        passes(1, 4)
        finishes(1, 2)
        turns(2, 0, 1)
        finishes(1, 3, 4)
        passes(2, 0, 1)
        turns(2, 2)
        passes(2, 2)
        turns(2, 3)
        passes(2, 3)
        turns(2, 4)
        passes(2, 4)
        finishes(2, 2, 3, 4, 0, 1)

    @pl.when(early)
    def _():
        finishes(0, *inner)
        for step in range(1, ITERS):
            turns(step, *inner)
            finishes(step - 1, *edges)
            passes(step, *inner)
            turns(step, *edges)
            passes(step, *edges)
            finishes(step, *inner)
        finishes(ITERS - 1, *edges)

    for seg in segments:
        store(seg).wait()

    @pl.when(has_prev)
    def _():
        for seg in segments:
            for step in range(ITERS):
                f_back(step, seg).wait_send()

    @pl.when(has_next)
    def _():
        facts_copy().wait_send()
        for seg in segments:
            q_forth(seg).wait_send()
        for seg in segments:
            for step in range(ITERS):
                u_forth(step, seg).wait_send()

    for step in range(ITERS):
        @pl.when(has_up)
        def _():
            rim_copy(step, 0).wait_send()

        @pl.when(has_down)
        def _():
            rim_copy(step, 1).wait_send()


def local(images, displacement, offsets, weights, stiffness):
    anywhere = pl.BlockSpec(memory_space=pl.ANY)
    dma, vmem, smem = pltpu.SemaphoreType.DMA, pltpu.VMEM, pltpu.SMEM
    segs = len(SEGS)
    given = (displacement.reshape(FIELDS, GRID, GRID), images, offsets.transpose(1, 2, 0), weights.T, stiffness)
    moved = pl.pallas_call(
        kernel,
        out_shape=jax.ShapeDtypeStruct((FIELDS, GRID, GRID), F32),
        in_specs=[anywhere] * 5,
        out_specs=anywhere,
        scratch_shapes=[
            vmem((RES, PIXELS, PIXELS), BF16),
            vmem((SKIPS + 1, 2 * REACH, HALF), BF16),
            vmem((SKIPS + 1, 2 * REACH, HALF), BF16),
            vmem((len(PAIRS), 3, GRID, GRID), BF16),
            vmem((RES, GRID, GRID), BF16),
            vmem((SKIPS, GRID, GRID), BF16),
            vmem((FIELDS, GRID + 2 * PAD, GRID), F32),
            vmem((FIELDS, GRID + 2 * PAD, GRID), F32),
            vmem((FIELDS, GRID + 2 * PAD, GRID), F32),
            vmem((FIELDS, GRID, GRID), F32),
            vmem((EDGE, GRID, GRID), F32),
            vmem((ITERS, EDGE, GRID, GRID), BF16),
            vmem((ITERS, EDGE, GRID, GRID), BF16),
            vmem((ITERS, EDGE, GRID, GRID), BF16),
            vmem((ITERS, EDGE, GRID, GRID), BF16),
            vmem((ITERS, 2, 16, GRID), F32),
            vmem((ITERS, 2, 16, GRID), F32),
            vmem((8, 128), jnp.int32),
            vmem((8, 128), jnp.int32),
            smem((8, 128), jnp.int32),
            smem((2, (RES + SKIPS) * SKIPS), jnp.int32),
            smem((SKIPS, 2, RES), jnp.int32),
            smem((SKIPS, RES), jnp.int32),
            smem((RES,), F32),
            dma((RES,)),
            dma((5 + segs,)),
            dma((ITERS, segs)),
            dma((ITERS, segs)),
            dma((ITERS, segs)),
            dma((ITERS, segs)),
            dma((segs,)),
            dma((segs,)),
            dma((ITERS, 2)),
            dma((ITERS, 2)),
            dma((2,)),
            pltpu.SemaphoreType.REGULAR,
        ],
        compiler_params=pltpu.CompilerParams(collective_id=0, has_side_effects=True, vmem_limit_bytes=24 << 20),
    )(*(pltpu.with_memory_space_constraint(each, pltpu.HBM) for each in given))
    return moved.reshape(RES, 2, GRID, GRID)


def solution(mesh):
    placed = (
        P("sec", "tile", None),
        P("sec", None, "tile", None),
        P("sec", None, None),
        P("sec", None),
        P("sec"),
    )
    return jax.shard_map(
        local, mesh=mesh, in_specs=placed, out_specs=P("sec", None, "tile", None), check_vma=False
    )
```

```python
import jax
import jax.numpy as jnp
from jax import lax
from jax.experimental import pallas as pl
from jax.experimental.pallas import tpu as pltpu
from jax.sharding import PartitionSpec as P

PIXELS = 512
HALF = PIXELS // 2
GRID = 128
SKIPS = 3
ITERS = 3
RES = 6
FIELDS = 2 * RES
EDGE = 2 * SKIPS
PAD = 8
BLOCK = 16
REACH = 72
MEET = 2 * REACH - GRID
F32, BF16 = jnp.float32, jnp.bfloat16
MESH = pl.DeviceIdType.MESH

SEGS = ((0, 16), (112, 16), (16, 32), (48, 32), (80, 32))
PAIRS = tuple((later, stride) for later in range(RES) for stride in range(1, SKIPS + 1))
CROSS = tuple(pair for pair in PAIRS if pair[0] < pair[1])
LOCAL = tuple(pair for pair in PAIRS if pair[0] >= pair[1])

kernel_sigma = 2.0
force_step = 0.5
elastic_step = 0.1


def slot_of(later, stride):
    return later * SKIPS + stride - 1


def dot_rows(left, right):
    return lax.dot_general(left, right, (((1,), (1,)), ((), ())), preferred_element_type=F32)


def meet(top, bottom):
    own = REACH - MEET
    return jnp.concatenate([top[:own], top[own:] + bottom[:MEET], bottom[MEET:]], axis=0)


def kernel(disp, images, offsets_hbm, weights_hbm, stiffness_hbm, out, img, first_t, last_t, cache, pool, precv,
           pad_a, pad_b, pad_c, fin, cross_own, usend, uprev, fsend, frecv, rimsend, rimrecv, meta_v, meta_r, meta_s, shift_s,
           offsets, weights, stiffness, img_sem, loc_sem, u_ssem, u_rsem, f_ssem, f_rsem, q_ssem, q_rsem, rim_ssem, rim_rsem, m_sem, round_sem):
    me, col = lax.axis_index("sec"), lax.axis_index("tile")
    has_prev, has_next = me > 0, me < lax.axis_size("sec") - 1
    has_up, has_down = col > 0, col < lax.axis_size("tile") - 1
    before, after = {"sec": me - 1}, {"sec": me + 1}
    pads = (pad_a, pad_b, pad_c)
    segments = range(len(SEGS))

    barrier = pltpu.get_barrier_semaphore()
    low_half, high_half = col % 4 < 2, col % 4 >= 2
    odd = col % 2
    partner, far = {"tile": col + 1 - 2 * odd}, {"tile": col - 1 + 2 * odd}
    has_far = (col > 0) & (col < lax.axis_size("tile") - 1)

    def tell(semaphore, there, target):
        @pl.when(there)
        def _():
            pl.semaphore_signal(semaphore, inc=1, device_id=target, device_id_type=MESH)

    for there, target in ((low_half & has_far, far), (has_prev, before), (has_next, after), (col >= 0, partner)):
        tell(barrier, there, target)

    scalars = [pltpu.make_async_copy(src, dst, loc_sem.at[place]) for place, (src, dst) in enumerate(
        ((offsets_hbm, offsets), (weights_hbm, weights), (stiffness_hbm, stiffness)))]
    for copy in scalars:
        copy.start()
    load_u = pltpu.make_async_copy(disp, pad_a.at[:, pl.ds(PAD, GRID), :], loc_sem.at[3])
    load_u.start()

    def fetch(section):
        return pltpu.make_async_copy(images.at[section], img.at[section], img_sem.at[section])

    for section in (3, 4, 5, 0, 1, 2):
        fetch(section).start()

    spacing = PIXELS // GRID

    def table(offset, carry):
        shift = (spacing - 1) / 2.0 + offset.astype(F32)
        cell = lax.broadcasted_iota(jnp.int32, (REACH, HALF), 0).astype(F32)
        pixel = lax.broadcasted_iota(jnp.int32, (REACH, HALF), 1).astype(F32)
        spread, peak, mass = [], [], []
        for low_cell, low_pixel in ((0, 0), (GRID - REACH, HALF)):
            gap = (pixel + low_pixel) - (spacing * (cell + low_cell) + shift)
            spread.append(gap)
            peak.append(jnp.exp(-gap * gap / (2.0 * kernel_sigma * kernel_sigma)))
            mass.append(jnp.sum(peak[-1], axis=1, keepdims=True))
        own = REACH - MEET
        shared = mass[0][own:] + mass[1][:MEET]
        mass = (jnp.concatenate([mass[0][:own], shared], axis=0), jnp.concatenate([shared, mass[1][MEET:]], axis=0))
        for half, ref in enumerate((first_t, last_t)):
            smooth = peak[half] / mass[half]
            ref[offset, 0:REACH, :] = smooth.astype(BF16)
            ref[offset, REACH:2 * REACH, :] = (smooth * spread[half] / (kernel_sigma * kernel_sigma)).astype(BF16)
        return carry

    lax.fori_loop(0, SKIPS + 1, table, 0)
    for copy in scalars:
        copy.wait()

    lane = lax.broadcasted_iota(jnp.int32, (8, 128), 1)
    facts = jnp.zeros((8, 128), jnp.int32)
    for section in range(SKIPS):
        for stride in range(SKIPS):
            base = (section * SKIPS + stride) * 3
            facts = jnp.where(lane == base, offsets[stride, 0, section + SKIPS], facts)
            facts = jnp.where(lane == base + 1, offsets[stride, 1, section + SKIPS], facts)
            facts = jnp.where(lane == base + 2, weights[stride, section + SKIPS], facts)
    meta_v[...] = facts
    for section in range(RES):
        for stride in range(SKIPS):
            for axis in range(2):
                shift_s[axis, (section + SKIPS) * SKIPS + stride] = offsets[stride, axis, section]
    rimsend[...] = jnp.zeros_like(rimsend)

    @pl.when(jnp.logical_not(has_prev))
    def _():
        meta_r[...] = jnp.zeros_like(meta_r)
        uprev[...] = jnp.zeros_like(uprev)
        precv[...] = jnp.zeros_like(precv)

    @pl.when(jnp.logical_not(has_next))
    def _():
        frecv[...] = jnp.zeros_like(frecv)

    @pl.when(jnp.logical_not(has_up))
    def _():
        rimrecv[:, 1] = jnp.zeros((ITERS, 16, GRID), F32)

    @pl.when(jnp.logical_not(has_down))
    def _():
        rimrecv[:, 0] = jnp.zeros((ITERS, 16, GRID), F32)

    load_u.wait()

    def halve(block, carry):
        at = pl.ds(pl.multiple_of(block * BLOCK, BLOCK), BLOCK)
        from_pad = pl.ds(pl.multiple_of(block * BLOCK + PAD, PAD), BLOCK)
        for field in range(EDGE):
            usend[0, field, at, :] = pad_a[EDGE + field, from_pad, :].astype(BF16)
        return carry

    lax.fori_loop(0, GRID // BLOCK, halve, 0)

    def keep_rims(step, source):
        for field in range(FIELDS):
            rimsend[step, 0, field:field + 1, :] = source[field, PAD:PAD + 1, :]
            rimsend[step, 1, field:field + 1, :] = source[field, PAD + GRID - 1:PAD + GRID, :]

    keep_rims(0, pad_a)

    pl.semaphore_wait(barrier, sum(there.astype(jnp.int32) for there in (has_prev, has_next, col >= 0, high_half & has_far)))
    tell(round_sem, high_half & has_far, far)

    def remote(src, dst, send_sem, recv_sem, target):
        return pltpu.make_async_remote_copy(
            src_ref=src, dst_ref=dst, send_sem=send_sem, recv_sem=recv_sem, device_id=target, device_id_type=MESH)

    def facts_copy():
        return remote(meta_v, meta_r, m_sem.at[0], m_sem.at[1], after)

    def rows_of(seg):
        start, size = SEGS[seg]
        return pl.ds(start, size)

    def u_forth(step, seg):
        at = rows_of(seg)
        return remote(usend.at[step, :, at, :], uprev.at[step, :, at, :], u_ssem.at[step, seg], u_rsem.at[step, seg], after)

    def f_back(step, seg):
        at = rows_of(seg)
        return remote(fsend.at[step, :, at, :], frecv.at[step, :, at, :], f_ssem.at[step, seg], f_rsem.at[step, seg], before)

    def q_forth(seg):
        at = rows_of(seg)
        return remote(pool.at[pl.ds(SKIPS, SKIPS), at, :], precv.at[:, at, :], q_ssem.at[seg], q_rsem.at[seg], after)

    def rim_copy(step, side):
        target = {"tile": col - 1 if side == 0 else col + 1}
        return remote(rimsend.at[step, side], rimrecv.at[step, side], rim_ssem.at[step, side], rim_rsem.at[step, side], target)

    def send_rims(step):
        @pl.when(has_up)
        def _():
            rim_copy(step, 0).start()

        @pl.when(has_down)
        def _():
            rim_copy(step, 1).start()

    @pl.when(has_next)
    def _():
        facts_copy().start()
        for seg in segments[:3]:
            u_forth(0, seg).start()

    @pl.when(high_half)
    def _():
        send_rims(0)

    zero_row = jnp.zeros((PAD, GRID), F32)
    for pad in pads:
        for field in range(FIELDS):
            pad[field, 0:PAD, :] = zero_row
            pad[field, PAD + GRID:, :] = zero_row

    def columns(section, first, last, count):
        halves = []
        for low in (0, HALF):
            top = dot_rows(first, img[section, low:low + HALF, 0:HALF])
            bottom = dot_rows(last, img[section, low:low + HALF, HALF:])
            halves.append([meet(top[REACH * one:REACH * (one + 1)], bottom[REACH * one:REACH * (one + 1)]).astype(BF16) for one in range(count)])
        return halves

    def section_pool(section):
        shifts = []
        for stride in range(1, SKIPS + 1):
            place = (section - stride + SKIPS) * SKIPS + stride - 1
            shifts.append((shift_s[0, place], shift_s[1, place]))
        first = jnp.concatenate([first_t[off_c] for _, off_c in shifts] + [first_t[0, 0:REACH, :]], axis=0)
        last = jnp.concatenate([last_t[off_c] for _, off_c in shifts] + [last_t[0, 0:REACH, :]], axis=0)
        low, high = columns(section, first, last, 2 * SKIPS + 1)
        for index, (off_r, _) in enumerate(shifts):
            slot = section * SKIPS + index
            top = dot_rows(first_t[off_r], jnp.concatenate(low[2 * index:2 * index + 2], axis=0))
            bottom = dot_rows(last_t[off_r], jnp.concatenate(high[2 * index:2 * index + 2], axis=0))
            smooth = meet(top[:REACH], bottom[:REACH]).astype(BF16)
            cache[slot, 0] = smooth[:, :GRID]
            cache[slot, 1] = meet(top[REACH:, :GRID], bottom[REACH:, :GRID]).astype(BF16)
            cache[slot, 2] = smooth[:, GRID:]
        pool[section] = meet(dot_rows(first_t[0, 0:REACH, :], low[-1]), dot_rows(last_t[0, 0:REACH, :], high[-1])).astype(BF16)

    def late_step(section, carry):
        fetch(section).wait()
        section_pool(section)
        return carry

    lax.fori_loop(SKIPS, RES, late_step, 0)

    @pl.when(has_next)
    def _():
        for seg in segments:
            if seg >= 3:
                u_forth(0, seg).start()
            q_forth(seg).start()

    for section in range(SKIPS):
        fetch(section).wait()

    @pl.when(has_prev)
    def _():
        facts_copy().wait_recv()

    to_scalars = pltpu.make_async_copy(meta_r, meta_s, loc_sem.at[4])
    to_scalars.start()
    to_scalars.wait()
    for place in range(SKIPS * SKIPS):
        for axis in range(2):
            shift_s[axis, place] = meta_s[0, 3 * place + axis]

    def early_step(section, carry):
        section_pool(section)
        return carry

    lax.fori_loop(0, SKIPS, early_step, 0)

    gain = [[force_step * weights[k - 1, s].astype(F32) for k in range(1, SKIPS + 1)] for s in range(RES)]
    stiff = [elastic_step * stiffness[s] for s in range(RES)]
    cross_gain = []
    for later, stride in CROSS:
        base = ((later - stride + SKIPS) * SKIPS + stride - 1) * 3
        cross_gain.append(force_step * meta_s[0, base + 2].astype(F32))

    def pull(slot, at, earlier_pool, row_gap, col_gap, scale):
        steep = (cache[slot, 1, at, :].astype(F32), cache[slot, 2, at, :].astype(F32))
        miss = cache[slot, 0, at, :].astype(F32) - earlier_pool + steep[0] * row_gap + steep[1] * col_gap
        weighted = scale * (miss / (1.0 + miss * miss))
        return weighted * steep[0], weighted * steep[1]

    def over(seg, body):
        start, size = SEGS[seg]

        def block_step(index, carry):
            low = start + index * BLOCK
            body(low, pl.ds(pl.multiple_of(low, BLOCK), BLOCK), pl.ds(pl.multiple_of(low + PAD, PAD), BLOCK))
            return carry

        lax.fori_loop(0, size // BLOCK, block_step, 0)

    def cross_pass(step, seg):
        pad = pads[step]

        def body(low, at, mid):
            own, back = [None] * EDGE, [None] * EDGE
            for index, (later, stride) in enumerate(CROSS):
                earlier = later - stride + SKIPS
                gaps = [pad[2 * later + c, mid, :] - uprev[step, 2 * earlier + c, at, :].astype(F32) for c in range(2)]
                pulled = pull(slot_of(later, stride), at, precv[earlier, at, :].astype(F32), gaps[0], gaps[1], cross_gain[index])
                for c in range(2):
                    here, there = 2 * later + c, 2 * earlier + c
                    own[here] = pulled[c] if own[here] is None else own[here] + pulled[c]
                    back[there] = pulled[c] if back[there] is None else back[there] + pulled[c]
            for field in range(EDGE):
                cross_own[field, at, :] = own[field]
                fsend[step, field, at, :] = back[field].astype(BF16)

        over(seg, body)

    def cross_turn(step, seg):
        @pl.when(has_prev)
        def _():
            u_forth(step, seg).wait_recv()
            if step == 0:
                q_forth(seg).wait_recv()

        cross_pass(step, seg)

        @pl.when(has_prev)
        def _():
            f_back(step, seg).start()

    def goal(step):
        return (pads[step + 1], PAD) if step + 1 < ITERS else (fin, 0)

    def local_pass(step, seg):
        pad, (target, base) = pads[step], goal(step)

        def body(low, at, mid):
            put = pl.ds(pl.multiple_of(low + base, PAD), BLOCK)
            above, below = pl.ds(low + PAD - 1, BLOCK), pl.ds(low + PAD + 1, BLOCK)
            edge = lax.broadcasted_iota(jnp.int32, (BLOCK, GRID), 1)
            total = []
            for field in range(FIELDS):
                here = pad[field, mid, :]
                left = jnp.where(edge == 0, 0.0, pltpu.roll(here, 1, 1))
                right = jnp.where(edge == GRID - 1, 0.0, pltpu.roll(here, GRID - 1, 1))
                beside = pad[field, above, :] + pad[field, below, :] + left + right
                total.append(here - stiff[field // 2] * (4.0 * here - beside))
                if field < EDGE:
                    total[field] -= cross_own[field, at, :]
            for later, stride in LOCAL:
                earlier = later - stride
                gaps = [pad[2 * later + c, mid, :] - pad[2 * earlier + c, mid, :] for c in range(2)]
                pulled = pull(slot_of(later, stride), at, pool[earlier, at, :].astype(F32), gaps[0], gaps[1], gain[earlier][stride - 1])
                for c in range(2):
                    total[2 * earlier + c] += pulled[c]
                    total[2 * later + c] -= pulled[c]
            for field in range(FIELDS):
                target[field, put, :] = total[field]

        over(seg, body)

    def finish(step, seg):
        target, base = goal(step)
        if seg < 2:
            side, row = ((1, 0), (0, GRID - 1))[seg]

            @pl.when((has_up, has_down)[seg])
            def _():
                rim_copy(step, side).wait_recv()

            for field in range(FIELDS):
                spot = slice(base + row, base + row + 1)
                target[field, spot, :] = target[field, spot, :] + stiff[field // 2] * rimrecv[step, side, field:field + 1, :]

        @pl.when(has_next)
        def _():
            f_back(step, seg).wait_recv()

        def body(low, at, mid):
            put = pl.ds(pl.multiple_of(low + base, PAD), BLOCK)
            for field in range(EDGE):
                done = target[EDGE + field, put, :] + frecv[step, field, at, :].astype(F32)
                target[EDGE + field, put, :] = done
                if step + 1 < ITERS:
                    usend[step + 1, field, at, :] = done.astype(BF16)

        over(seg, body)
        if step + 1 < ITERS:
            @pl.when(has_next)
            def _():
                u_forth(step + 1, seg).start()

            if seg == 1:
                keep_rims(step + 1, pads[step + 1])
                send_rims(step + 1)
        else:
            store(seg).start()

    def store(seg):
        at = rows_of(seg)
        return pltpu.make_async_copy(fin.at[:, at, :], out.at[:, at, :], loc_sem.at[5 + seg])

    edges, inner = segments[:2], segments[2:]

    def turns(step, *group):
        for seg in group:
            cross_turn(step, seg)

    def passes(step, *group):
        for seg in group:
            local_pass(step, seg)

    def finishes(step, *group):
        for seg in group:
            finish(step, seg)

    turns(0, 0, 1, 2)
    passes(0, 0, 1)
    turns(0, 3)
    passes(0, 2)
    turns(0, 4)
    passes(0, 3, 4)

    @pl.when(low_half)
    def _():
        @pl.when(has_far)
        def _():
            pl.semaphore_wait(round_sem, 1)

        send_rims(0)

    @pl.when(high_half)
    def _():
        finishes(0, *edges)
        finishes(0, 2)
        turns(1, *edges)
        finishes(0, 3, 4)
        passes(1, 0, 1)
        turns(1, 2)
        passes(1, 2)
        turns(1, 3)
        passes(1, 3)
        finishes(1, 0, 1)
        turns(1, 4)
        passes(1, 4)
        finishes(1, 2)
        turns(2, 0, 1)
        finishes(1, 3, 4)
        passes(2, 0, 1)
        turns(2, 2)
        passes(2, 2)
        turns(2, 3)
        passes(2, 3)
        turns(2, 4)
        passes(2, 4)
        finishes(2, 2, 3, 4, 0, 1)

    @pl.when(low_half)
    def _():
        finishes(0, *segments)
        turns(1, *edges)
        passes(1, *edges)
        for seg in inner:
            turns(1, seg)
            passes(1, seg)
        finishes(1, *inner)
        turns(2, *inner)
        finishes(1, *edges)
        passes(2, *inner)
        turns(2, *edges)
        passes(2, *edges)
        finishes(2, *inner)
        finishes(2, *edges)

    for seg in segments:
        store(seg).wait()

    @pl.when(has_prev)
    def _():
        for seg in segments:
            for step in range(ITERS):
                f_back(step, seg).wait_send()

    @pl.when(has_next)
    def _():
        facts_copy().wait_send()
        for seg in segments:
            q_forth(seg).wait_send()
        for seg in segments:
            for step in range(ITERS):
                u_forth(step, seg).wait_send()

    for step in range(ITERS):
        @pl.when(has_up)
        def _():
            rim_copy(step, 0).wait_send()

        @pl.when(has_down)
        def _():
            rim_copy(step, 1).wait_send()


def local(images, displacement, offsets, weights, stiffness):
    anywhere = pl.BlockSpec(memory_space=pl.ANY)
    dma, vmem, smem = pltpu.SemaphoreType.DMA, pltpu.VMEM, pltpu.SMEM
    segs = len(SEGS)
    given = (displacement.reshape(FIELDS, GRID, GRID), images, offsets.transpose(1, 2, 0), weights.T, stiffness)
    moved = pl.pallas_call(
        kernel,
        out_shape=jax.ShapeDtypeStruct((FIELDS, GRID, GRID), F32),
        in_specs=[anywhere] * 5,
        out_specs=anywhere,
        scratch_shapes=[
            vmem((RES, PIXELS, PIXELS), BF16),
            vmem((SKIPS + 1, 2 * REACH, HALF), BF16),
            vmem((SKIPS + 1, 2 * REACH, HALF), BF16),
            vmem((len(PAIRS), 3, GRID, GRID), BF16),
            vmem((RES, GRID, GRID), BF16),
            vmem((SKIPS, GRID, GRID), BF16),
            vmem((FIELDS, GRID + 2 * PAD, GRID), F32),
            vmem((FIELDS, GRID + 2 * PAD, GRID), F32),
            vmem((FIELDS, GRID + 2 * PAD, GRID), F32),
            vmem((FIELDS, GRID, GRID), F32),
            vmem((EDGE, GRID, GRID), F32),
            vmem((ITERS, EDGE, GRID, GRID), BF16),
            vmem((ITERS, EDGE, GRID, GRID), BF16),
            vmem((ITERS, EDGE, GRID, GRID), BF16),
            vmem((ITERS, EDGE, GRID, GRID), BF16),
            vmem((ITERS, 2, 16, GRID), F32),
            vmem((ITERS, 2, 16, GRID), F32),
            vmem((8, 128), jnp.int32),
            vmem((8, 128), jnp.int32),
            smem((8, 128), jnp.int32),
            smem((2, (RES + SKIPS) * SKIPS), jnp.int32),
            smem((SKIPS, 2, RES), jnp.int32),
            smem((SKIPS, RES), jnp.int32),
            smem((RES,), F32),
            dma((RES,)),
            dma((5 + segs,)),
            dma((ITERS, segs)),
            dma((ITERS, segs)),
            dma((ITERS, segs)),
            dma((ITERS, segs)),
            dma((segs,)),
            dma((segs,)),
            dma((ITERS, 2)),
            dma((ITERS, 2)),
            dma((2,)),
            pltpu.SemaphoreType.REGULAR,
        ],
        compiler_params=pltpu.CompilerParams(collective_id=0, has_side_effects=True, vmem_limit_bytes=24 << 20),
    )(*(pltpu.with_memory_space_constraint(each, pltpu.HBM) for each in given))
    return moved.reshape(RES, 2, GRID, GRID)


def solution(mesh):
    placed = (
        P("sec", "tile", None),
        P("sec", None, "tile", None),
        P("sec", None, None),
        P("sec", None),
        P("sec"),
    )
    return jax.shard_map(
        local, mesh=mesh, in_specs=placed, out_specs=P("sec", None, "tile", None), check_vma=False
    )
```

```python
import jax
import jax.numpy as jnp
from jax import lax
from jax.experimental import pallas as pl
from jax.experimental.pallas import tpu as pltpu
from jax.sharding import PartitionSpec as P

PIXELS = 512
HALF = PIXELS // 2
GRID = 128
SKIPS = 3
ITERS = 3
RES = 6
FIELDS = 2 * RES
EDGE = 2 * SKIPS
PAD = 8
BLOCK = 16
REACH = 72
MEET = 2 * REACH - GRID
F32, BF16 = jnp.float32, jnp.bfloat16
MESH = pl.DeviceIdType.MESH

SEGS = ((0, 16), (112, 16), (16, 32), (48, 32), (80, 32))
PAIRS = tuple((later, stride) for later in range(RES) for stride in range(1, SKIPS + 1))
CROSS = tuple(pair for pair in PAIRS if pair[0] < pair[1])
LOCAL = tuple(pair for pair in PAIRS if pair[0] >= pair[1])

kernel_sigma = 2.0
force_step = 0.5
elastic_step = 0.1


def slot_of(later, stride):
    return later * SKIPS + stride - 1


def dot_rows(left, right):
    return lax.dot_general(left, right, (((1,), (1,)), ((), ())), preferred_element_type=F32)


def meet(top, bottom):
    own = REACH - MEET
    return jnp.concatenate([top[:own], top[own:] + bottom[:MEET], bottom[MEET:]], axis=0)


def kernel(disp, images, offsets_hbm, weights_hbm, stiffness_hbm, out, img, first_t, last_t, cache, pool, precv,
           pad_a, pad_b, pad_c, fin, cross_own, usend, uprev, fsend, frecv, rimsend, rimrecv, meta_v, meta_r, meta_s, shift_s,
           offsets, weights, stiffness, img_sem, loc_sem, u_ssem, u_rsem, f_ssem, f_rsem, q_ssem, q_rsem, rim_ssem, rim_rsem, m_sem, round_sem):
    me, col = lax.axis_index("sec"), lax.axis_index("tile")
    has_prev, has_next = me > 0, me < lax.axis_size("sec") - 1
    has_up, has_down = col > 0, col < lax.axis_size("tile") - 1
    before, after = {"sec": me - 1}, {"sec": me + 1}
    pads = (pad_a, pad_b, pad_c)
    segments = range(len(SEGS))

    barrier = pltpu.get_barrier_semaphore()
    low_half, high_half = col % 4 < 2, col % 4 >= 2
    odd = col % 2
    partner, far = {"tile": col + 1 - 2 * odd}, {"tile": col - 1 + 2 * odd}
    has_far = (col > 0) & (col < lax.axis_size("tile") - 1)

    def tell(semaphore, there, target):
        @pl.when(there)
        def _():
            pl.semaphore_signal(semaphore, inc=1, device_id=target, device_id_type=MESH)

    for there, target in ((low_half & has_far, far), (has_prev, before), (has_next, after), (col >= 0, partner)):
        tell(barrier, there, target)

    scalars = [pltpu.make_async_copy(src, dst, loc_sem.at[place]) for place, (src, dst) in enumerate(
        ((offsets_hbm, offsets), (weights_hbm, weights), (stiffness_hbm, stiffness)))]
    for copy in scalars:
        copy.start()
    load_u = pltpu.make_async_copy(disp, pad_a.at[:, pl.ds(PAD, GRID), :], loc_sem.at[3])
    load_u.start()

    def fetch(section):
        return pltpu.make_async_copy(images.at[section], img.at[section], img_sem.at[section])

    for section in (3, 4, 5, 0, 1, 2):
        fetch(section).start()

    spacing = PIXELS // GRID

    def table(offset, carry):
        shift = (spacing - 1) / 2.0 + offset.astype(F32)
        cell = lax.broadcasted_iota(jnp.int32, (REACH, HALF), 0).astype(F32)
        pixel = lax.broadcasted_iota(jnp.int32, (REACH, HALF), 1).astype(F32)
        spread, peak, mass = [], [], []
        for low_cell, low_pixel in ((0, 0), (GRID - REACH, HALF)):
            gap = (pixel + low_pixel) - (spacing * (cell + low_cell) + shift)
            spread.append(gap)
            peak.append(jnp.exp(-gap * gap / (2.0 * kernel_sigma * kernel_sigma)))
            mass.append(jnp.sum(peak[-1], axis=1, keepdims=True))
        own = REACH - MEET
        shared = mass[0][own:] + mass[1][:MEET]
        mass = (jnp.concatenate([mass[0][:own], shared], axis=0), jnp.concatenate([shared, mass[1][MEET:]], axis=0))
        for half, ref in enumerate((first_t, last_t)):
            smooth = peak[half] / mass[half]
            ref[offset, 0:REACH, :] = smooth.astype(BF16)
            ref[offset, REACH:2 * REACH, :] = (smooth * spread[half] / (kernel_sigma * kernel_sigma)).astype(BF16)
        return carry

    lax.fori_loop(0, SKIPS + 1, table, 0)
    for copy in scalars:
        copy.wait()

    lane = lax.broadcasted_iota(jnp.int32, (8, 128), 1)
    facts = jnp.zeros((8, 128), jnp.int32)
    for section in range(SKIPS):
        for stride in range(SKIPS):
            base = (section * SKIPS + stride) * 3
            facts = jnp.where(lane == base, offsets[stride, 0, section + SKIPS], facts)
            facts = jnp.where(lane == base + 1, offsets[stride, 1, section + SKIPS], facts)
            facts = jnp.where(lane == base + 2, weights[stride, section + SKIPS], facts)
    meta_v[...] = facts
    for section in range(RES):
        for stride in range(SKIPS):
            for axis in range(2):
                shift_s[axis, (section + SKIPS) * SKIPS + stride] = offsets[stride, axis, section]
    rimsend[...] = jnp.zeros_like(rimsend)

    @pl.when(jnp.logical_not(has_prev))
    def _():
        meta_r[...] = jnp.zeros_like(meta_r)
        uprev[...] = jnp.zeros_like(uprev)
        precv[...] = jnp.zeros_like(precv)

    @pl.when(jnp.logical_not(has_next))
    def _():
        frecv[...] = jnp.zeros_like(frecv)

    @pl.when(jnp.logical_not(has_up))
    def _():
        rimrecv[:, 1] = jnp.zeros((ITERS, 16, GRID), F32)

    @pl.when(jnp.logical_not(has_down))
    def _():
        rimrecv[:, 0] = jnp.zeros((ITERS, 16, GRID), F32)

    load_u.wait()

    def halve(block, carry):
        at = pl.ds(pl.multiple_of(block * BLOCK, BLOCK), BLOCK)
        from_pad = pl.ds(pl.multiple_of(block * BLOCK + PAD, PAD), BLOCK)
        for field in range(EDGE):
            usend[0, field, at, :] = pad_a[EDGE + field, from_pad, :].astype(BF16)
        return carry

    lax.fori_loop(0, GRID // BLOCK, halve, 0)

    def keep_rims(step, source):
        for field in range(FIELDS):
            rimsend[step, 0, field:field + 1, :] = source[field, PAD:PAD + 1, :]
            rimsend[step, 1, field:field + 1, :] = source[field, PAD + GRID - 1:PAD + GRID, :]

    keep_rims(0, pad_a)

    pl.semaphore_wait(barrier, sum(there.astype(jnp.int32) for there in (has_prev, has_next, col >= 0, high_half & has_far)))
    tell(round_sem, high_half & has_far, far)

    def remote(src, dst, send_sem, recv_sem, target):
        return pltpu.make_async_remote_copy(
            src_ref=src, dst_ref=dst, send_sem=send_sem, recv_sem=recv_sem, device_id=target, device_id_type=MESH)

    def facts_copy():
        return remote(meta_v, meta_r, m_sem.at[0], m_sem.at[1], after)

    def rows_of(seg):
        start, size = SEGS[seg]
        return pl.ds(start, size)

    def u_forth(step, seg):
        at = rows_of(seg)
        return remote(usend.at[step, :, at, :], uprev.at[step, :, at, :], u_ssem.at[step, seg], u_rsem.at[step, seg], after)

    def f_back(step, seg):
        at = rows_of(seg)
        return remote(fsend.at[step, :, at, :], frecv.at[step, :, at, :], f_ssem.at[step, seg], f_rsem.at[step, seg], before)

    def q_forth(seg):
        at = rows_of(seg)
        return remote(pool.at[pl.ds(SKIPS, SKIPS), at, :], precv.at[:, at, :], q_ssem.at[seg], q_rsem.at[seg], after)

    def rim_copy(step, side):
        target = {"tile": col - 1 if side == 0 else col + 1}
        return remote(rimsend.at[step, side], rimrecv.at[step, side], rim_ssem.at[step, side], rim_rsem.at[step, side], target)

    def send_rims(step):
        @pl.when(has_up)
        def _():
            rim_copy(step, 0).start()

        @pl.when(has_down)
        def _():
            rim_copy(step, 1).start()

    @pl.when(has_next)
    def _():
        facts_copy().start()
        for seg in segments[:3]:
            u_forth(0, seg).start()

    @pl.when(high_half)
    def _():
        send_rims(0)

    zero_row = jnp.zeros((PAD, GRID), F32)
    for pad in pads:
        for field in range(FIELDS):
            pad[field, 0:PAD, :] = zero_row
            pad[field, PAD + GRID:, :] = zero_row

    def columns(section, first, last, count):
        halves = []
        for low in (0, HALF):
            top = dot_rows(first, img[section, low:low + HALF, 0:HALF])
            bottom = dot_rows(last, img[section, low:low + HALF, HALF:])
            halves.append([meet(top[REACH * one:REACH * (one + 1)], bottom[REACH * one:REACH * (one + 1)]).astype(BF16) for one in range(count)])
        return halves

    def section_pool(section):
        shifts = []
        for stride in range(1, SKIPS + 1):
            place = (section - stride + SKIPS) * SKIPS + stride - 1
            shifts.append((shift_s[0, place], shift_s[1, place]))
        first = jnp.concatenate([first_t[off_c] for _, off_c in shifts] + [first_t[0, 0:REACH, :]], axis=0)
        last = jnp.concatenate([last_t[off_c] for _, off_c in shifts] + [last_t[0, 0:REACH, :]], axis=0)
        low, high = columns(section, first, last, 2 * SKIPS + 1)
        for index, (off_r, _) in enumerate(shifts):
            slot = section * SKIPS + index
            top = dot_rows(first_t[off_r], jnp.concatenate(low[2 * index:2 * index + 2], axis=0))
            bottom = dot_rows(last_t[off_r], jnp.concatenate(high[2 * index:2 * index + 2], axis=0))
            smooth = meet(top[:REACH], bottom[:REACH]).astype(BF16)
            cache[slot, 0] = smooth[:, :GRID]
            cache[slot, 1] = meet(top[REACH:, :GRID], bottom[REACH:, :GRID]).astype(BF16)
            cache[slot, 2] = smooth[:, GRID:]
        pool[section] = meet(dot_rows(first_t[0, 0:REACH, :], low[-1]), dot_rows(last_t[0, 0:REACH, :], high[-1])).astype(BF16)

    def late_step(section, carry):
        fetch(section).wait()
        section_pool(section)
        return carry

    lax.fori_loop(SKIPS, RES, late_step, 0)

    @pl.when(has_next)
    def _():
        for seg in segments:
            if seg >= 3:
                u_forth(0, seg).start()
            q_forth(seg).start()

    for section in range(SKIPS):
        fetch(section).wait()

    @pl.when(has_prev)
    def _():
        facts_copy().wait_recv()

    to_scalars = pltpu.make_async_copy(meta_r, meta_s, loc_sem.at[4])
    to_scalars.start()
    to_scalars.wait()
    for place in range(SKIPS * SKIPS):
        for axis in range(2):
            shift_s[axis, place] = meta_s[0, 3 * place + axis]

    def early_step(section, carry):
        section_pool(section)
        return carry

    lax.fori_loop(0, SKIPS, early_step, 0)

    gain = [[force_step * weights[k - 1, s].astype(F32) for k in range(1, SKIPS + 1)] for s in range(RES)]
    stiff = [elastic_step * stiffness[s] for s in range(RES)]
    cross_gain = []
    for later, stride in CROSS:
        base = ((later - stride + SKIPS) * SKIPS + stride - 1) * 3
        cross_gain.append(force_step * meta_s[0, base + 2].astype(F32))

    def pull(slot, at, earlier_pool, row_gap, col_gap, scale):
        steep = (cache[slot, 1, at, :].astype(F32), cache[slot, 2, at, :].astype(F32))
        miss = cache[slot, 0, at, :].astype(F32) - earlier_pool + steep[0] * row_gap + steep[1] * col_gap
        weighted = scale * (miss / (1.0 + miss * miss))
        return weighted * steep[0], weighted * steep[1]

    def over(seg, body):
        start, size = SEGS[seg]

        def block_step(index, carry):
            low = start + index * BLOCK
            body(low, pl.ds(pl.multiple_of(low, BLOCK), BLOCK), pl.ds(pl.multiple_of(low + PAD, PAD), BLOCK))
            return carry

        lax.fori_loop(0, size // BLOCK, block_step, 0)

    def cross_pass(step, seg):
        pad = pads[step]

        def body(low, at, mid):
            own, back = [None] * EDGE, [None] * EDGE
            for index, (later, stride) in enumerate(CROSS):
                earlier = later - stride + SKIPS
                gaps = [pad[2 * later + c, mid, :] - uprev[step, 2 * earlier + c, at, :].astype(F32) for c in range(2)]
                pulled = pull(slot_of(later, stride), at, precv[earlier, at, :].astype(F32), gaps[0], gaps[1], cross_gain[index])
                for c in range(2):
                    here, there = 2 * later + c, 2 * earlier + c
                    own[here] = pulled[c] if own[here] is None else own[here] + pulled[c]
                    back[there] = pulled[c] if back[there] is None else back[there] + pulled[c]
            for field in range(EDGE):
                cross_own[field, at, :] = own[field]
                fsend[step, field, at, :] = back[field].astype(BF16)

        over(seg, body)

    def cross_turn(step, seg):
        @pl.when(has_prev)
        def _():
            u_forth(step, seg).wait_recv()
            if step == 0:
                q_forth(seg).wait_recv()

        cross_pass(step, seg)

        @pl.when(has_prev)
        def _():
            f_back(step, seg).start()

    def goal(step):
        return (pads[step + 1], PAD) if step + 1 < ITERS else (fin, 0)

    def local_pass(step, seg):
        pad, (target, base) = pads[step], goal(step)

        def body(low, at, mid):
            put = pl.ds(pl.multiple_of(low + base, PAD), BLOCK)
            above, below = pl.ds(low + PAD - 1, BLOCK), pl.ds(low + PAD + 1, BLOCK)
            edge = lax.broadcasted_iota(jnp.int32, (BLOCK, GRID), 1)
            total = []
            for field in range(FIELDS):
                here = pad[field, mid, :]
                left = jnp.where(edge == 0, 0.0, pltpu.roll(here, 1, 1))
                right = jnp.where(edge == GRID - 1, 0.0, pltpu.roll(here, GRID - 1, 1))
                beside = pad[field, above, :] + pad[field, below, :] + left + right
                total.append(here - stiff[field // 2] * (4.0 * here - beside))
                if field < EDGE:
                    total[field] -= cross_own[field, at, :]
            for later, stride in LOCAL:
                earlier = later - stride
                gaps = [pad[2 * later + c, mid, :] - pad[2 * earlier + c, mid, :] for c in range(2)]
                pulled = pull(slot_of(later, stride), at, pool[earlier, at, :].astype(F32), gaps[0], gaps[1], gain[earlier][stride - 1])
                for c in range(2):
                    total[2 * earlier + c] += pulled[c]
                    total[2 * later + c] -= pulled[c]
            for field in range(FIELDS):
                target[field, put, :] = total[field]

        over(seg, body)

    def finish(step, seg):
        target, base = goal(step)
        if seg < 2:
            side, row = ((1, 0), (0, GRID - 1))[seg]

            @pl.when((has_up, has_down)[seg])
            def _():
                rim_copy(step, side).wait_recv()

            for field in range(FIELDS):
                spot = slice(base + row, base + row + 1)
                target[field, spot, :] = target[field, spot, :] + stiff[field // 2] * rimrecv[step, side, field:field + 1, :]

        @pl.when(has_next)
        def _():
            f_back(step, seg).wait_recv()

        def body(low, at, mid):
            put = pl.ds(pl.multiple_of(low + base, PAD), BLOCK)
            for field in range(EDGE):
                done = target[EDGE + field, put, :] + frecv[step, field, at, :].astype(F32)
                target[EDGE + field, put, :] = done
                if step + 1 < ITERS:
                    usend[step + 1, field, at, :] = done.astype(BF16)

        over(seg, body)
        if step + 1 < ITERS:
            @pl.when(has_next)
            def _():
                u_forth(step + 1, seg).start()

            if seg == 1:
                keep_rims(step + 1, pads[step + 1])
                send_rims(step + 1)
        else:
            store(seg).start()

    def store(seg):
        at = rows_of(seg)
        return pltpu.make_async_copy(fin.at[:, at, :], out.at[:, at, :], loc_sem.at[5 + seg])

    edges, inner = segments[:2], segments[2:]

    def turns(step, *group):
        for seg in group:
            cross_turn(step, seg)

    def passes(step, *group):
        for seg in group:
            local_pass(step, seg)

    def finishes(step, *group):
        for seg in group:
            finish(step, seg)

    turns(0, 0, 1, 2)
    passes(0, 0, 1)
    turns(0, 3)
    passes(0, 2)
    turns(0, 4)
    passes(0, 3, 4)

    @pl.when(low_half)
    def _():
        @pl.when(has_far)
        def _():
            pl.semaphore_wait(round_sem, 1)

        send_rims(0)

    @pl.when(high_half)
    def _():
        finishes(0, *edges)
        finishes(0, 2)
        turns(1, *edges)
        finishes(0, 3, 4)
        passes(1, 0, 1)
        turns(1, 2)
        passes(1, 2)
        turns(1, 3)
        passes(1, 3)
        finishes(1, 0, 1)
        turns(1, 4)
        passes(1, 4)
        finishes(1, 2)
        turns(2, 0, 1)
        finishes(1, 3, 4)
        passes(2, 0, 1)
        turns(2, 2)
        passes(2, 2)
        turns(2, 3)
        passes(2, 3)
        turns(2, 4)
        passes(2, 4)
        finishes(2, 2, 3, 4, 0, 1)

    @pl.when(low_half)
    def _():
        finishes(0, *segments)
        turns(1, *edges)
        passes(1, *edges)
        for seg in inner:
            turns(1, seg)
            passes(1, seg)
        finishes(1, *inner)
        finishes(1, *edges)
        turns(2, *inner)
        passes(2, *inner)
        turns(2, *edges)
        passes(2, *edges)
        finishes(2, *inner)
        finishes(2, *edges)

    for seg in segments:
        store(seg).wait()

    @pl.when(has_prev)
    def _():
        for seg in segments:
            for step in range(ITERS):
                f_back(step, seg).wait_send()

    @pl.when(has_next)
    def _():
        facts_copy().wait_send()
        for seg in segments:
            q_forth(seg).wait_send()
        for seg in segments:
            for step in range(ITERS):
                u_forth(step, seg).wait_send()

    for step in range(ITERS):
        @pl.when(has_up)
        def _():
            rim_copy(step, 0).wait_send()

        @pl.when(has_down)
        def _():
            rim_copy(step, 1).wait_send()


def local(images, displacement, offsets, weights, stiffness):
    anywhere = pl.BlockSpec(memory_space=pl.ANY)
    dma, vmem, smem = pltpu.SemaphoreType.DMA, pltpu.VMEM, pltpu.SMEM
    segs = len(SEGS)
    given = (displacement.reshape(FIELDS, GRID, GRID), images, offsets.transpose(1, 2, 0), weights.T, stiffness)
    moved = pl.pallas_call(
        kernel,
        out_shape=jax.ShapeDtypeStruct((FIELDS, GRID, GRID), F32),
        in_specs=[anywhere] * 5,
        out_specs=anywhere,
        scratch_shapes=[
            vmem((RES, PIXELS, PIXELS), BF16),
            vmem((SKIPS + 1, 2 * REACH, HALF), BF16),
            vmem((SKIPS + 1, 2 * REACH, HALF), BF16),
            vmem((len(PAIRS), 3, GRID, GRID), BF16),
            vmem((RES, GRID, GRID), BF16),
            vmem((SKIPS, GRID, GRID), BF16),
            vmem((FIELDS, GRID + 2 * PAD, GRID), F32),
            vmem((FIELDS, GRID + 2 * PAD, GRID), F32),
            vmem((FIELDS, GRID + 2 * PAD, GRID), F32),
            vmem((FIELDS, GRID, GRID), F32),
            vmem((EDGE, GRID, GRID), F32),
            vmem((ITERS, EDGE, GRID, GRID), BF16),
            vmem((ITERS, EDGE, GRID, GRID), BF16),
            vmem((ITERS, EDGE, GRID, GRID), BF16),
            vmem((ITERS, EDGE, GRID, GRID), BF16),
            vmem((ITERS, 2, 16, GRID), F32),
            vmem((ITERS, 2, 16, GRID), F32),
            vmem((8, 128), jnp.int32),
            vmem((8, 128), jnp.int32),
            smem((8, 128), jnp.int32),
            smem((2, (RES + SKIPS) * SKIPS), jnp.int32),
            smem((SKIPS, 2, RES), jnp.int32),
            smem((SKIPS, RES), jnp.int32),
            smem((RES,), F32),
            dma((RES,)),
            dma((5 + segs,)),
            dma((ITERS, segs)),
            dma((ITERS, segs)),
            dma((ITERS, segs)),
            dma((ITERS, segs)),
            dma((segs,)),
            dma((segs,)),
            dma((ITERS, 2)),
            dma((ITERS, 2)),
            dma((2,)),
            pltpu.SemaphoreType.REGULAR,
        ],
        compiler_params=pltpu.CompilerParams(collective_id=0, has_side_effects=True, vmem_limit_bytes=24 << 20),
    )(*(pltpu.with_memory_space_constraint(each, pltpu.HBM) for each in given))
    return moved.reshape(RES, 2, GRID, GRID)


def solution(mesh):
    placed = (
        P("sec", "tile", None),
        P("sec", None, "tile", None),
        P("sec", None, None),
        P("sec", None),
        P("sec"),
    )
    return jax.shard_map(
        local, mesh=mesh, in_specs=placed, out_specs=P("sec", None, "tile", None), check_vma=False
    )
```
